32 devices in a mesh: dom: 8 (over y, x, core), grp: 4 (over z).
Axes of the slice: x: 2, y: 2, z: 4, core: 2. Of those that a mesh axis runs over, the one named last changes fastest.
Arguments:
- history: bfloat16 [16, 4, 128, 4096], P('dom', None, 'grp'), may hold values from -6 to 6
- face_patch: int32 [16, 6], replicated, may hold values from -1 to 15, as said below
- refined: int32 [16], replicated, may hold values 0 or 1
- dest_slot: int32 [16], replicated, may hold values from 0 to 15, as said below
- w_in: bfloat16 [640, 512], replicated, may hold values from -0.25 to 0.25
- in_bias: float32 [512], replicated, may hold values from -3 to 3
- w_out: bfloat16 [512, 128], replicated, may hold values from -0.25 to 0.25
Outputs:
- new_states: bfloat16 [16, 2, 128, 4096], P('dom', None, 'grp')
The draws below stay inside these ranges and needn't reach their ends.
Inputs may be any that keep to these rules, and one draw needn't show every extreme that they name: `dest_slot`: A permutation of the slots. Slot s lies on dom index s // 2; patch p starts at slot p, on index p // 2. No patch moves by more than one index of dom, from one index at most 1 patches go to each neighbouring index, and 1 is reached between some pair of indices. `face_patch`: -1 where the face lies on the window's boundary, else a patch other than p, aligned with p cell for cell on that face; its dom index is within one of p's both before and after rebalancing.
All inputs are finite; a program needn't handle non-finite values.
Results may differ from the reference program's by a relative error of at most 0.0071.
Values may be sent and summed in bfloat16 or wider, within the bound.
No kernel may reach another device: no remote copies, remote signals or barrier semaphores. Data moves between devices by JAX's collectives and lax.ppermute only.
A program may use at most 128 MiB of HBM per device.

```python
import jax
import jax.numpy as jnp
import numpy as np
from jax import lax

CH = 128
HID = 512
SIDE = 16
HIST = 4
PD = 2
MOVE = 1
PATCHES = 16


def migration_plan(key):
    dom_count = PATCHES // PD
    key_counts, key_pick, key_order = jax.random.split(jax.random.fold_in(key, 7), 3)
    swap_counts = jax.random.randint(key_counts, (dom_count - 1,), 0, MOVE + 1)
    forced = jax.random.randint(key_pick, (), 0, dom_count - 1)
    swap_counts = jnp.where(jnp.arange(dom_count - 1) == forced, MOVE, swap_counts)
    orders = jax.vmap(lambda sub_key: jax.random.permutation(sub_key, PD))(jax.random.split(key_order, dom_count))
    bounds = jnp.arange(dom_count - 1)
    right_ids = bounds[:, None] * PD + orders[:-1, MOVE:2 * MOVE]
    left_ids = (bounds[:, None] + 1) * PD + orders[1:, :MOVE]
    active = jnp.arange(MOVE)[None, :] < swap_counts[:, None]
    dest_ids = jnp.arange(PATCHES, dtype=jnp.int32)
    dest_ids = dest_ids.at[right_ids.reshape(-1)].set(jnp.where(active, left_ids, right_ids).reshape(-1))
    dest_ids = dest_ids.at[left_ids.reshape(-1)].set(jnp.where(active, right_ids, left_ids).reshape(-1))
    return dest_ids.astype(jnp.int32)


def draw_dest_slot(key, part):
    return migration_plan(key)


def draw_face_patch(key, part):
    dest_ids = migration_plan(key)
    key_pick, key_edge = jax.random.split(jax.random.fold_in(key, 19))
    patch_ids = jnp.arange(PATCHES, dtype=jnp.int32)[:, None]
    home_dev = patch_ids // PD
    low_end = jnp.maximum(home_dev - 1, 0) * PD
    high_end = jnp.minimum(home_dev + 2, PATCHES // PD) * PD
    raw_pick = jax.random.randint(key_pick, (PATCHES, 6), 0, 3 * PD)
    partner = low_end + raw_pick % (high_end - low_end)
    too_far = jnp.abs(dest_ids[partner] // PD - dest_ids[patch_ids] // PD) > 1
    on_edge = jax.random.randint(key_edge, (PATCHES, 6), 0, 6) == 0
    return jnp.where(too_far | on_edge | (partner == patch_ids), -1, partner).astype(jnp.int32)


def set_ends(values, rng, low, top_value):
    longest = values.shape.index(max(values.shape))
    spots = []
    for shift in (0, 1):
        where = [jax.random.randint(jax.random.fold_in(rng, axis), (), 0, length) for axis, length in enumerate(values.shape)]
        where[longest] = (where[longest] + shift) % values.shape[longest]
        spots.append(tuple(where))
    return values.at[spots[0]].set(low).at[spots[1]].set(top_value)


def shard_levels(stream_key, extent, shards, low, high):
    level, own = 1.0, jax.random.fold_in(stream_key, 6)
    for dim, shards_of in shards:
        draws = jnp.exp(jax.random.uniform(jax.random.fold_in(own, dim), (shards_of,), jnp.float32, low / len(shards), high / len(shards)))
        level = level * jnp.repeat(draws, extent[dim] // shards_of).reshape([-1 if axis == dim else 1 for axis in range(len(extent))])
    return level


def noise(own_key, extent, scale, bound, cuts=(), kind=jnp.bfloat16):
    result = jax.random.normal(own_key, extent, jnp.float32) * scale
    if len(cuts) > 0:
        result = shard_levels(own_key, extent, cuts, -0.22, 0.18) * result
    return jnp.clip(result, min=-bound, max=bound).astype(kind)


def setup_inputs(seed: int = 0) -> dict:
    splits = jax.random.split(jax.random.key(seed), 8)
    history = noise(splits[0], (PATCHES, HIST, CH, SIDE**3), 1.0, 6.0, ((0, 8), (2, 4)))
    face_patch = draw_face_patch(jax.random.fold_in(splits[7], 71), 0)
    refined = set_ends((jax.random.randint(splits[2], (PATCHES,), 0, 4) < 1).astype(jnp.int32), jax.random.fold_in(splits[2], 1), 0, 1)
    dest_slot = draw_dest_slot(jax.random.fold_in(splits[7], 71), 0)
    w_in = noise(splits[4], ((HIST + 1) * CH, HID), ((HIST + 1) * CH) ** -0.5, 0.25)
    in_bias = noise(splits[5], (HID,), 0.5, 3.0, (), jnp.float32)
    w_out = noise(splits[6], (HID, CH), HID ** -0.5, 0.25)
    return dict(history=history, face_patch=face_patch, refined=refined, dest_slot=dest_slot, w_in=w_in, in_bias=in_bias, w_out=w_out)


OPPOSITE = np.array([1, 0, 3, 2, 5, 4])


def face_layers(grid_field):
    return jnp.stack([grid_field[..., 0, :, :], grid_field[..., -1, :, :],
                      grid_field[..., :, 0, :], grid_field[..., :, -1, :],
                      grid_field[..., :, :, 0], grid_field[..., :, :, -1]], axis=-4)


def surround(grid_field, picked):
    widths = [(0, 0)] * (grid_field.ndim - 3) + [(1, 1)] * 3
    padded = jnp.pad(grid_field, widths)
    padded = padded.at[..., 0, 1:-1, 1:-1].set(picked[..., 0, :, :, :])
    padded = padded.at[..., -1, 1:-1, 1:-1].set(picked[..., 1, :, :, :])
    padded = padded.at[..., 1:-1, 0, 1:-1].set(picked[..., 2, :, :, :])
    padded = padded.at[..., 1:-1, -1, 1:-1].set(picked[..., 3, :, :, :])
    padded = padded.at[..., 1:-1, 1:-1, 0].set(picked[..., 4, :, :, :])
    padded = padded.at[..., 1:-1, 1:-1, -1].set(picked[..., 5, :, :, :])
    neighbour_sum = (padded[..., 2:, 1:-1, 1:-1] + padded[..., :-2, 1:-1, 1:-1]
                     + padded[..., 1:-1, 2:, 1:-1] + padded[..., 1:-1, :-2, 1:-1]
                     + padded[..., 1:-1, 1:-1, 2:] + padded[..., 1:-1, 1:-1, :-2])
    return neighbour_sum - 6.0 * grid_field


def advance(history, face_patch, refined, w_in, in_bias, w_out):
    how_many = history.shape[0]
    newest = history[:, 0].astype(jnp.float32).reshape(how_many, CH, SIDE, SIDE, SIDE)
    layers = face_layers(newest)[:, OPPOSITE]
    usable = face_patch >= 0
    picked = layers[jnp.maximum(face_patch, 0), jnp.arange(6)[None, :]]
    picked = jnp.where(usable[:, :, None, None, None], picked, jnp.zeros_like(picked))
    step_sizes = 1.0 - 0.5 * refined.astype(jnp.float32)

    def one_patch(patch_args):
        patch_states, faces, step_size = patch_args
        grid_field = patch_states[0].astype(jnp.float32).reshape(CH, SIDE, SIDE, SIDE)
        spread = surround(grid_field, faces).reshape(CH, SIDE ** 3).astype(jnp.bfloat16)
        inputs = jnp.concatenate([patch_states, spread[None]], 0).reshape((HIST + 1) * CH, SIDE ** 3)
        preact = jnp.dot(inputs.T, w_in, preferred_element_type=jnp.float32) + in_bias
        hidden = jax.nn.silu(preact).astype(jnp.bfloat16)
        update = jnp.dot(hidden, w_out, preferred_element_type=jnp.float32).astype(jnp.bfloat16)
        return (patch_states[0].astype(jnp.float32) + step_size * update.T.astype(jnp.float32)).astype(jnp.bfloat16)

    return lax.map(one_patch, (history, picked, step_sizes))


def reference(history, face_patch, refined, dest_slot, w_in, in_bias, w_out):
    first_state = advance(history, face_patch, refined, w_in, in_bias, w_out)
    carried = jnp.concatenate([first_state[:, None], history[:, :HIST - 1]], 1)
    second_state = advance(carried, face_patch, refined, w_in, in_bias, w_out)
    both_states = jnp.stack([first_state, second_state], 1)
    return jnp.zeros_like(both_states).at[dest_slot].set(both_states)
```

```python
import functools

import jax
import jax.numpy as jnp
import numpy as np
from jax import lax
from jax.experimental import pallas as pl
from jax.experimental.pallas import tpu as pltpu
from jax.sharding import PartitionSpec as P

SIDE = 16
HIST = 4
PLANE = SIDE * SIDE


OPPOSITE = np.array([1, 0, 3, 2, 5, 4])


def padded(array, sides, width):
    for axis, dim in sides:
        size, length = (lax.axis_size(axis), array.shape[dim])
        up = [(i, (i + 1) % size) for i in range(size - 1)]
        down = [(j, i) for i, j in up]
        last = lax.slice_in_dim(array, length - width, length, axis=dim)
        first = lax.slice_in_dim(array, 0, width, axis=dim)
        before = lax.ppermute(last, axis, up)
        after = lax.ppermute(first, axis, down)
        array = jnp.concatenate([before, array, after], axis=dim)
    return array


def select_table(side_len, stride, offset):
    rows = jnp.arange(side_len)[:, None]
    cols = jnp.arange(side_len * side_len)[None, :]
    return (cols == rows * stride + offset).astype(jnp.bfloat16)


def take_face(grid_rows, table):
    return jnp.einsum("ncxq,kq->ncxk", grid_rows, table, preferred_element_type=jnp.float32).astype(
        jnp.bfloat16
    )


def place_face(face_rows, table):
    return jnp.einsum("ncxk,kq->ncxq", face_rows, table, preferred_element_type=jnp.float32)


def laplace_cells(newest, positions, usable):
    how_many, channels, cell_count = newest.shape
    plane = SIDE * SIDE
    grid_rows = newest.reshape(how_many, channels, SIDE, plane)
    y_low = select_table(SIDE, 1, 0)
    y_high = select_table(SIDE, 1, plane - SIDE)
    z_low = select_table(SIDE, SIDE, 0)
    z_high = select_table(SIDE, SIDE, SIDE - 1)
    layers = jnp.stack(
        [
            grid_rows[:, :, 0, :],
            grid_rows[:, :, -1, :],
            take_face(grid_rows, y_low).reshape(how_many, channels, plane),
            take_face(grid_rows, y_high).reshape(how_many, channels, plane),
            take_face(grid_rows, z_low).reshape(how_many, channels, plane),
            take_face(grid_rows, z_high).reshape(how_many, channels, plane),
        ],
        1,
    )
    layers = layers[:, OPPOSITE]
    beside_all = padded(layers, (("dom", 0),), how_many)
    picked = beside_all[positions, jnp.arange(6)[None, :]]
    picked = jnp.where(usable[:, :, None, None], picked, jnp.zeros_like(picked))
    field = grid_rows.astype(jnp.float32)
    picked_wide = picked.astype(jnp.float32)
    x_plus = jnp.concatenate([field[:, :, 1:, :], picked_wide[:, 1][:, :, None, :]], 2)
    x_minus = jnp.concatenate([picked_wide[:, 0][:, :, None, :], field[:, :, :-1, :]], 2)
    zero_row = jnp.zeros((how_many, channels, SIDE, SIDE), jnp.float32)
    y_plus = jnp.concatenate([field[..., SIDE:], zero_row], 3)
    y_plus = y_plus + place_face(picked[:, 3].reshape(how_many, channels, SIDE, SIDE), y_high)
    y_minus = jnp.concatenate([zero_row, field[..., :-SIDE]], 3)
    y_minus = y_minus + place_face(picked[:, 2].reshape(how_many, channels, SIDE, SIDE), y_low)
    z_index = jnp.arange(plane) % SIDE
    zero_cell = jnp.zeros((how_many, channels, SIDE, 1), jnp.float32)
    z_plus = jnp.concatenate([field[..., 1:], zero_cell], 3)
    z_plus = jnp.where(z_index == SIDE - 1, 0.0, z_plus)
    z_plus = z_plus + place_face(picked[:, 5].reshape(how_many, channels, SIDE, SIDE), z_high)
    z_minus = jnp.concatenate([zero_cell, field[..., :-1]], 3)
    z_minus = jnp.where(z_index == 0, 0.0, z_minus)
    z_minus = z_minus + place_face(picked[:, 4].reshape(how_many, channels, SIDE, SIDE), z_low)
    neighbour_sum = x_plus + x_minus + y_plus + y_minus + z_plus + z_minus
    spread = neighbour_sum - 6.0 * field
    return spread.reshape(how_many, channels, cell_count).astype(jnp.bfloat16)


def local_general(history, face_patch, refined, dest_slot, w_in, in_bias, w_out):
    per_dev = history.shape[0]
    my_index = lax.axis_index("dom")
    lowest = (my_index - 1) * per_dev
    my_slots = my_index * per_dev + jnp.arange(per_dev, dtype=jnp.int32)
    patch_ids = jnp.arange(dest_slot.shape[0], dtype=jnp.int32)
    inverse = jnp.zeros_like(dest_slot).at[dest_slot].set(patch_ids)

    def advance(inputs):
        how_many = inputs.shape[0]
        cell_count = inputs.shape[3]
        stacked = inputs.reshape(how_many, -1, cell_count)
        preact = (
            jnp.einsum("nkc,kh->nch", stacked, w_in, preferred_element_type=jnp.float32) + in_bias
        )
        hidden = jax.nn.silu(preact).astype(jnp.bfloat16)
        update = jnp.einsum(
            "nch,hk->nkc", hidden, w_out, preferred_element_type=jnp.float32
        ).astype(jnp.bfloat16)
        back = lax.all_to_all(update, "grp", split_axis=1, concat_axis=2, tiled=True)
        return (back, update, inputs[:, : HIST - 1])

    first_nb = face_patch[my_slots]
    first_pos = jnp.clip(first_nb - lowest, 0, 3 * per_dev - 1)
    first_ok = first_nb >= 0
    first_spread = laplace_cells(history[:, 0], first_pos, first_ok)
    first_in = jnp.concatenate([history, first_spread[:, None]], 1)
    first_back, first_cells, first_kept = advance(
        lax.all_to_all(first_in, "grp", split_axis=3, concat_axis=2, tiled=True)
    )
    first_step = 1.0 - 0.5 * refined[my_slots].astype(jnp.float32)
    first_state = (
        history[:, 0].astype(jnp.float32)
        + first_step[:, None, None] * first_back.astype(jnp.float32)
    ).astype(jnp.bfloat16)
    carried = jnp.concatenate([first_state[:, None], history[:, : HIST - 1]], 1)
    owners = inverse[my_slots]
    second_nb = face_patch[owners]
    second_pos = jnp.clip(dest_slot[jnp.maximum(second_nb, 0)] - lowest, 0, 3 * per_dev - 1)
    second_ok = second_nb >= 0
    second_step = 1.0 - 0.5 * refined[owners].astype(jnp.float32)
    sources = inverse[my_slots]
    beside_all = padded(carried.reshape(per_dev, -1), (("dom", 0),), per_dev)
    moved_carried = jnp.take(beside_all, sources - lowest, axis=0).reshape(carried.shape)
    newest = moved_carried[:, 0]
    second_spread = laplace_cells(newest, second_pos, second_ok)
    second_in = jnp.concatenate([moved_carried, second_spread[:, None]], 1)
    second_back, unused_cells, unused_kept = advance(
        lax.all_to_all(second_in, "grp", split_axis=3, concat_axis=2, tiled=True)
    )
    second_state = (
        newest.astype(jnp.float32) + second_step[:, None, None] * second_back.astype(jnp.float32)
    ).astype(jnp.bfloat16)
    return jnp.stack([moved_carried[:, 0], second_state], 1)


SLAB = 4 * PLANE
HALF = 2 * PLANE
FACE_LANES = 3 * PLANE
PLAN_SIZE = 64
VMEM = pltpu.VMEM
SMEM = pltpu.SMEM


def face_tables():
    lay = np.zeros((SLAB, PLANE), np.float32)
    put = np.zeros((PLANE, SLAB), np.float32)
    source = {2: lambda m: 240 + m, 3: lambda m: m, 4: lambda m: 16 * m + 15, 5: lambda m: 16 * m}
    target = {2: lambda m: m, 3: lambda m: 240 + m, 4: lambda m: 16 * m, 5: lambda m: 16 * m + 15}
    for face in (2, 3, 4, 5):
        for plane in range(4):
            for m in range(SIDE):
                lane = (face - 2) * 64 + plane * 16 + m
                lay[plane * PLANE + source[face](m), lane] = 1
                put[lane, plane * PLANE + target[face](m)] = 1
    flat = np.zeros((PLANE, PLANE), np.float32)
    for y in range(SIDE):
        for z in range(SIDE):
            flat[y * SIDE + z, y * SIDE + z] = -6
            for dy, dz in ((1, 0), (-1, 0), (0, 1), (0, -1)):
                if 0 <= y + dy < SIDE and 0 <= z + dz < SIDE:
                    flat[(y + dy) * SIDE + z + dz, y * SIDE + z] = 1
    return lay, put, flat


def vmem_specs(count):
    return [pl.BlockSpec(memory_space=VMEM)] * count


def plan_kernel(per_dev, place, face_patch, refined, dest_slot, plan):
    dom, grp = place[0], place[1]
    patches = dest_slot.shape[0]
    plan[0] = dom
    plan[1] = grp
    up, down = jnp.int32(0), jnp.int32(0)
    for s in range(per_dev):
        new_dom = dest_slot[dom * per_dev + s] // per_dev
        up = jnp.where(new_dom == dom + 1, s, up)
        down = jnp.where(new_dom == dom - 1, s, down)
    plan[2] = up
    plan[3] = down
    for j in range(per_dev):
        code, patch = jnp.int32(0), jnp.int32(0)
        for o in (-1, 0, 1):
            for s in range(per_dev):
                p = (dom + o) * per_dev + s
                ok = (p >= 0) & (p < patches)
                p = jnp.clip(p, 0, patches - 1)
                ok = ok & (dest_slot[p] == dom * per_dev + j)
                code = jnp.where(ok, s if o == 0 else per_dev + (o + 1) // 2, code)
                patch = jnp.where(ok, p, patch)
        plan[4 + j] = code
        plan[6 + j] = refined[patch]
        for f in range(6):
            beside = face_patch[patch, f]
            slot = dest_slot[jnp.maximum(beside, 0)]
            plan[8 + 6 * j + f] = jnp.where(beside < 0, -1, slot - (dom - 1) * per_dev)


def send_kernel(plan, up_in, down_in, up_out, down_out):
    up_out[...] = up_in[0]
    down_out[...] = down_in[0]


def pack_kernel(states, *refs):
    plan = refs[0]
    own = refs[1 : 1 + states]
    below, above = refs[1 + states : 3 + states]
    outs = refs[3 + states :]
    grp, size = plan[1], len(outs)
    per_dev = own[0].shape[0]

    def emit(j, t, take):
        for k in range(size):
            slab = lax.rem(grp + k, size)
            low = pl.multiple_of(slab * HALF, HALF)
            high = pl.multiple_of((2 * size - 1 - slab) * HALF, HALF)
            outs[k][j, t, :, 0:HALF] = take(pl.ds(low, HALF))
            outs[k][j, t, :, HALF:SLAB] = take(pl.ds(high, HALF))

    for j in range(per_dev):
        code = plan[4 + j]

        @pl.when(code < per_dev)
        def _():
            for t in range(states):
                emit(j, t, lambda lanes: own[t][jnp.minimum(code, per_dev - 1), 0, :, lanes])

        @pl.when(code == per_dev)
        def _():
            for t in range(states):
                emit(j, t, lambda lanes: below[t, :, lanes])

        @pl.when(code == per_dev + 1)
        def _():
            for t in range(states):
                emit(j, t, lambda lanes: above[t, :, lanes])


def emit_edges(plan, slab, lay, a_out, b_out, f_out):
    even = lax.rem(plan[1], 2) == 0
    for j in range(slab.shape[0]):
        @pl.when(even)
        def _():
            a_out[j] = slab[j, :, PLANE : 3 * PLANE]
            b_out[j, :, 0:PLANE] = slab[j, :, 0:PLANE]
            b_out[j, :, PLANE:HALF] = slab[j, :, 3 * PLANE : SLAB]

        @pl.when(jnp.logical_not(even))
        def _():
            b_out[j] = slab[j, :, PLANE : 3 * PLANE]
            a_out[j, :, 0:PLANE] = slab[j, :, 0:PLANE]
            a_out[j, :, PLANE:HALF] = slab[j, :, 3 * PLANE : SLAB]

        f_out[j, :, 0:PLANE] = jnp.dot(
            slab[j], lay[...], preferred_element_type=jnp.float32
        ).astype(jnp.bfloat16)
        f_out[j, :, PLANE:HALF] = slab[j, :, 0:PLANE]
        f_out[j, :, HALF:FACE_LANES] = slab[j, :, 3 * PLANE : SLAB]


def edge_kernel(plan, lay, *refs):
    pieces, (slab, a_out, b_out, f_out) = refs[:-4], refs[-4:]
    grp, size = plan[1], len(pieces)
    width = pieces[0].shape[2]
    for k in range(size):
        rows = pl.ds(pl.multiple_of(lax.rem(grp - k + size, size) * width, width), width)
        for j in range(slab.shape[0]):
            slab[j, rows, :] = pieces[k][j, 0]
    emit_edges(plan, slab, lay, a_out, b_out, f_out)


def laplacian(plan, slab, a_in, b_in, mine, below, above, put, flat, spread, first_row):
    f32 = jnp.float32
    grp = plan[1]
    per_dev, channels = slab.shape[0], slab.shape[1]
    even = lax.rem(grp, 2) == 0
    lowest, highest = grp == 0, grp == 3
    cands = [ref.at[s] for ref in (below, mine, above) for s in range(per_dev)]
    face_of_lane = lax.broadcasted_iota(jnp.int32, (channels, PLANE), 1) // 64
    for j in range(per_dev):
        layer = [slab[j, :, i * PLANE : (i + 1) * PLANE] for i in range(4)]
        wide = [x.astype(f32) for x in layer]
        a, b = a_in[j].astype(f32), b_in[j].astype(f32)
        inner = jnp.where(even, a, b)
        outer = jnp.where(even, b, a)
        inner0 = jnp.where(highest, wide[2], inner[:, :PLANE])
        inner1 = jnp.where(highest, wide[1], inner[:, PLANE:])
        code = [plan[8 + 6 * j + f] for f in range(6)]
        lane_code = jnp.where(
            face_of_lane < 2,
            jnp.where(face_of_lane == 0, code[2], code[3]),
            jnp.where(face_of_lane == 2, code[4], code[5]),
        )
        face0 = jnp.zeros((channels, PLANE), f32)
        face1 = jnp.zeros((channels, PLANE), f32)
        rest = jnp.zeros((channels, PLANE), f32)
        for c, cand in enumerate(cands):
            face0 = jnp.where(code[0] == c, cand[:, HALF:FACE_LANES].astype(f32), face0)
            face1 = jnp.where(code[1] == c, cand[:, PLANE:HALF].astype(f32), face1)
            rest = jnp.where(lane_code == c, cand[:, 0:PLANE].astype(f32), rest)
        outer0 = jnp.where(lowest, face0, outer[:, :PLANE])
        outer1 = jnp.where(lowest, face1, outer[:, PLANE:])
        placed = jnp.dot(rest.astype(jnp.bfloat16), put[...], preferred_element_type=f32)
        sides = (
            (outer0, wide[1]),
            (wide[0], inner0),
            (inner1, wide[3]),
            (wide[2], outer1),
        )
        for i in range(4):
            total = jnp.dot(layer[i], flat[...], preferred_element_type=f32)
            total = total + placed[:, i * PLANE : (i + 1) * PLANE] + sides[i][0] + sides[i][1]
            spread[first_row : first_row + channels, j * SLAB + i * PLANE : j * SLAB + (i + 1) * PLANE] = (
                total.astype(jnp.bfloat16)
            )


TILE = 512


def network(plan, inputs, slab, w_in, bias, w_out, state):
    per_dev = slab.shape[0]
    per_slab = SLAB // TILE
    steps = [1.0 - 0.5 * plan[6 + j].astype(jnp.float32) for j in range(per_dev)]
    for j in range(per_dev):
        for n in range(per_slab):
            lanes = slice(j * SLAB + n * TILE, j * SLAB + (n + 1) * TILE)
            pre = jnp.dot(w_in[...], inputs[:, lanes], preferred_element_type=jnp.float32) + bias[...]
            half = 0.5 * pre
            hidden = (half + half * jnp.tanh(half)).astype(jnp.bfloat16)
            update = jnp.dot(w_out[...], hidden, preferred_element_type=jnp.float32)
            update = update.astype(jnp.bfloat16).astype(jnp.float32)
            here = slice(n * TILE, (n + 1) * TILE)
            state[j, :, here] = (slab[j, :, here].astype(jnp.float32) + steps[j] * update).astype(
                jnp.bfloat16
            )


def emit_back(plan, state, backs):
    grp, size = plan[1], len(backs)
    width = backs[0].shape[1]
    for k in range(size):
        rows = pl.ds(pl.multiple_of(lax.rem(grp - k + size, size) * width, width), width)
        for j in range(state.shape[0]):
            backs[k][j] = state[j, rows, :]


def first_kernel(size, plan, lay, put, flat, w_in, bias, w_out, slab, a_in, b_in, mine, below, above, *refs):
    pieces = refs[:size]
    kept, state, a_out, b_out, f_out = refs[size : size + 5]
    backs = refs[size + 5 : 2 * size + 5]
    inputs = refs[2 * size + 5]
    grp = plan[1]
    per_dev, channels = slab.shape[0], slab.shape[1]
    width = pieces[0].shape[2]
    states = pieces[0].shape[1]
    for k in range(size):
        row = lax.rem(grp - k + size, size) * width
        for t in range(states):
            rows = pl.ds(pl.multiple_of((t + 1) * channels + row, width), width)
            for j in range(per_dev):
                inputs[rows, j * SLAB : (j + 1) * SLAB] = pieces[k][j, t]
    for j in range(per_dev):
        inputs[0:channels, j * SLAB : (j + 1) * SLAB] = slab[j]
    laplacian(plan, slab, a_in, b_in, mine, below, above, put, flat, inputs, HIST * channels)
    network(plan, inputs, slab, w_in, bias, w_out, state)
    emit_edges(plan, state, lay, a_out, b_out, f_out)
    emit_back(plan, state, backs)
    kept[...] = inputs[0 : (HIST - 1) * channels, :]


def second_kernel(size, plan, put, flat, w_in, bias, w_out, slab, a_in, b_in, mine, below, above, kept, *refs):
    backs = refs[:size]
    state, inputs = refs[size : size + 2]
    per_dev, channels = slab.shape[0], slab.shape[1]
    inputs[channels : HIST * channels, :] = kept[...]
    for j in range(per_dev):
        inputs[0:channels, j * SLAB : (j + 1) * SLAB] = slab[j]
    laplacian(plan, slab, a_in, b_in, mine, below, above, put, flat, inputs, HIST * channels)
    network(plan, inputs, slab, w_in, bias, w_out, state)
    emit_back(plan, state, backs)


def finish_kernel(size, plan, *refs):
    out = refs[-1]
    grp = plan[1]
    for t in range(2):
        for k in range(size):
            piece = refs[t * size + k]
            slab = lax.rem(grp + k, size)
            low = pl.multiple_of(slab * HALF, HALF)
            high = pl.multiple_of((2 * size - 1 - slab) * HALF, HALF)
            for j in range(piece.shape[0]):
                out[j, t, :, pl.ds(low, HALF)] = piece[j, :, 0:HALF]
                out[j, t, :, pl.ds(high, HALF)] = piece[j, :, HALF:SLAB]


def local_folded(history, face_patch, refined, dest_slot, w_in, in_bias, w_out):
    bf16 = jnp.bfloat16
    per_dev, hist, width, cells = history.shape
    size = lax.axis_size("grp")
    channels = width * size
    hidden = w_in.shape[1]
    doms = lax.axis_size("dom")
    smem = pl.BlockSpec(memory_space=SMEM)
    shape = jax.ShapeDtypeStruct
    place = jnp.stack([lax.axis_index("dom"), lax.axis_index("grp")]).astype(jnp.int32)
    plan = pl.pallas_call(
        functools.partial(plan_kernel, per_dev),
        out_shape=shape((PLAN_SIZE,), jnp.int32),
        in_specs=[smem] * 4,
        out_specs=smem,
        name="plan",
    )(place, face_patch, refined, dest_slot)

    up_ring = [(i, (i + 1) % doms) for i in range(doms)]
    down_ring = [(i, (i - 1) % doms) for i in range(doms)]

    def movers(first, states):
        block = (1, 1, width, cells)
        out = [shape((states, width, cells), bf16)] * 2
        return pl.pallas_call(
            send_kernel,
            grid_spec=pltpu.PrefetchScalarGridSpec(
                num_scalar_prefetch=1,
                grid=(states,),
                in_specs=[
                    pl.BlockSpec(block, lambda t, plan: (plan[2], first + t, 0, 0)),
                    pl.BlockSpec(block, lambda t, plan: (plan[3], first + t, 0, 0)),
                ],
                out_specs=[pl.BlockSpec((1, width, cells), lambda t, plan: (t, 0, 0))] * 2,
            ),
            out_shape=out,
            name="movers",
        )(plan, history, history)

    def across_dom(up, down):
        return lax.ppermute(up, "dom", up_ring), lax.ppermute(down, "dom", down_ring)

    def pack(first, states, below, above):
        specs = [
            pl.BlockSpec((per_dev, 1, width, cells), functools.partial(lambda t, i: (0, t, 0, 0), first + t))
            for t in range(states)
        ]
        whole = pl.BlockSpec((states, width, cells), lambda i: (0, 0, 0))
        return pl.pallas_call(
            functools.partial(pack_kernel, states),
            grid=(1,),
            out_shape=[shape((per_dev, states, width, SLAB), bf16)] * size,
            in_specs=[smem] + specs + [whole] * 2,
            out_specs=[pl.BlockSpec((per_dev, states, width, SLAB), lambda i: (0, 0, 0, 0))] * size,
            name="pack",
        )(plan, *([history] * states), below, above)

    def across_grp(pieces, sign):
        moved = [pieces[0]]
        for k in range(1, size):
            moved.append(lax.ppermute(pieces[k], "grp", [(i, (i + sign * k) % size) for i in range(size)]))
        return moved

    pair_a = [(i, i ^ 1) for i in range(size)]
    pair_b = [(i, i if i in (0, size - 1) else ((i + 1) ^ 1) - 1) for i in range(size)]

    def exchange(a_out, b_out, f_out):
        a_in = lax.ppermute(a_out, "grp", pair_a)
        b_in = lax.ppermute(b_out, "grp", pair_b)
        below, above = across_dom(f_out, f_out)
        return a_in, b_in, f_out, below, above

    lay, put, flat = (jnp.asarray(table, bf16) for table in face_tables())
    w_in_t, w_out_t = w_in.T, w_out.T
    bias = in_bias[:, None]

    first_up, first_down = movers(0, 1)
    below0, above0 = across_dom(first_up, first_down)
    rest_up, rest_down = movers(1, hist - 1)
    below1, above1 = across_dom(rest_up, rest_down)
    newest = across_grp(pack(0, 1, below0, above0), 1)
    older = across_grp(pack(1, hist - 1, below1, above1), 1)

    slab_shape = shape((per_dev, channels, SLAB), bf16)
    edge_shapes = [
        shape((per_dev, channels, HALF), bf16),
        shape((per_dev, channels, HALF), bf16),
        shape((per_dev, channels, FACE_LANES), bf16),
    ]
    back_shapes = [shape((per_dev, width, SLAB), bf16)] * size
    slab0, *edges = pl.pallas_call(
        edge_kernel,
        out_shape=[slab_shape] + edge_shapes,
        in_specs=[smem] + vmem_specs(1 + size),
        out_specs=vmem_specs(4),
        name="edges",
    )(plan, lay, *newest)

    inputs = pltpu.VMEM(((hist + 1) * channels, per_dev * SLAB), bf16)
    kept, slab1, *rest = pl.pallas_call(
        functools.partial(first_kernel, size),
        out_shape=[shape(((hist - 1) * channels, per_dev * SLAB), bf16), slab_shape] + edge_shapes + back_shapes,
        in_specs=[smem] + vmem_specs(12 + size),
        out_specs=vmem_specs(5 + size),
        scratch_shapes=[inputs],
        name="first",
    )(plan, lay, put, flat, w_in_t, bias, w_out_t, slab0, *exchange(*edges), *older)

    parts = exchange(*rest[:3])
    back1 = across_grp(rest[3:], -1)
    state = pltpu.VMEM((per_dev, channels, SLAB), bf16)
    back2 = pl.pallas_call(
        functools.partial(second_kernel, size),
        out_shape=back_shapes,
        in_specs=[smem] + vmem_specs(12),
        out_specs=vmem_specs(size),
        scratch_shapes=[state, inputs],
        name="second",
    )(plan, put, flat, w_in_t, bias, w_out_t, slab1, *parts, kept)
    back2 = across_grp(back2, -1)

    return pl.pallas_call(
        functools.partial(finish_kernel, size),
        out_shape=shape((per_dev, 2, width, cells), bf16),
        in_specs=[smem] + vmem_specs(2 * size),
        out_specs=pl.BlockSpec(memory_space=VMEM),
        name="finish",
    )(plan, *back1, *back2)


def solution(mesh):
    placed = (P("dom", None, "grp", None), P(), P(), P(), P(), P(), P())
    body = local_folded if mesh.shape["grp"] == 4 else local_general
    return jax.shard_map(
        body, mesh=mesh, in_specs=placed, out_specs=P("dom", None, "grp", None), check_vma=False
    )
```

```python
import functools

import jax
import jax.numpy as jnp
import numpy as np
from jax import lax
from jax.experimental import pallas as pl
from jax.experimental.pallas import tpu as pltpu
from jax.sharding import PartitionSpec as P

SIDE = 16
HIST = 4
PLANE = SIDE * SIDE


OPPOSITE = np.array([1, 0, 3, 2, 5, 4])


def padded(array, sides, width):
    for axis, dim in sides:
        size, length = (lax.axis_size(axis), array.shape[dim])
        up = [(i, (i + 1) % size) for i in range(size - 1)]
        down = [(j, i) for i, j in up]
        last = lax.slice_in_dim(array, length - width, length, axis=dim)
        first = lax.slice_in_dim(array, 0, width, axis=dim)
        before = lax.ppermute(last, axis, up)
        after = lax.ppermute(first, axis, down)
        array = jnp.concatenate([before, array, after], axis=dim)
    return array


def select_table(side_len, stride, offset):
    rows = jnp.arange(side_len)[:, None]
    cols = jnp.arange(side_len * side_len)[None, :]
    return (cols == rows * stride + offset).astype(jnp.bfloat16)


def take_face(grid_rows, table):
    return jnp.einsum("ncxq,kq->ncxk", grid_rows, table, preferred_element_type=jnp.float32).astype(
        jnp.bfloat16
    )


def place_face(face_rows, table):
    return jnp.einsum("ncxk,kq->ncxq", face_rows, table, preferred_element_type=jnp.float32)


def laplace_cells(newest, positions, usable):
    how_many, channels, cell_count = newest.shape
    plane = SIDE * SIDE
    grid_rows = newest.reshape(how_many, channels, SIDE, plane)
    y_low = select_table(SIDE, 1, 0)
    y_high = select_table(SIDE, 1, plane - SIDE)
    z_low = select_table(SIDE, SIDE, 0)
    z_high = select_table(SIDE, SIDE, SIDE - 1)
    layers = jnp.stack(
        [
            grid_rows[:, :, 0, :],
            grid_rows[:, :, -1, :],
            take_face(grid_rows, y_low).reshape(how_many, channels, plane),
            take_face(grid_rows, y_high).reshape(how_many, channels, plane),
            take_face(grid_rows, z_low).reshape(how_many, channels, plane),
            take_face(grid_rows, z_high).reshape(how_many, channels, plane),
        ],
        1,
    )
    layers = layers[:, OPPOSITE]
    beside_all = padded(layers, (("dom", 0),), how_many)
    picked = beside_all[positions, jnp.arange(6)[None, :]]
    picked = jnp.where(usable[:, :, None, None], picked, jnp.zeros_like(picked))
    field = grid_rows.astype(jnp.float32)
    picked_wide = picked.astype(jnp.float32)
    x_plus = jnp.concatenate([field[:, :, 1:, :], picked_wide[:, 1][:, :, None, :]], 2)
    x_minus = jnp.concatenate([picked_wide[:, 0][:, :, None, :], field[:, :, :-1, :]], 2)
    zero_row = jnp.zeros((how_many, channels, SIDE, SIDE), jnp.float32)
    y_plus = jnp.concatenate([field[..., SIDE:], zero_row], 3)
    y_plus = y_plus + place_face(picked[:, 3].reshape(how_many, channels, SIDE, SIDE), y_high)
    y_minus = jnp.concatenate([zero_row, field[..., :-SIDE]], 3)
    y_minus = y_minus + place_face(picked[:, 2].reshape(how_many, channels, SIDE, SIDE), y_low)
    z_index = jnp.arange(plane) % SIDE
    zero_cell = jnp.zeros((how_many, channels, SIDE, 1), jnp.float32)
    z_plus = jnp.concatenate([field[..., 1:], zero_cell], 3)
    z_plus = jnp.where(z_index == SIDE - 1, 0.0, z_plus)
    z_plus = z_plus + place_face(picked[:, 5].reshape(how_many, channels, SIDE, SIDE), z_high)
    z_minus = jnp.concatenate([zero_cell, field[..., :-1]], 3)
    z_minus = jnp.where(z_index == 0, 0.0, z_minus)
    z_minus = z_minus + place_face(picked[:, 4].reshape(how_many, channels, SIDE, SIDE), z_low)
    neighbour_sum = x_plus + x_minus + y_plus + y_minus + z_plus + z_minus
    spread = neighbour_sum - 6.0 * field
    return spread.reshape(how_many, channels, cell_count).astype(jnp.bfloat16)


def local_general(history, face_patch, refined, dest_slot, w_in, in_bias, w_out):
    per_dev = history.shape[0]
    my_index = lax.axis_index("dom")
    lowest = (my_index - 1) * per_dev
    my_slots = my_index * per_dev + jnp.arange(per_dev, dtype=jnp.int32)
    patch_ids = jnp.arange(dest_slot.shape[0], dtype=jnp.int32)
    inverse = jnp.zeros_like(dest_slot).at[dest_slot].set(patch_ids)

    def advance(inputs):
        how_many = inputs.shape[0]
        cell_count = inputs.shape[3]
        stacked = inputs.reshape(how_many, -1, cell_count)
        preact = (
            jnp.einsum("nkc,kh->nch", stacked, w_in, preferred_element_type=jnp.float32) + in_bias
        )
        hidden = jax.nn.silu(preact).astype(jnp.bfloat16)
        update = jnp.einsum(
            "nch,hk->nkc", hidden, w_out, preferred_element_type=jnp.float32
        ).astype(jnp.bfloat16)
        back = lax.all_to_all(update, "grp", split_axis=1, concat_axis=2, tiled=True)
        return (back, update, inputs[:, : HIST - 1])

    first_nb = face_patch[my_slots]
    first_pos = jnp.clip(first_nb - lowest, 0, 3 * per_dev - 1)
    first_ok = first_nb >= 0
    first_spread = laplace_cells(history[:, 0], first_pos, first_ok)
    first_in = jnp.concatenate([history, first_spread[:, None]], 1)
    first_back, first_cells, first_kept = advance(
        lax.all_to_all(first_in, "grp", split_axis=3, concat_axis=2, tiled=True)
    )
    first_step = 1.0 - 0.5 * refined[my_slots].astype(jnp.float32)
    first_state = (
        history[:, 0].astype(jnp.float32)
        + first_step[:, None, None] * first_back.astype(jnp.float32)
    ).astype(jnp.bfloat16)
    carried = jnp.concatenate([first_state[:, None], history[:, : HIST - 1]], 1)
    owners = inverse[my_slots]
    second_nb = face_patch[owners]
    second_pos = jnp.clip(dest_slot[jnp.maximum(second_nb, 0)] - lowest, 0, 3 * per_dev - 1)
    second_ok = second_nb >= 0
    second_step = 1.0 - 0.5 * refined[owners].astype(jnp.float32)
    sources = inverse[my_slots]
    beside_all = padded(carried.reshape(per_dev, -1), (("dom", 0),), per_dev)
    moved_carried = jnp.take(beside_all, sources - lowest, axis=0).reshape(carried.shape)
    newest = moved_carried[:, 0]
    second_spread = laplace_cells(newest, second_pos, second_ok)
    second_in = jnp.concatenate([moved_carried, second_spread[:, None]], 1)
    second_back, unused_cells, unused_kept = advance(
        lax.all_to_all(second_in, "grp", split_axis=3, concat_axis=2, tiled=True)
    )
    second_state = (
        newest.astype(jnp.float32) + second_step[:, None, None] * second_back.astype(jnp.float32)
    ).astype(jnp.bfloat16)
    return jnp.stack([moved_carried[:, 0], second_state], 1)


SLAB = 4 * PLANE
HALF = 2 * PLANE
FACE_LANES = 3 * PLANE
PLAN_SIZE = 64
VMEM = pltpu.VMEM
SMEM = pltpu.SMEM


def face_tables():
    lay = np.zeros((SLAB, PLANE), np.float32)
    put = np.zeros((PLANE, SLAB), np.float32)
    source = {2: lambda m: 240 + m, 3: lambda m: m, 4: lambda m: 16 * m + 15, 5: lambda m: 16 * m}
    target = {2: lambda m: m, 3: lambda m: 240 + m, 4: lambda m: 16 * m, 5: lambda m: 16 * m + 15}
    for face in (2, 3, 4, 5):
        for plane in range(4):
            for m in range(SIDE):
                lane = (face - 2) * 64 + plane * 16 + m
                lay[plane * PLANE + source[face](m), lane] = 1
                put[lane, plane * PLANE + target[face](m)] = 1
    flat = np.zeros((PLANE, PLANE), np.float32)
    for y in range(SIDE):
        for z in range(SIDE):
            flat[y * SIDE + z, y * SIDE + z] = -6
            for dy, dz in ((1, 0), (-1, 0), (0, 1), (0, -1)):
                if 0 <= y + dy < SIDE and 0 <= z + dz < SIDE:
                    flat[(y + dy) * SIDE + z + dz, y * SIDE + z] = 1
    return lay, put, flat


def vmem_specs(count):
    return [pl.BlockSpec(memory_space=VMEM)] * count


def plan_kernel(per_dev, place, face_patch, refined, dest_slot, *refs):
    plan = refs[-1]
    dom, grp = place[0], place[1]
    patches = dest_slot.shape[0]
    plan[0] = dom
    plan[1] = grp
    up, down = jnp.int32(0), jnp.int32(0)
    for s in range(per_dev):
        new_dom = dest_slot[dom * per_dev + s] // per_dev
        up = jnp.where(new_dom == dom + 1, s, up)
        down = jnp.where(new_dom == dom - 1, s, down)
    plan[2] = up
    plan[3] = down
    for j in range(per_dev):
        code, patch = jnp.int32(0), jnp.int32(0)
        for o in (-1, 0, 1):
            for s in range(per_dev):
                p = (dom + o) * per_dev + s
                ok = (p >= 0) & (p < patches)
                p = jnp.clip(p, 0, patches - 1)
                ok = ok & (dest_slot[p] == dom * per_dev + j)
                code = jnp.where(ok, s if o == 0 else per_dev + (o + 1) // 2, code)
                patch = jnp.where(ok, p, patch)
        plan[4 + j] = code
        plan[6 + j] = refined[patch]
        for f in range(6):
            beside = face_patch[f, patch]
            slot = dest_slot[jnp.maximum(beside, 0)]
            plan[8 + 6 * j + f] = jnp.where(beside < 0, -1, slot - (dom - 1) * per_dev)


def send_kernel(plan, up_in, down_in, up_out, down_out):
    up_out[...] = up_in[0]
    down_out[...] = down_in[0]


def pack_kernel(states, *refs):
    plan = refs[0]
    own = refs[1 : 1 + states]
    below, above = refs[1 + states : 3 + states]
    outs = refs[-4:]
    grp, size = plan[1], len(outs)
    per_dev = own[0].shape[0]

    def emit(j, t, take):
        for k in range(size):
            slab = lax.rem(grp + k, size)
            low = pl.multiple_of(slab * HALF, HALF)
            high = pl.multiple_of((2 * size - 1 - slab) * HALF, HALF)
            outs[k][j, t, :, 0:HALF] = take(pl.ds(low, HALF))
            outs[k][j, t, :, HALF:SLAB] = take(pl.ds(high, HALF))

    for j in range(per_dev):
        code = plan[4 + j]

        @pl.when(code < per_dev)
        def _():
            for t in range(states):
                emit(j, t, lambda lanes: own[t][jnp.minimum(code, per_dev - 1), 0, :, lanes])

        @pl.when(code == per_dev)
        def _():
            for t in range(states):
                emit(j, t, lambda lanes: below[t, :, lanes])

        @pl.when(code == per_dev + 1)
        def _():
            for t in range(states):
                emit(j, t, lambda lanes: above[t, :, lanes])


def emit_edges(plan, slab, lay, a_out, b_out, f_out):
    even = lax.rem(plan[1], 2) == 0
    for j in range(slab.shape[0]):
        @pl.when(even)
        def _():
            a_out[j] = slab[j, :, PLANE : 3 * PLANE]
            b_out[j, :, 0:PLANE] = slab[j, :, 0:PLANE]
            b_out[j, :, PLANE:HALF] = slab[j, :, 3 * PLANE : SLAB]

        @pl.when(jnp.logical_not(even))
        def _():
            b_out[j] = slab[j, :, PLANE : 3 * PLANE]
            a_out[j, :, 0:PLANE] = slab[j, :, 0:PLANE]
            a_out[j, :, PLANE:HALF] = slab[j, :, 3 * PLANE : SLAB]

        f_out[j, :, 0:PLANE] = jnp.dot(
            slab[j], lay[...], preferred_element_type=jnp.float32
        ).astype(jnp.bfloat16)
        f_out[j, :, PLANE:HALF] = slab[j, :, 0:PLANE]
        f_out[j, :, HALF:FACE_LANES] = slab[j, :, 3 * PLANE : SLAB]


def early_pack_kernel(place, state, *refs):
    outs = refs[-4:]
    size = len(outs)
    for j in range(state.shape[0]):
        for k in range(size):
            slab = lax.rem(place[1] + k, size)
            low = pl.multiple_of(slab * HALF, HALF)
            high = pl.multiple_of((2 * size - 1 - slab) * HALF, HALF)
            outs[k][j, 0, :, 0:HALF] = state[j, 0, :, pl.ds(low, HALF)]
            outs[k][j, 0, :, HALF:SLAB] = state[j, 0, :, pl.ds(high, HALF)]


def gather_kernel(size, plan, *refs):
    pieces, (slab, up, down) = refs[:size], refs[-3:]
    grp = plan[1]
    width = pieces[0].shape[2]
    for k in range(size):
        rows = pl.ds(pl.multiple_of(lax.rem(grp - k + size, size) * width, width), width)
        for j in range(slab.shape[0]):
            slab[j, rows, :] = pieces[k][j, 0]
    up[...] = slab[plan[2]]
    down[...] = slab[plan[3]]


def settle(plan, j, slab, below, above, store):
    per_dev = slab.shape[0]
    code = plan[4 + j]

    @pl.when(code < per_dev)
    def _():
        store(slab[jnp.minimum(code, per_dev - 1)])

    @pl.when(code == per_dev)
    def _():
        store(below[...])

    @pl.when(code == per_dev + 1)
    def _():
        store(above[...])


def edge_kernel(plan, lay, old, below, above, *refs):
    slab, a_out, b_out, f_out = refs[-4:]
    for j in range(slab.shape[0]):

        def store(value):
            slab[j] = value

        settle(plan, j, old, below, above, store)
    emit_edges(plan, slab, lay, a_out, b_out, f_out)


def laplacian(plan, slab, a_in, b_in, mine, below, above, put, flat, spread, first_row):
    f32 = jnp.float32
    grp = plan[1]
    per_dev, channels = slab.shape[0], slab.shape[1]
    even = lax.rem(grp, 2) == 0
    lowest, highest = grp == 0, grp == 3
    cands = [ref.at[s] for ref in (below, mine, above) for s in range(per_dev)]
    face_of_lane = lax.broadcasted_iota(jnp.int32, (channels, PLANE), 1) // 64
    for j in range(per_dev):
        layer = [slab[j, :, i * PLANE : (i + 1) * PLANE] for i in range(4)]
        wide = [x.astype(f32) for x in layer]
        a, b = a_in[j].astype(f32), b_in[j].astype(f32)
        inner = jnp.where(even, a, b)
        outer = jnp.where(even, b, a)
        inner0 = jnp.where(highest, wide[2], inner[:, :PLANE])
        inner1 = jnp.where(highest, wide[1], inner[:, PLANE:])
        code = [plan[8 + 6 * j + f] for f in range(6)]
        lane_code = jnp.where(
            face_of_lane < 2,
            jnp.where(face_of_lane == 0, code[2], code[3]),
            jnp.where(face_of_lane == 2, code[4], code[5]),
        )
        face0 = jnp.zeros((channels, PLANE), f32)
        face1 = jnp.zeros((channels, PLANE), f32)
        rest = jnp.zeros((channels, PLANE), f32)
        for c, cand in enumerate(cands):
            face0 = jnp.where(code[0] == c, cand[:, HALF:FACE_LANES].astype(f32), face0)
            face1 = jnp.where(code[1] == c, cand[:, PLANE:HALF].astype(f32), face1)
            rest = jnp.where(lane_code == c, cand[:, 0:PLANE].astype(f32), rest)
        outer0 = jnp.where(lowest, face0, outer[:, :PLANE])
        outer1 = jnp.where(lowest, face1, outer[:, PLANE:])
        placed = jnp.dot(rest.astype(jnp.bfloat16), put[...], preferred_element_type=f32)
        sides = (
            (outer0, wide[1]),
            (wide[0], inner0),
            (inner1, wide[3]),
            (wide[2], outer1),
        )
        for i in range(4):
            total = jnp.dot(layer[i], flat[...], preferred_element_type=f32)
            total = total + placed[:, i * PLANE : (i + 1) * PLANE] + sides[i][0] + sides[i][1]
            spread[first_row : first_row + channels, j * SLAB + i * PLANE : j * SLAB + (i + 1) * PLANE] = (
                total.astype(jnp.bfloat16)
            )


TILE = 512


def network(plan, inputs, slab, w_in, bias, w_out, state):
    per_dev = slab.shape[0]
    per_slab = SLAB // TILE
    steps = [1.0 - 0.5 * plan[6 + j].astype(jnp.float32) for j in range(per_dev)]
    for j in range(per_dev):
        for n in range(per_slab):
            lanes = slice(j * SLAB + n * TILE, j * SLAB + (n + 1) * TILE)
            pre = jnp.dot(w_in[...], inputs[:, lanes], preferred_element_type=jnp.float32) + bias[...]
            half = 0.5 * pre
            hidden = (half + half * jnp.tanh(half)).astype(jnp.bfloat16)
            update = jnp.dot(w_out[...], hidden, preferred_element_type=jnp.float32)
            update = update.astype(jnp.bfloat16).astype(jnp.float32)
            here = slice(n * TILE, (n + 1) * TILE)
            state[j, :, here] = (slab[j, :, here].astype(jnp.float32) + steps[j] * update).astype(
                jnp.bfloat16
            )


def emit_back(plan, state, backs):
    grp, size = plan[1], len(backs)
    width = backs[0].shape[1]
    for k in range(size):
        rows = pl.ds(pl.multiple_of(lax.rem(grp - k + size, size) * width, width), width)
        for j in range(state.shape[0]):
            backs[k][j] = state[j, rows, :]


def first_kernel(size, plan, lay, put, flat, w_in, bias, w_out, slab, a_in, b_in, mine, below, above, old, old_below, old_above, *refs):
    pieces = refs[:size]
    kept, state, a_out, b_out, f_out = refs[size : size + 5]
    backs = refs[size + 5 : 2 * size + 5]
    inputs = refs[2 * size + 5]
    grp = plan[1]
    per_dev, channels = slab.shape[0], slab.shape[1]
    width = pieces[0].shape[2]
    states = pieces[0].shape[1]
    for k in range(size):
        row = lax.rem(grp - k + size, size) * width
        for t in range(states):
            rows = pl.ds(pl.multiple_of((t + 2) * channels + row, width), width)
            for j in range(per_dev):
                inputs[rows, j * SLAB : (j + 1) * SLAB] = pieces[k][j, t]
    for j in range(per_dev):
        inputs[0:channels, j * SLAB : (j + 1) * SLAB] = slab[j]

        def store(value):
            inputs[channels : 2 * channels, j * SLAB : (j + 1) * SLAB] = value

        settle(plan, j, old, old_below, old_above, store)
    laplacian(plan, slab, a_in, b_in, mine, below, above, put, flat, inputs, HIST * channels)
    network(plan, inputs, slab, w_in, bias, w_out, state)
    emit_edges(plan, state, lay, a_out, b_out, f_out)
    emit_back(plan, state, backs)
    kept[...] = inputs[0 : (HIST - 1) * channels, :]


def second_kernel(size, plan, put, flat, w_in, bias, w_out, slab, a_in, b_in, mine, below, above, kept, *refs):
    backs = refs[:size]
    state, inputs = refs[size : size + 2]
    per_dev, channels = slab.shape[0], slab.shape[1]
    inputs[channels : HIST * channels, :] = kept[...]
    for j in range(per_dev):
        inputs[0:channels, j * SLAB : (j + 1) * SLAB] = slab[j]
    laplacian(plan, slab, a_in, b_in, mine, below, above, put, flat, inputs, HIST * channels)
    network(plan, inputs, slab, w_in, bias, w_out, state)
    emit_back(plan, state, backs)


def finish_kernel(size, plan, *refs):
    out = refs[-1]
    grp = plan[1]
    for t in range(2):
        for k in range(size):
            piece = refs[t * size + k]
            slab = lax.rem(grp + k, size)
            low = pl.multiple_of(slab * HALF, HALF)
            high = pl.multiple_of((2 * size - 1 - slab) * HALF, HALF)
            for j in range(piece.shape[0]):
                out[j, t, :, pl.ds(low, HALF)] = piece[j, :, 0:HALF]
                out[j, t, :, pl.ds(high, HALF)] = piece[j, :, HALF:SLAB]


def local_folded(history, face_patch, refined, dest_slot, w_in, in_bias, w_out):
    bf16 = jnp.bfloat16
    per_dev, hist, width, cells = history.shape
    size = lax.axis_size("grp")
    channels = width * size
    hidden = w_in.shape[1]
    doms = lax.axis_size("dom")
    smem = pl.BlockSpec(memory_space=SMEM)
    anywhere = pl.BlockSpec(memory_space=pl.ANY)
    shape = jax.ShapeDtypeStruct
    place = jnp.stack([lax.axis_index("dom"), lax.axis_index("grp")]).astype(jnp.int32)
    up_ring = [(i, (i + 1) % doms) for i in range(doms)]
    down_ring = [(i, (i - 1) % doms) for i in range(doms)]

    def early_pack(state, *after):
        return pl.pallas_call(
            early_pack_kernel,
            grid=(1,),
            out_shape=[shape((per_dev, 1, width, SLAB), bf16)] * size,
            in_specs=[smem, pl.BlockSpec((per_dev, 1, width, cells), lambda i: (0, state, 0, 0))]
            + [anywhere] * len(after),
            out_specs=[pl.BlockSpec((per_dev, 1, width, SLAB), lambda i: (0, 0, 0, 0))] * size,
            name="early_pack",
        )(place, history, *after)

    newest = early_pack(0)
    plan = pl.pallas_call(
        functools.partial(plan_kernel, per_dev),
        out_shape=shape((PLAN_SIZE,), jnp.int32),
        in_specs=[smem] * 4 + [anywhere] * size,
        out_specs=smem,
        name="plan",
    )(place, face_patch.T, refined, dest_slot, *newest)


    def movers(first, states):
        block = (1, 1, width, cells)
        out = [shape((states, width, cells), bf16)] * 2
        return pl.pallas_call(
            send_kernel,
            grid_spec=pltpu.PrefetchScalarGridSpec(
                num_scalar_prefetch=1,
                grid=(states,),
                in_specs=[
                    pl.BlockSpec(block, lambda t, plan: (plan[2], first + t, 0, 0)),
                    pl.BlockSpec(block, lambda t, plan: (plan[3], first + t, 0, 0)),
                ],
                out_specs=[pl.BlockSpec((1, width, cells), lambda t, plan: (t, 0, 0))] * 2,
            ),
            out_shape=out,
            name="movers",
        )(plan, history, history)

    def across_dom(up, down):
        return lax.ppermute(up, "dom", up_ring), lax.ppermute(down, "dom", down_ring)

    def pack(first, states, below, above, *after):
        specs = [
            pl.BlockSpec((per_dev, 1, width, cells), functools.partial(lambda t, i: (0, t, 0, 0), first + t))
            for t in range(states)
        ]
        whole = pl.BlockSpec((states, width, cells), lambda i: (0, 0, 0))
        return pl.pallas_call(
            functools.partial(pack_kernel, states),
            grid=(1,),
            out_shape=[shape((per_dev, states, width, SLAB), bf16)] * size,
            in_specs=[smem] + specs + [whole] * 2 + [anywhere] * len(after),
            out_specs=[pl.BlockSpec((per_dev, states, width, SLAB), lambda i: (0, 0, 0, 0))] * size,
            name="pack",
        )(plan, *([history] * states), below, above, *after)

    def across_grp(pieces, sign):
        moved = [pieces[0]]
        for k in range(1, size):
            moved.append(lax.ppermute(pieces[k], "grp", [(i, (i + sign * k) % size) for i in range(size)]))
        return moved

    pair_a = [(i, i ^ 1) for i in range(size)]
    pair_b = [(i, i if i in (0, size - 1) else ((i + 1) ^ 1) - 1) for i in range(size)]

    def exchange(a_out, b_out, f_out):
        a_in = lax.ppermute(a_out, "grp", pair_a)
        b_in = lax.ppermute(b_out, "grp", pair_b)
        below, above = across_dom(f_out, f_out)
        return a_in, b_in, f_out, below, above

    lay, put, flat = (jnp.asarray(table, bf16) for table in face_tables())
    w_in_t, w_out_t = w_in.T, w_out.T
    bias = in_bias[:, None]

    def gather(pieces, *after):
        slab, up, down = pl.pallas_call(
            functools.partial(gather_kernel, size),
            out_shape=[slab_shape] + [shape((channels, SLAB), bf16)] * 2,
            in_specs=[smem] + vmem_specs(size) + [anywhere] * len(after),
            out_specs=vmem_specs(3),
            name="gather",
        )(plan, *pieces, *after)
        return (slab, *across_dom(up, down))

    slab_shape = shape((per_dev, channels, SLAB), bf16)
    edge_shapes = [
        shape((per_dev, channels, HALF), bf16),
        shape((per_dev, channels, HALF), bf16),
        shape((per_dev, channels, FACE_LANES), bf16),
    ]
    back_shapes = [shape((per_dev, width, SLAB), bf16)] * size
    up, down = movers(2, hist - 2)
    below, above = across_dom(up, down)
    second_newest = early_pack(1, up, down)
    next_pieces = across_grp(second_newest, 1)
    old0 = gather(across_grp(newest, 1), *second_newest)
    packed = pack(2, hist - 2, below, above, old0[0])
    older = across_grp(packed, 1)
    slab0, *edges = pl.pallas_call(
        edge_kernel,
        out_shape=[slab_shape] + edge_shapes,
        in_specs=[smem] + vmem_specs(4) + [anywhere] * size,
        out_specs=vmem_specs(4),
        name="edges",
    )(plan, lay, *old0, *packed)
    old1 = gather(next_pieces, *edges)

    inputs = pltpu.VMEM(((hist + 1) * channels, per_dev * SLAB), bf16)
    kept, slab1, *rest = pl.pallas_call(
        functools.partial(first_kernel, size),
        out_shape=[shape(((hist - 1) * channels, per_dev * SLAB), bf16), slab_shape] + edge_shapes + back_shapes,
        in_specs=[smem] + vmem_specs(15 + size),
        out_specs=vmem_specs(5 + size),
        scratch_shapes=[inputs],
        name="first",
    )(plan, lay, put, flat, w_in_t, bias, w_out_t, slab0, *exchange(*edges), *old1, *older)

    parts = exchange(*rest[:3])
    back1 = across_grp(rest[3:], -1)
    state = pltpu.VMEM((per_dev, channels, SLAB), bf16)
    back2 = pl.pallas_call(
        functools.partial(second_kernel, size),
        out_shape=back_shapes,
        in_specs=[smem] + vmem_specs(12),
        out_specs=vmem_specs(size),
        scratch_shapes=[state, inputs],
        name="second",
    )(plan, put, flat, w_in_t, bias, w_out_t, slab1, *parts, kept)
    back2 = across_grp(back2, -1)

    return pl.pallas_call(
        functools.partial(finish_kernel, size),
        out_shape=shape((per_dev, 2, width, cells), bf16),
        in_specs=[smem] + vmem_specs(2 * size),
        out_specs=pl.BlockSpec(memory_space=VMEM),
        name="finish",
    )(plan, *back1, *back2)


def solution(mesh):
    placed = (P("dom", None, "grp", None), P(), P(), P(), P(), P(), P())
    body = local_folded if mesh.shape["grp"] == 4 else local_general
    return jax.shard_map(
        body, mesh=mesh, in_specs=placed, out_specs=P("dom", None, "grp", None), check_vma=False
    )
```

```python
import functools

import jax
import jax.numpy as jnp
import numpy as np
from jax import lax
from jax.experimental import pallas as pl
from jax.experimental.pallas import tpu as pltpu
from jax.sharding import PartitionSpec as P

SIDE = 16
HIST = 4
PLANE = SIDE * SIDE


OPPOSITE = np.array([1, 0, 3, 2, 5, 4])


def padded(array, sides, width):
    for axis, dim in sides:
        size, length = (lax.axis_size(axis), array.shape[dim])
        up = [(i, (i + 1) % size) for i in range(size - 1)]
        down = [(j, i) for i, j in up]
        last = lax.slice_in_dim(array, length - width, length, axis=dim)
        first = lax.slice_in_dim(array, 0, width, axis=dim)
        before = lax.ppermute(last, axis, up)
        after = lax.ppermute(first, axis, down)
        array = jnp.concatenate([before, array, after], axis=dim)
    return array


def select_table(side_len, stride, offset):
    rows = jnp.arange(side_len)[:, None]
    cols = jnp.arange(side_len * side_len)[None, :]
    return (cols == rows * stride + offset).astype(jnp.bfloat16)


def take_face(grid_rows, table):
    return jnp.einsum("ncxq,kq->ncxk", grid_rows, table, preferred_element_type=jnp.float32).astype(
        jnp.bfloat16
    )


def place_face(face_rows, table):
    return jnp.einsum("ncxk,kq->ncxq", face_rows, table, preferred_element_type=jnp.float32)


def laplace_cells(newest, positions, usable):
    how_many, channels, cell_count = newest.shape
    plane = SIDE * SIDE
    grid_rows = newest.reshape(how_many, channels, SIDE, plane)
    y_low = select_table(SIDE, 1, 0)
    y_high = select_table(SIDE, 1, plane - SIDE)
    z_low = select_table(SIDE, SIDE, 0)
    z_high = select_table(SIDE, SIDE, SIDE - 1)
    layers = jnp.stack(
        [
            grid_rows[:, :, 0, :],
            grid_rows[:, :, -1, :],
            take_face(grid_rows, y_low).reshape(how_many, channels, plane),
            take_face(grid_rows, y_high).reshape(how_many, channels, plane),
            take_face(grid_rows, z_low).reshape(how_many, channels, plane),
            take_face(grid_rows, z_high).reshape(how_many, channels, plane),
        ],
        1,
    )
    layers = layers[:, OPPOSITE]
    beside_all = padded(layers, (("dom", 0),), how_many)
    picked = beside_all[positions, jnp.arange(6)[None, :]]
    picked = jnp.where(usable[:, :, None, None], picked, jnp.zeros_like(picked))
    field = grid_rows.astype(jnp.float32)
    picked_wide = picked.astype(jnp.float32)
    x_plus = jnp.concatenate([field[:, :, 1:, :], picked_wide[:, 1][:, :, None, :]], 2)
    x_minus = jnp.concatenate([picked_wide[:, 0][:, :, None, :], field[:, :, :-1, :]], 2)
    zero_row = jnp.zeros((how_many, channels, SIDE, SIDE), jnp.float32)
    y_plus = jnp.concatenate([field[..., SIDE:], zero_row], 3)
    y_plus = y_plus + place_face(picked[:, 3].reshape(how_many, channels, SIDE, SIDE), y_high)
    y_minus = jnp.concatenate([zero_row, field[..., :-SIDE]], 3)
    y_minus = y_minus + place_face(picked[:, 2].reshape(how_many, channels, SIDE, SIDE), y_low)
    z_index = jnp.arange(plane) % SIDE
    zero_cell = jnp.zeros((how_many, channels, SIDE, 1), jnp.float32)
    z_plus = jnp.concatenate([field[..., 1:], zero_cell], 3)
    z_plus = jnp.where(z_index == SIDE - 1, 0.0, z_plus)
    z_plus = z_plus + place_face(picked[:, 5].reshape(how_many, channels, SIDE, SIDE), z_high)
    z_minus = jnp.concatenate([zero_cell, field[..., :-1]], 3)
    z_minus = jnp.where(z_index == 0, 0.0, z_minus)
    z_minus = z_minus + place_face(picked[:, 4].reshape(how_many, channels, SIDE, SIDE), z_low)
    neighbour_sum = x_plus + x_minus + y_plus + y_minus + z_plus + z_minus
    spread = neighbour_sum - 6.0 * field
    return spread.reshape(how_many, channels, cell_count).astype(jnp.bfloat16)


def local_general(history, face_patch, refined, dest_slot, w_in, in_bias, w_out):
    per_dev = history.shape[0]
    my_index = lax.axis_index("dom")
    lowest = (my_index - 1) * per_dev
    my_slots = my_index * per_dev + jnp.arange(per_dev, dtype=jnp.int32)
    patch_ids = jnp.arange(dest_slot.shape[0], dtype=jnp.int32)
    inverse = jnp.zeros_like(dest_slot).at[dest_slot].set(patch_ids)

    def advance(inputs):
        how_many = inputs.shape[0]
        cell_count = inputs.shape[3]
        stacked = inputs.reshape(how_many, -1, cell_count)
        preact = (
            jnp.einsum("nkc,kh->nch", stacked, w_in, preferred_element_type=jnp.float32) + in_bias
        )
        hidden = jax.nn.silu(preact).astype(jnp.bfloat16)
        update = jnp.einsum(
            "nch,hk->nkc", hidden, w_out, preferred_element_type=jnp.float32
        ).astype(jnp.bfloat16)
        back = lax.all_to_all(update, "grp", split_axis=1, concat_axis=2, tiled=True)
        return (back, update, inputs[:, : HIST - 1])

    first_nb = face_patch[my_slots]
    first_pos = jnp.clip(first_nb - lowest, 0, 3 * per_dev - 1)
    first_ok = first_nb >= 0
    first_spread = laplace_cells(history[:, 0], first_pos, first_ok)
    first_in = jnp.concatenate([history, first_spread[:, None]], 1)
    first_back, _, _ = advance(
        lax.all_to_all(first_in, "grp", split_axis=3, concat_axis=2, tiled=True)
    )
    first_step = 1.0 - 0.5 * refined[my_slots].astype(jnp.float32)
    first_state = (
        history[:, 0].astype(jnp.float32)
        + first_step[:, None, None] * first_back.astype(jnp.float32)
    ).astype(jnp.bfloat16)
    carried = jnp.concatenate([first_state[:, None], history[:, : HIST - 1]], 1)
    owners = inverse[my_slots]
    second_nb = face_patch[owners]
    second_pos = jnp.clip(dest_slot[jnp.maximum(second_nb, 0)] - lowest, 0, 3 * per_dev - 1)
    second_ok = second_nb >= 0
    second_step = 1.0 - 0.5 * refined[owners].astype(jnp.float32)
    sources = inverse[my_slots]
    beside_all = padded(carried.reshape(per_dev, -1), (("dom", 0),), per_dev)
    moved_carried = jnp.take(beside_all, sources - lowest, axis=0).reshape(carried.shape)
    newest = moved_carried[:, 0]
    second_spread = laplace_cells(newest, second_pos, second_ok)
    second_in = jnp.concatenate([moved_carried, second_spread[:, None]], 1)
    second_back, _, _ = advance(
        lax.all_to_all(second_in, "grp", split_axis=3, concat_axis=2, tiled=True)
    )
    second_state = (
        newest.astype(jnp.float32) + second_step[:, None, None] * second_back.astype(jnp.float32)
    ).astype(jnp.bfloat16)
    return jnp.stack([moved_carried[:, 0], second_state], 1)


SLAB = 4 * PLANE
HALF = 2 * PLANE
FACE_LANES = 3 * PLANE
PLAN_SIZE = 64
VMEM = pltpu.VMEM
SMEM = pltpu.SMEM


def face_tables():
    lay = np.zeros((SLAB, PLANE), np.float32)
    put = np.zeros((PLANE, SLAB), np.float32)
    source = {2: lambda m: 240 + m, 3: lambda m: m, 4: lambda m: 16 * m + 15, 5: lambda m: 16 * m}
    target = {2: lambda m: m, 3: lambda m: 240 + m, 4: lambda m: 16 * m, 5: lambda m: 16 * m + 15}
    for face in (2, 3, 4, 5):
        for plane in range(4):
            for m in range(SIDE):
                lane = (face - 2) * 64 + plane * 16 + m
                lay[plane * PLANE + source[face](m), lane] = 1
                put[lane, plane * PLANE + target[face](m)] = 1
    flat = np.zeros((PLANE, PLANE), np.float32)
    for y in range(SIDE):
        for z in range(SIDE):
            flat[y * SIDE + z, y * SIDE + z] = -6
            for dy, dz in ((1, 0), (-1, 0), (0, 1), (0, -1)):
                if 0 <= y + dy < SIDE and 0 <= z + dz < SIDE:
                    flat[(y + dy) * SIDE + z + dz, y * SIDE + z] = 1
    return lay, put, flat


def vmem_specs(count):
    return [pl.BlockSpec(memory_space=VMEM)] * count


def plan_kernel(per_dev, place, face_patch, refined, dest_slot, *refs):
    plan = refs[-1]
    dom, grp = place[0], place[1]
    patches = dest_slot.shape[0]
    plan[0] = dom
    plan[1] = grp
    up, down = jnp.int32(0), jnp.int32(0)
    for s in range(per_dev):
        new_dom = dest_slot[dom * per_dev + s] // per_dev
        up = jnp.where(new_dom == dom + 1, s, up)
        down = jnp.where(new_dom == dom - 1, s, down)
    plan[2] = up
    plan[3] = down
    for j in range(per_dev):
        code, patch = jnp.int32(0), jnp.int32(0)
        for o in (-1, 0, 1):
            for s in range(per_dev):
                p = (dom + o) * per_dev + s
                ok = (p >= 0) & (p < patches)
                p = jnp.clip(p, 0, patches - 1)
                ok = ok & (dest_slot[p] == dom * per_dev + j)
                code = jnp.where(ok, s if o == 0 else per_dev + (o + 1) // 2, code)
                patch = jnp.where(ok, p, patch)
        plan[4 + j] = code
        plan[6 + j] = refined[patch]
        for f in range(6):
            beside = face_patch[f, patch]
            slot = dest_slot[jnp.maximum(beside, 0)]
            plan[8 + 6 * j + f] = jnp.where(beside < 0, -1, slot - (dom - 1) * per_dev)


def slab_lanes(slab, size):
    low = pl.multiple_of(slab * HALF, HALF)
    high = pl.multiple_of((2 * size - 1 - slab) * HALF, HALF)
    return ((slice(0, HALF), pl.ds(low, HALF)), (slice(HALF, SLAB), pl.ds(high, HALF)))


def channel_rows(grp, k, size, width, first=0):
    row = lax.rem(grp - k + size, size) * width
    return pl.ds(pl.multiple_of(first + row, width), width)


def settle(plan, j, own, below, above, store):
    per_dev = own.shape[0]
    code = plan[4 + j]

    @pl.when(code < per_dev)
    def _():
        store(own.at[jnp.minimum(code, per_dev - 1)])

    @pl.when(code == per_dev)
    def _():
        store(below)

    @pl.when(code == per_dev + 1)
    def _():
        store(above)


def send_kernel(plan, up_in, down_in, up_out, down_out):
    up_out[...] = up_in[0]
    down_out[...] = down_in[0]


def early_pack_kernel(size, states, place, *refs):
    for k in range(1, size + 1):
        k = k % size
        out = refs[k - size]
        for here, there in slab_lanes(lax.rem(place[1] + k, size), size):
            for t in range(states):
                for j in range(out.shape[0]):
                    out[j, t, :, here] = refs[t][j, 0, :, there]


def pack_kernel(size, states, plan, below, above, *refs):
    outs = refs[-size:]
    for t in range(states):
        for j in range(refs[t].shape[0]):

            def store(source):
                for k in range(1, size + 1):
                    k = k % size
                    for here, there in slab_lanes(lax.rem(plan[1] + k, size), size):
                        outs[k][j, t, :, here] = source[0, :, there]

            settle(plan, j, refs[t], below.at[pl.ds(t, 1)], above.at[pl.ds(t, 1)], store)


def emit_edges(plan, slab, lay, a_out, b_out, f_out):
    even = lax.rem(plan[1], 2) == 0
    for j in range(slab.shape[0]):
        @pl.when(even)
        def _():
            a_out[j] = slab[j, :, PLANE : 3 * PLANE]
            b_out[j, :, 0:PLANE] = slab[j, :, 0:PLANE]
            b_out[j, :, PLANE:HALF] = slab[j, :, 3 * PLANE : SLAB]

        @pl.when(jnp.logical_not(even))
        def _():
            b_out[j] = slab[j, :, PLANE : 3 * PLANE]
            a_out[j, :, 0:PLANE] = slab[j, :, 0:PLANE]
            a_out[j, :, PLANE:HALF] = slab[j, :, 3 * PLANE : SLAB]

        f_out[j, :, 0:PLANE] = jnp.dot(
            slab[j], lay[...], preferred_element_type=jnp.float32
        ).astype(jnp.bfloat16)
        f_out[j, :, PLANE:HALF] = slab[j, :, 0:PLANE]
        f_out[j, :, HALF:FACE_LANES] = slab[j, :, 3 * PLANE : SLAB]


def gather_kernel(size, plan, *refs):
    pieces, (slab, up, down) = refs[:size], refs[-3:]
    per_dev, states, width = pieces[0].shape[:3]
    for k in range(size):
        rows = channel_rows(plan[1], k, size, width)
        for t in range(states):
            up[t, rows] = pieces[k][plan[2], t]
            down[t, rows] = pieces[k][plan[3], t]
            for j in range(per_dev):
                slab[j, t, rows] = pieces[k][j, t]


def edge_kernel(plan, lay, old, below, above, *refs):
    slab, a_out, b_out, f_out = refs[-4:]
    for j in range(slab.shape[0]):

        def store(source):
            slab[j] = source[0]

        settle(plan, j, old, below, above, store)
    emit_edges(plan, slab, lay, a_out, b_out, f_out)


def laplacian(plan, slab, a_in, b_in, mine, below, above, put, flat, spread, first_row):
    f32 = jnp.float32
    grp = plan[1]
    per_dev, channels = slab.shape[0], slab.shape[1]
    even = lax.rem(grp, 2) == 0
    lowest, highest = grp == 0, grp == 3
    cands = [ref.at[s] for ref in (below, mine, above) for s in range(per_dev)]
    face_of_lane = lax.broadcasted_iota(jnp.int32, (channels, PLANE), 1) // 64
    for j in range(per_dev):
        layer = [slab[j, :, i * PLANE : (i + 1) * PLANE] for i in range(4)]
        wide = [x.astype(f32) for x in layer]
        a, b = a_in[j].astype(f32), b_in[j].astype(f32)
        inner = jnp.where(even, a, b)
        outer = jnp.where(even, b, a)
        inner0 = jnp.where(highest, wide[2], inner[:, :PLANE])
        inner1 = jnp.where(highest, wide[1], inner[:, PLANE:])
        code = [plan[8 + 6 * j + f] for f in range(6)]
        lane_code = jnp.where(
            face_of_lane < 2,
            jnp.where(face_of_lane == 0, code[2], code[3]),
            jnp.where(face_of_lane == 2, code[4], code[5]),
        )
        face0 = jnp.zeros((channels, PLANE), f32)
        face1 = jnp.zeros((channels, PLANE), f32)
        rest = jnp.zeros((channels, PLANE), f32)
        for c, cand in enumerate(cands):
            face0 = jnp.where(code[0] == c, cand[:, HALF:FACE_LANES].astype(f32), face0)
            face1 = jnp.where(code[1] == c, cand[:, PLANE:HALF].astype(f32), face1)
            rest = jnp.where(lane_code == c, cand[:, 0:PLANE].astype(f32), rest)
        outer0 = jnp.where(lowest, face0, outer[:, :PLANE])
        outer1 = jnp.where(lowest, face1, outer[:, PLANE:])
        placed = jnp.dot(rest.astype(jnp.bfloat16), put[...], preferred_element_type=f32)
        sides = (
            (outer0, wide[1]),
            (wide[0], inner0),
            (inner1, wide[3]),
            (wide[2], outer1),
        )
        for i in range(4):
            total = jnp.dot(layer[i], flat[...], preferred_element_type=f32)
            total = total + placed[:, i * PLANE : (i + 1) * PLANE] + sides[i][0] + sides[i][1]
            spread[first_row : first_row + channels, j * SLAB + i * PLANE : j * SLAB + (i + 1) * PLANE] = (
                total.astype(jnp.bfloat16)
            )


TILE = 512


def network(plan, inputs, slab, w_in, bias, w_out, state):
    per_dev = slab.shape[0]
    per_slab = SLAB // TILE
    steps = [1.0 - 0.5 * plan[6 + j].astype(jnp.float32) for j in range(per_dev)]
    for j in range(per_dev):
        for n in range(per_slab):
            lanes = slice(j * SLAB + n * TILE, j * SLAB + (n + 1) * TILE)
            pre = jnp.dot(w_in[...], inputs[:, lanes], preferred_element_type=jnp.float32) + bias[...]
            half = 0.5 * pre
            hidden = (half + half * jnp.tanh(half)).astype(jnp.bfloat16)
            update = jnp.dot(w_out[...], hidden, preferred_element_type=jnp.float32)
            update = update.astype(jnp.bfloat16).astype(jnp.float32)
            here = slice(n * TILE, (n + 1) * TILE)
            state[j, :, here] = (slab[j, :, here].astype(jnp.float32) + steps[j] * update).astype(
                jnp.bfloat16
            )


def emit_back(plan, state, backs):
    grp, size = plan[1], len(backs)
    width = backs[0].shape[1]
    for k in range(size):
        rows = pl.ds(pl.multiple_of(lax.rem(grp - k + size, size) * width, width), width)
        for j in range(state.shape[0]):
            backs[k][j] = state[j, rows, :]


def first_kernel(size, plan, lay, put, flat, w_in, bias, w_out, slab, a_in, b_in, mine, below, above, old, old_below, old_above, *refs):
    pieces = refs[:size]
    kept, state, a_out, b_out, f_out = refs[size : size + 5]
    backs = refs[size + 5 : 2 * size + 5]
    inputs = refs[2 * size + 5]
    per_dev, channels = slab.shape[0], slab.shape[1]
    width, early = pieces[0].shape[2], old.shape[1]
    for j in range(per_dev):
        lanes = slice(j * SLAB, (j + 1) * SLAB)
        for k in range(size):
            for t in range(pieces[k].shape[1]):
                rows = channel_rows(plan[1], k, size, width, (1 + early + t) * channels)
                inputs[rows, lanes] = pieces[k][j, t]
        inputs[0:channels, lanes] = slab[j]

        def store(source):
            for t in range(early):
                inputs[(1 + t) * channels : (2 + t) * channels, lanes] = source[t]

        settle(plan, j, old, old_below, old_above, store)
    laplacian(plan, slab, a_in, b_in, mine, below, above, put, flat, inputs, HIST * channels)
    network(plan, inputs, slab, w_in, bias, w_out, state)
    emit_edges(plan, state, lay, a_out, b_out, f_out)
    emit_back(plan, state, backs)
    kept[...] = inputs[0 : (HIST - 1) * channels, :]


def second_kernel(size, plan, put, flat, w_in, bias, w_out, slab, a_in, b_in, mine, below, above, kept, *refs):
    backs = refs[:size]
    state, inputs = refs[size : size + 2]
    per_dev, channels = slab.shape[0], slab.shape[1]
    inputs[channels : HIST * channels, :] = kept[...]
    for j in range(per_dev):
        inputs[0:channels, j * SLAB : (j + 1) * SLAB] = slab[j]
    laplacian(plan, slab, a_in, b_in, mine, below, above, put, flat, inputs, HIST * channels)
    network(plan, inputs, slab, w_in, bias, w_out, state)
    emit_back(plan, state, backs)


def finish_kernel(size, plan, *refs):
    out = refs[-1]
    for k in range(size):
        for here, there in slab_lanes(lax.rem(plan[1] + k, size), size):
            for j in range(out.shape[0]):
                out[j, 0, :, there] = refs[k][j, :, here]


def local_folded(history, face_patch, refined, dest_slot, w_in, in_bias, w_out):
    bf16 = jnp.bfloat16
    per_dev, hist, width, cells = history.shape
    size = lax.axis_size("grp")
    channels = width * size
    doms = lax.axis_size("dom")
    smem = pl.BlockSpec(memory_space=SMEM)
    anywhere = pl.BlockSpec(memory_space=pl.ANY)
    shape = jax.ShapeDtypeStruct
    place = jnp.stack([lax.axis_index("dom"), lax.axis_index("grp")]).astype(jnp.int32)
    up_ring = [(i, (i + 1) % doms) for i in range(doms)]
    down_ring = [(i, (i - 1) % doms) for i in range(doms)]

    def state_block(t):
        return pl.BlockSpec((per_dev, 1, width, cells), lambda i: (0, t, 0, 0))

    def early_pack(first, states, *after):
        return pl.pallas_call(
            functools.partial(early_pack_kernel, size, states),
            grid=(1,),
            out_shape=[shape((per_dev, states, width, SLAB), bf16)] * size,
            in_specs=[smem] + [state_block(first + t) for t in range(states)] + [anywhere] * len(after),
            out_specs=[pl.BlockSpec((per_dev, states, width, SLAB), lambda i: (0, 0, 0, 0))] * size,
        )(place, *([history] * states), *after)

    early = 1
    late = hist - 1 - early
    newest = early_pack(0, 1)
    plan = pl.pallas_call(
        functools.partial(plan_kernel, per_dev),
        out_shape=shape((PLAN_SIZE,), jnp.int32),
        in_specs=[smem] * 4 + [anywhere] * size,
        out_specs=smem,
        name="plan",
    )(place, face_patch.T, refined, dest_slot, *newest)

    def movers(first, states):
        block = (1, 1, width, cells)
        return pl.pallas_call(
            send_kernel,
            grid_spec=pltpu.PrefetchScalarGridSpec(
                num_scalar_prefetch=1,
                grid=(states,),
                in_specs=[
                    pl.BlockSpec(block, lambda i, plan: (plan[2], first + i, 0, 0)),
                    pl.BlockSpec(block, lambda i, plan: (plan[3], first + i, 0, 0)),
                ],
                out_specs=[pl.BlockSpec((1, width, cells), lambda i, plan: (i, 0, 0))] * 2,
            ),
            out_shape=[shape((states, width, cells), bf16)] * 2,
        )(plan, history, history)

    def across_dom(up, down):
        return lax.ppermute(up, "dom", up_ring), lax.ppermute(down, "dom", down_ring)

    def pack(first, states, below, above, *after):
        whole = pl.BlockSpec((states, width, cells), lambda i: (0, 0, 0))
        block = (per_dev, states, width, SLAB)
        return pl.pallas_call(
            functools.partial(pack_kernel, size, states),
            grid=(1,),
            out_shape=[shape(block, bf16)] * size,
            in_specs=[smem, whole, whole]
            + [state_block(first + t) for t in range(states)]
            + [anywhere] * len(after),
            out_specs=[pl.BlockSpec(block, lambda i: (0, 0, 0, 0))] * size,
        )(plan, below, above, *([history] * states), *after)

    def across_grp(pieces, sign):
        moved = [pieces[0]]
        for k in range(1, size):
            moved.append(lax.ppermute(pieces[k], "grp", [(i, (i + sign * k) % size) for i in range(size)]))
        return moved

    pair_a = [(i, i ^ 1) for i in range(size)]
    pair_b = [(i, i if i in (0, size - 1) else ((i + 1) ^ 1) - 1) for i in range(size)]

    def exchange(a_out, b_out, f_out):
        a_in = lax.ppermute(a_out, "grp", pair_a)
        b_in = lax.ppermute(b_out, "grp", pair_b)
        below, above = across_dom(f_out, f_out)
        return a_in, b_in, f_out, below, above

    lay, put, flat = (jnp.asarray(table, bf16) for table in face_tables())
    w_in_t, w_out_t = w_in.T, w_out.T
    bias = in_bias[:, None]

    slab_shape = shape((per_dev, channels, SLAB), bf16)
    edge_shapes = [
        shape((per_dev, channels, HALF), bf16),
        shape((per_dev, channels, HALF), bf16),
        shape((per_dev, channels, FACE_LANES), bf16),
    ]
    back_shapes = [shape((per_dev, width, SLAB), bf16)] * size

    def gather(pieces, *after):
        states = pieces[0].shape[1]
        return pl.pallas_call(
            functools.partial(gather_kernel, size),
            out_shape=[shape((per_dev, states, channels, SLAB), bf16)]
            + [shape((states, channels, SLAB), bf16)] * 2,
            in_specs=[smem] + vmem_specs(size) + [anywhere] * len(after),
            out_specs=vmem_specs(3),
        )(plan, *pieces, *after)

    newest = across_grp(newest, 1)
    up, down = movers(1 + early, late)
    below, above = across_dom(up, down)
    middle = early_pack(1, early, up)
    old0, up0, down0 = gather(newest, *middle)
    middle = across_grp(middle, 1)
    below0, above0 = across_dom(up0, down0)
    packed = pack(1 + early, late, below, above, up0)
    oldest = across_grp(packed, 1)
    slab0, *edges = pl.pallas_call(
        edge_kernel,
        out_shape=[slab_shape] + edge_shapes,
        in_specs=[smem] + vmem_specs(4) + [anywhere] * size,
        out_specs=vmem_specs(4),
        name="edges",
    )(plan, lay, old0, below0, above0, *packed)
    old1, up1, down1 = gather(middle, *edges)
    below1, above1 = across_dom(up1, down1)

    inputs = pltpu.VMEM(((hist + 1) * channels, per_dev * SLAB), bf16)
    kept, slab1, *rest = pl.pallas_call(
        functools.partial(first_kernel, size),
        out_shape=[shape(((hist - 1) * channels, per_dev * SLAB), bf16), slab_shape] + edge_shapes + back_shapes,
        in_specs=[smem] + vmem_specs(15 + size),
        out_specs=vmem_specs(5 + size),
        scratch_shapes=[inputs],
        name="first",
    )(
        plan, lay, put, flat, w_in_t, bias, w_out_t, slab0, *exchange(*edges),
        old1, below1, above1, *oldest,
    )

    parts = exchange(*rest[:3])
    back1 = across_grp(rest[3:], -1)
    state = pltpu.VMEM((per_dev, channels, SLAB), bf16)
    back2 = pl.pallas_call(
        functools.partial(second_kernel, size),
        out_shape=back_shapes,
        in_specs=[smem] + vmem_specs(12),
        out_specs=vmem_specs(size),
        scratch_shapes=[state, inputs],
        name="second",
    )(plan, put, flat, w_in_t, bias, w_out_t, slab1, *parts, kept)

    def finish(state, pieces, *before):
        return pl.pallas_call(
            functools.partial(finish_kernel, size),
            grid=(1,),
            out_shape=shape((per_dev, 2, width, cells), bf16),
            in_specs=[smem]
            + [pl.BlockSpec((per_dev, width, SLAB), lambda i: (0, 0, 0))] * size
            + [anywhere] * len(before),
            out_specs=state_block(state),
            input_output_aliases={1 + size: 0} if before else {},
        )(plan, *pieces, *before)

    out = finish(0, back1)
    back2 = across_grp(back2, -1)
    return finish(1, back2, out)


def solution(mesh):
    placed = (P("dom", None, "grp", None), P(), P(), P(), P(), P(), P())
    folded = mesh.shape["grp"] == 4

    def body(*arrays):
        return (local_folded if folded else local_general)(*arrays)

    return jax.shard_map(
        body, mesh=mesh, in_specs=placed, out_specs=P("dom", None, "grp", None), check_vma=False
    )
```

```python
import functools

import jax
import jax.numpy as jnp
import numpy as np
from jax import lax
from jax.experimental import pallas as pl
from jax.experimental.pallas import tpu as pltpu
from jax.sharding import PartitionSpec as P

SIDE = 16
HIST = 4
PLANE = SIDE * SIDE


OPPOSITE = np.array([1, 0, 3, 2, 5, 4])


def padded(array, sides, width):
    for axis, dim in sides:
        size, length = (lax.axis_size(axis), array.shape[dim])
        up = [(i, (i + 1) % size) for i in range(size - 1)]
        down = [(j, i) for i, j in up]
        last = lax.slice_in_dim(array, length - width, length, axis=dim)
        first = lax.slice_in_dim(array, 0, width, axis=dim)
        before = lax.ppermute(last, axis, up)
        after = lax.ppermute(first, axis, down)
        array = jnp.concatenate([before, array, after], axis=dim)
    return array


def select_table(side_len, stride, offset):
    rows = jnp.arange(side_len)[:, None]
    cols = jnp.arange(side_len * side_len)[None, :]
    return (cols == rows * stride + offset).astype(jnp.bfloat16)


def take_face(grid_rows, table):
    return jnp.einsum("ncxq,kq->ncxk", grid_rows, table, preferred_element_type=jnp.float32).astype(
        jnp.bfloat16
    )


def place_face(face_rows, table):
    return jnp.einsum("ncxk,kq->ncxq", face_rows, table, preferred_element_type=jnp.float32)


def laplace_cells(newest, positions, usable):
    how_many, channels, cell_count = newest.shape
    plane = SIDE * SIDE
    grid_rows = newest.reshape(how_many, channels, SIDE, plane)
    y_low = select_table(SIDE, 1, 0)
    y_high = select_table(SIDE, 1, plane - SIDE)
    z_low = select_table(SIDE, SIDE, 0)
    z_high = select_table(SIDE, SIDE, SIDE - 1)
    layers = jnp.stack(
        [
            grid_rows[:, :, 0, :],
            grid_rows[:, :, -1, :],
            take_face(grid_rows, y_low).reshape(how_many, channels, plane),
            take_face(grid_rows, y_high).reshape(how_many, channels, plane),
            take_face(grid_rows, z_low).reshape(how_many, channels, plane),
            take_face(grid_rows, z_high).reshape(how_many, channels, plane),
        ],
        1,
    )
    layers = layers[:, OPPOSITE]
    beside_all = padded(layers, (("dom", 0),), how_many)
    picked = beside_all[positions, jnp.arange(6)[None, :]]
    picked = jnp.where(usable[:, :, None, None], picked, jnp.zeros_like(picked))
    field = grid_rows.astype(jnp.float32)
    picked_wide = picked.astype(jnp.float32)
    x_plus = jnp.concatenate([field[:, :, 1:, :], picked_wide[:, 1][:, :, None, :]], 2)
    x_minus = jnp.concatenate([picked_wide[:, 0][:, :, None, :], field[:, :, :-1, :]], 2)
    zero_row = jnp.zeros((how_many, channels, SIDE, SIDE), jnp.float32)
    y_plus = jnp.concatenate([field[..., SIDE:], zero_row], 3)
    y_plus = y_plus + place_face(picked[:, 3].reshape(how_many, channels, SIDE, SIDE), y_high)
    y_minus = jnp.concatenate([zero_row, field[..., :-SIDE]], 3)
    y_minus = y_minus + place_face(picked[:, 2].reshape(how_many, channels, SIDE, SIDE), y_low)
    z_index = jnp.arange(plane) % SIDE
    zero_cell = jnp.zeros((how_many, channels, SIDE, 1), jnp.float32)
    z_plus = jnp.concatenate([field[..., 1:], zero_cell], 3)
    z_plus = jnp.where(z_index == SIDE - 1, 0.0, z_plus)
    z_plus = z_plus + place_face(picked[:, 5].reshape(how_many, channels, SIDE, SIDE), z_high)
    z_minus = jnp.concatenate([zero_cell, field[..., :-1]], 3)
    z_minus = jnp.where(z_index == 0, 0.0, z_minus)
    z_minus = z_minus + place_face(picked[:, 4].reshape(how_many, channels, SIDE, SIDE), z_low)
    neighbour_sum = x_plus + x_minus + y_plus + y_minus + z_plus + z_minus
    spread = neighbour_sum - 6.0 * field
    return spread.reshape(how_many, channels, cell_count).astype(jnp.bfloat16)


def local_general(history, face_patch, refined, dest_slot, w_in, in_bias, w_out):
    per_dev = history.shape[0]
    my_index = lax.axis_index("dom")
    lowest = (my_index - 1) * per_dev
    my_slots = my_index * per_dev + jnp.arange(per_dev, dtype=jnp.int32)
    patch_ids = jnp.arange(dest_slot.shape[0], dtype=jnp.int32)
    inverse = jnp.zeros_like(dest_slot).at[dest_slot].set(patch_ids)

    def advance(inputs):
        how_many = inputs.shape[0]
        cell_count = inputs.shape[3]
        stacked = inputs.reshape(how_many, -1, cell_count)
        preact = (
            jnp.einsum("nkc,kh->nch", stacked, w_in, preferred_element_type=jnp.float32) + in_bias
        )
        hidden = jax.nn.silu(preact).astype(jnp.bfloat16)
        update = jnp.einsum(
            "nch,hk->nkc", hidden, w_out, preferred_element_type=jnp.float32
        ).astype(jnp.bfloat16)
        back = lax.all_to_all(update, "grp", split_axis=1, concat_axis=2, tiled=True)
        return (back, update, inputs[:, : HIST - 1])

    first_nb = face_patch[my_slots]
    first_pos = jnp.clip(first_nb - lowest, 0, 3 * per_dev - 1)
    first_ok = first_nb >= 0
    first_spread = laplace_cells(history[:, 0], first_pos, first_ok)
    first_in = jnp.concatenate([history, first_spread[:, None]], 1)
    first_back, _, _ = advance(
        lax.all_to_all(first_in, "grp", split_axis=3, concat_axis=2, tiled=True)
    )
    first_step = 1.0 - 0.5 * refined[my_slots].astype(jnp.float32)
    first_state = (
        history[:, 0].astype(jnp.float32)
        + first_step[:, None, None] * first_back.astype(jnp.float32)
    ).astype(jnp.bfloat16)
    carried = jnp.concatenate([first_state[:, None], history[:, : HIST - 1]], 1)
    owners = inverse[my_slots]
    second_nb = face_patch[owners]
    second_pos = jnp.clip(dest_slot[jnp.maximum(second_nb, 0)] - lowest, 0, 3 * per_dev - 1)
    second_ok = second_nb >= 0
    second_step = 1.0 - 0.5 * refined[owners].astype(jnp.float32)
    sources = inverse[my_slots]
    beside_all = padded(carried.reshape(per_dev, -1), (("dom", 0),), per_dev)
    moved_carried = jnp.take(beside_all, sources - lowest, axis=0).reshape(carried.shape)
    newest = moved_carried[:, 0]
    second_spread = laplace_cells(newest, second_pos, second_ok)
    second_in = jnp.concatenate([moved_carried, second_spread[:, None]], 1)
    second_back, _, _ = advance(
        lax.all_to_all(second_in, "grp", split_axis=3, concat_axis=2, tiled=True)
    )
    second_state = (
        newest.astype(jnp.float32) + second_step[:, None, None] * second_back.astype(jnp.float32)
    ).astype(jnp.bfloat16)
    return jnp.stack([moved_carried[:, 0], second_state], 1)


SLAB = 4 * PLANE
HALF = 2 * PLANE
FACE_LANES = 3 * PLANE
PLAN_SIZE = 64
SMALL, LARGE = 8, 16
VMEM = pltpu.VMEM
SMEM = pltpu.SMEM


def face_tables():
    lay = np.zeros((SLAB, PLANE), np.float32)
    put = np.zeros((PLANE, SLAB), np.float32)
    source = {2: lambda m: 240 + m, 3: lambda m: m, 4: lambda m: 16 * m + 15, 5: lambda m: 16 * m}
    target = {2: lambda m: m, 3: lambda m: 240 + m, 4: lambda m: 16 * m, 5: lambda m: 16 * m + 15}
    for face in (2, 3, 4, 5):
        for plane in range(4):
            for m in range(SIDE):
                lane = (face - 2) * 64 + plane * 16 + m
                lay[plane * PLANE + source[face](m), lane] = 1
                put[lane, plane * PLANE + target[face](m)] = 1
    flat = np.zeros((PLANE, PLANE), np.float32)
    for y in range(SIDE):
        for z in range(SIDE):
            flat[y * SIDE + z, y * SIDE + z] = -6
            for dy, dz in ((1, 0), (-1, 0), (0, 1), (0, -1)):
                if 0 <= y + dy < SIDE and 0 <= z + dz < SIDE:
                    flat[(y + dy) * SIDE + z + dz, y * SIDE + z] = 1
    return lay, put, flat


def grant(mebibytes):
    return pltpu.CompilerParams(vmem_limit_bytes=mebibytes * 2**20)


def vmem_specs(count):
    return [pl.BlockSpec(memory_space=VMEM)] * count


def plan_kernel(per_dev, place, face_patch, refined, dest_slot, *refs):
    plan = refs[-1]
    dom, grp = place[0], place[1]
    patches = dest_slot.shape[0]
    plan[0] = dom
    plan[1] = grp
    up, down = jnp.int32(0), jnp.int32(0)
    for s in range(per_dev):
        new_dom = dest_slot[dom * per_dev + s] // per_dev
        up = jnp.where(new_dom == dom + 1, s, up)
        down = jnp.where(new_dom == dom - 1, s, down)
    plan[2] = up
    plan[3] = down
    for j in range(per_dev):
        code, patch = jnp.int32(0), jnp.int32(0)
        for o in (-1, 0, 1):
            for s in range(per_dev):
                p = (dom + o) * per_dev + s
                ok = (p >= 0) & (p < patches)
                p = jnp.clip(p, 0, patches - 1)
                ok = ok & (dest_slot[p] == dom * per_dev + j)
                code = jnp.where(ok, s if o == 0 else per_dev + (o + 1) // 2, code)
                patch = jnp.where(ok, p, patch)
        plan[4 + j] = code
        plan[6 + j] = refined[patch]
        for f in range(6):
            beside = face_patch[f, patch]
            slot = dest_slot[jnp.maximum(beside, 0)]
            plan[8 + 6 * j + f] = jnp.where(beside < 0, -1, slot - (dom - 1) * per_dev)


def slab_lanes(slab, size):
    low = pl.multiple_of(slab * HALF, HALF)
    high = pl.multiple_of((2 * size - 1 - slab) * HALF, HALF)
    return ((slice(0, HALF), pl.ds(low, HALF)), (slice(HALF, SLAB), pl.ds(high, HALF)))


def channel_rows(grp, k, size, width, first=0):
    row = lax.rem(grp - k + size, size) * width
    return pl.ds(pl.multiple_of(first + row, width), width)


def settle(plan, j, own, below, above, store):
    per_dev = own.shape[0]
    code = plan[4 + j]

    @pl.when(code < per_dev)
    def _():
        store(own.at[jnp.minimum(code, per_dev - 1)])

    @pl.when(code == per_dev)
    def _():
        store(below)

    @pl.when(code == per_dev + 1)
    def _():
        store(above)


def send_kernel(plan, up_in, down_in, up_out, down_out):
    up_out[...] = up_in[0]
    down_out[...] = down_in[0]


def early_pack_kernel(size, states, place, *refs):
    for k in range(1, size + 1):
        k = k % size
        out = refs[k - size]
        for here, there in slab_lanes(lax.rem(place[1] + k, size), size):
            for t in range(states):
                for j in range(out.shape[0]):
                    out[j, t, :, here] = refs[t][j, 0, :, there]


def pack_kernel(size, states, plan, below, above, *refs):
    outs = refs[-size:]
    for t in range(states):
        for j in range(refs[t].shape[0]):

            def store(source):
                for k in range(1, size + 1):
                    k = k % size
                    for here, there in slab_lanes(lax.rem(plan[1] + k, size), size):
                        outs[k][j, t, :, here] = source[0, :, there]

            settle(plan, j, refs[t], below.at[pl.ds(t, 1)], above.at[pl.ds(t, 1)], store)


def emit_edges(plan, slab, lay, a_out, b_out, f_out):
    even = lax.rem(plan[1], 2) == 0
    for j in range(slab.shape[0]):
        @pl.when(even)
        def _():
            a_out[j] = slab[j, :, PLANE : 3 * PLANE]
            b_out[j, :, 0:PLANE] = slab[j, :, 0:PLANE]
            b_out[j, :, PLANE:HALF] = slab[j, :, 3 * PLANE : SLAB]

        @pl.when(jnp.logical_not(even))
        def _():
            b_out[j] = slab[j, :, PLANE : 3 * PLANE]
            a_out[j, :, 0:PLANE] = slab[j, :, 0:PLANE]
            a_out[j, :, PLANE:HALF] = slab[j, :, 3 * PLANE : SLAB]

        f_out[j, :, 0:PLANE] = jnp.dot(
            slab[j], lay[...], preferred_element_type=jnp.float32
        ).astype(jnp.bfloat16)
        f_out[j, :, PLANE:HALF] = slab[j, :, 0:PLANE]
        f_out[j, :, HALF:FACE_LANES] = slab[j, :, 3 * PLANE : SLAB]


def gather_kernel(size, plan, *refs):
    pieces, (slab, up, down) = refs[:size], refs[-3:]
    per_dev, states, width = pieces[0].shape[:3]
    for k in range(size):
        rows = channel_rows(plan[1], k, size, width)
        for t in range(states):
            up[t, rows] = pieces[k][plan[2], t]
            down[t, rows] = pieces[k][plan[3], t]
            for j in range(per_dev):
                slab[j, t, rows] = pieces[k][j, t]


def edge_kernel(plan, lay, old, below, above, *refs):
    slab, a_out, b_out, f_out = refs[-4:]
    for j in range(slab.shape[0]):

        def store(source):
            slab[j] = source[0]

        settle(plan, j, old, below, above, store)
    emit_edges(plan, slab, lay, a_out, b_out, f_out)


def laplacian(plan, slab, a_in, b_in, mine, below, above, put, flat, spread, first_row):
    f32 = jnp.float32
    grp = plan[1]
    per_dev, channels = slab.shape[0], slab.shape[1]
    even = lax.rem(grp, 2) == 0
    lowest, highest = grp == 0, grp == 3
    cands = [ref.at[s] for ref in (below, mine, above) for s in range(per_dev)]
    face_of_lane = lax.broadcasted_iota(jnp.int32, (channels, PLANE), 1) // 64
    for j in range(per_dev):
        layer = [slab[j, :, i * PLANE : (i + 1) * PLANE] for i in range(4)]
        wide = [x.astype(f32) for x in layer]
        a, b = a_in[j].astype(f32), b_in[j].astype(f32)
        inner = jnp.where(even, a, b)
        outer = jnp.where(even, b, a)
        inner0 = jnp.where(highest, wide[2], inner[:, :PLANE])
        inner1 = jnp.where(highest, wide[1], inner[:, PLANE:])
        code = [plan[8 + 6 * j + f] for f in range(6)]
        lane_code = jnp.where(
            face_of_lane < 2,
            jnp.where(face_of_lane == 0, code[2], code[3]),
            jnp.where(face_of_lane == 2, code[4], code[5]),
        )
        face0 = jnp.zeros((channels, PLANE), f32)
        face1 = jnp.zeros((channels, PLANE), f32)
        rest = jnp.zeros((channels, PLANE), f32)
        for c, cand in enumerate(cands):
            face0 = jnp.where(code[0] == c, cand[:, HALF:FACE_LANES].astype(f32), face0)
            face1 = jnp.where(code[1] == c, cand[:, PLANE:HALF].astype(f32), face1)
            rest = jnp.where(lane_code == c, cand[:, 0:PLANE].astype(f32), rest)
        outer0 = jnp.where(lowest, face0, outer[:, :PLANE])
        outer1 = jnp.where(lowest, face1, outer[:, PLANE:])
        placed = jnp.dot(rest.astype(jnp.bfloat16), put[...], preferred_element_type=f32)
        sides = (
            (outer0, wide[1]),
            (wide[0], inner0),
            (inner1, wide[3]),
            (wide[2], outer1),
        )
        for i in range(4):
            total = jnp.dot(layer[i], flat[...], preferred_element_type=f32)
            total = total + placed[:, i * PLANE : (i + 1) * PLANE] + sides[i][0] + sides[i][1]
            spread[first_row : first_row + channels, j * SLAB + i * PLANE : j * SLAB + (i + 1) * PLANE] = (
                total.astype(jnp.bfloat16)
            )


TILE = 512


def network(plan, inputs, slab, w_in, bias, w_out, state):
    per_dev = slab.shape[0]
    per_slab = SLAB // TILE
    steps = [1.0 - 0.5 * plan[6 + j].astype(jnp.float32) for j in range(per_dev)]
    for j in range(per_dev):
        for n in range(per_slab):
            lanes = slice(j * SLAB + n * TILE, j * SLAB + (n + 1) * TILE)
            pre = jnp.dot(w_in[...], inputs[:, lanes], preferred_element_type=jnp.float32) + bias[...]
            half = 0.5 * pre
            hidden = (half + half * jnp.tanh(half)).astype(jnp.bfloat16)
            update = jnp.dot(w_out[...], hidden, preferred_element_type=jnp.float32)
            update = update.astype(jnp.bfloat16).astype(jnp.float32)
            here = slice(n * TILE, (n + 1) * TILE)
            state[j, :, here] = (slab[j, :, here].astype(jnp.float32) + steps[j] * update).astype(
                jnp.bfloat16
            )


def emit_back(plan, state, backs):
    grp, size = plan[1], len(backs)
    width = backs[0].shape[1]
    for k in range(size):
        rows = pl.ds(pl.multiple_of(lax.rem(grp - k + size, size) * width, width), width)
        for j in range(state.shape[0]):
            backs[k][j] = state[j, rows, :]


def first_kernel(size, plan, lay, put, flat, w_in, bias, w_out, slab, a_in, b_in, mine, below, above, old, old_below, old_above, *refs):
    pieces = refs[:size]
    kept, state, a_out, b_out, f_out = refs[size : size + 5]
    backs = refs[size + 5 : 2 * size + 5]
    inputs = refs[2 * size + 5]
    per_dev, channels = slab.shape[0], slab.shape[1]
    width, early = pieces[0].shape[2], old.shape[1]
    for j in range(per_dev):
        lanes = slice(j * SLAB, (j + 1) * SLAB)
        for k in range(size):
            for t in range(pieces[k].shape[1]):
                rows = channel_rows(plan[1], k, size, width, (1 + early + t) * channels)
                inputs[rows, lanes] = pieces[k][j, t]
        inputs[0:channels, lanes] = slab[j]

        def store(source):
            for t in range(early):
                inputs[(1 + t) * channels : (2 + t) * channels, lanes] = source[t]

        settle(plan, j, old, old_below, old_above, store)
    laplacian(plan, slab, a_in, b_in, mine, below, above, put, flat, inputs, HIST * channels)
    network(plan, inputs, slab, w_in, bias, w_out, state)
    emit_edges(plan, state, lay, a_out, b_out, f_out)
    emit_back(plan, state, backs)
    kept[...] = inputs[0 : (HIST - 1) * channels, :]


def second_kernel(size, plan, put, flat, w_in, bias, w_out, slab, a_in, b_in, mine, below, above, kept, *refs):
    backs = refs[:size]
    state, inputs = refs[size : size + 2]
    per_dev, channels = slab.shape[0], slab.shape[1]
    inputs[channels : HIST * channels, :] = kept[...]
    for j in range(per_dev):
        inputs[0:channels, j * SLAB : (j + 1) * SLAB] = slab[j]
    laplacian(plan, slab, a_in, b_in, mine, below, above, put, flat, inputs, HIST * channels)
    network(plan, inputs, slab, w_in, bias, w_out, state)
    emit_back(plan, state, backs)


def finish_kernel(size, plan, *refs):
    out = refs[-1]
    for k in range(size):
        for here, there in slab_lanes(lax.rem(plan[1] + k, size), size):
            for j in range(out.shape[0]):
                out[j, 0, :, there] = refs[k][j, :, here]


def local_folded(history, face_patch, refined, dest_slot, w_in, in_bias, w_out):
    bf16 = jnp.bfloat16
    per_dev, hist, width, cells = history.shape
    size = lax.axis_size("grp")
    channels = width * size
    doms = lax.axis_size("dom")
    smem = pl.BlockSpec(memory_space=SMEM)
    anywhere = pl.BlockSpec(memory_space=pl.ANY)
    shape = jax.ShapeDtypeStruct
    place = jnp.stack([lax.axis_index("dom"), lax.axis_index("grp")]).astype(jnp.int32)
    up_ring = [(i, (i + 1) % doms) for i in range(doms)]
    down_ring = [(i, (i - 1) % doms) for i in range(doms)]

    def state_block(t):
        return pl.BlockSpec((per_dev, 1, width, cells), lambda i: (0, t, 0, 0))

    def early_pack(first, states, *after):
        return pl.pallas_call(
            functools.partial(early_pack_kernel, size, states),
            grid=(1,),
            out_shape=[shape((per_dev, states, width, SLAB), bf16)] * size,
            in_specs=[smem] + [state_block(first + t) for t in range(states)] + [anywhere] * len(after),
            out_specs=vmem_specs(size),
            compiler_params=grant(SMALL),
        )(place, *([history] * states), *after)

    early = 1
    late = hist - 1 - early
    newest = early_pack(0, 1)
    plan = pl.pallas_call(
        functools.partial(plan_kernel, per_dev),
        out_shape=shape((PLAN_SIZE,), jnp.int32),
        in_specs=[smem] * 4 + [anywhere] * size,
        out_specs=smem,
        compiler_params=grant(SMALL),
        name="plan",
    )(place, face_patch.T, refined, dest_slot, *newest)

    def movers(first, states):
        block = (1, 1, width, cells)
        return pl.pallas_call(
            send_kernel,
            grid_spec=pltpu.PrefetchScalarGridSpec(
                num_scalar_prefetch=1,
                grid=(states,),
                in_specs=[
                    pl.BlockSpec(block, lambda i, plan: (plan[2], first + i, 0, 0)),
                    pl.BlockSpec(block, lambda i, plan: (plan[3], first + i, 0, 0)),
                ],
                out_specs=[pl.BlockSpec((1, width, cells), lambda i, plan: (i, 0, 0))] * 2,
            ),
            out_shape=[shape((states, width, cells), bf16)] * 2,
            compiler_params=grant(SMALL),
        )(plan, history, history)

    def across_dom(up, down):
        return lax.ppermute(up, "dom", up_ring), lax.ppermute(down, "dom", down_ring)

    def pack(first, states, below, above, *after):
        block = (per_dev, states, width, SLAB)
        return pl.pallas_call(
            functools.partial(pack_kernel, size, states),
            grid=(1,),
            out_shape=[shape(block, bf16)] * size,
            in_specs=[smem] + vmem_specs(2)
            + [state_block(first + t) for t in range(states)]
            + [anywhere] * len(after),
            out_specs=vmem_specs(size),
            compiler_params=grant(SMALL),
        )(plan, below, above, *([history] * states), *after)

    def across_grp(pieces, sign):
        moved = [pieces[0]]
        for k in range(1, size):
            moved.append(lax.ppermute(pieces[k], "grp", [(i, (i + sign * k) % size) for i in range(size)]))
        return moved

    pair_a = [(i, i ^ 1) for i in range(size)]
    pair_b = [(i, i if i in (0, size - 1) else ((i + 1) ^ 1) - 1) for i in range(size)]

    def exchange(a_out, b_out, f_out):
        a_in = lax.ppermute(a_out, "grp", pair_a)
        b_in = lax.ppermute(b_out, "grp", pair_b)
        below, above = across_dom(f_out, f_out)
        return a_in, b_in, f_out, below, above

    lay, put, flat = (jnp.asarray(table, bf16) for table in face_tables())
    w_in_t, w_out_t = w_in.T, w_out.T
    bias = in_bias[:, None]

    slab_shape = shape((per_dev, channels, SLAB), bf16)
    edge_shapes = [
        shape((per_dev, channels, HALF), bf16),
        shape((per_dev, channels, HALF), bf16),
        shape((per_dev, channels, FACE_LANES), bf16),
    ]
    back_shapes = [shape((per_dev, width, SLAB), bf16)] * size

    def gather(pieces, *after):
        states = pieces[0].shape[1]
        return pl.pallas_call(
            functools.partial(gather_kernel, size),
            out_shape=[shape((per_dev, states, channels, SLAB), bf16)]
            + [shape((states, channels, SLAB), bf16)] * 2,
            in_specs=[smem] + vmem_specs(size) + [anywhere] * len(after),
            out_specs=vmem_specs(3),
            compiler_params=grant(SMALL),
        )(plan, *pieces, *after)

    newest = across_grp(newest, 1)
    up, down = movers(1 + early, late)
    below, above = across_dom(up, down)
    middle = early_pack(1, early, up)
    old0, up0, down0 = gather(newest, *middle)
    middle = across_grp(middle, 1)
    below0, above0 = across_dom(up0, down0)
    packed = pack(1 + early, late, below, above, up0)
    oldest = across_grp(packed, 1)
    slab0, *edges = pl.pallas_call(
        edge_kernel,
        out_shape=[slab_shape] + edge_shapes,
        in_specs=[smem] + vmem_specs(4) + [anywhere] * size,
        out_specs=vmem_specs(4),
        compiler_params=grant(SMALL),
        name="edges",
    )(plan, lay, old0, below0, above0, *packed)
    old1, up1, down1 = gather(middle, *edges)
    below1, above1 = across_dom(up1, down1)

    inputs = pltpu.VMEM(((hist + 1) * channels, per_dev * SLAB), bf16)
    kept, slab1, *rest = pl.pallas_call(
        functools.partial(first_kernel, size),
        out_shape=[shape(((hist - 1) * channels, per_dev * SLAB), bf16), slab_shape] + edge_shapes + back_shapes,
        in_specs=[smem] + vmem_specs(15 + size),
        out_specs=vmem_specs(5 + size),
        scratch_shapes=[inputs],
        compiler_params=grant(LARGE),
        name="first",
    )(
        plan, lay, put, flat, w_in_t, bias, w_out_t, slab0, *exchange(*edges),
        old1, below1, above1, *oldest,
    )

    parts = exchange(*rest[:3])
    back1 = across_grp(rest[3:], -1)
    state = pltpu.VMEM((per_dev, channels, SLAB), bf16)
    back2 = pl.pallas_call(
        functools.partial(second_kernel, size),
        out_shape=back_shapes,
        in_specs=[smem] + vmem_specs(12),
        out_specs=vmem_specs(size),
        scratch_shapes=[state, inputs],
        compiler_params=grant(LARGE),
        name="second",
    )(plan, put, flat, w_in_t, bias, w_out_t, slab1, *parts, kept)

    def finish(state, pieces, *before):
        return pl.pallas_call(
            functools.partial(finish_kernel, size),
            grid=(1,),
            out_shape=shape((per_dev, 2, width, cells), bf16),
            in_specs=[smem] + vmem_specs(size) + [anywhere] * len(before),
            out_specs=state_block(state),
            input_output_aliases={1 + size: 0} if before else {},
            compiler_params=grant(SMALL),
        )(plan, *pieces, *before)

    out = finish(0, back1)
    back2 = across_grp(back2, -1)
    return finish(1, back2, out)


def solution(mesh):
    placed = (P("dom", None, "grp", None), P(), P(), P(), P(), P(), P())
    folded = mesh.shape["grp"] == 4

    def body(*arrays):
        return (local_folded if folded else local_general)(*arrays)

    return jax.shard_map(
        body, mesh=mesh, in_specs=placed, out_specs=P("dom", None, "grp", None), check_vma=False
    )
```

```python
import functools

import jax
import jax.numpy as jnp
import numpy as np
from jax import lax
from jax.experimental import pallas as pl
from jax.experimental.pallas import tpu as pltpu
from jax.sharding import PartitionSpec as P

SIDE = 16
HIST = 4
PLANE = SIDE * SIDE


OPPOSITE = np.array([1, 0, 3, 2, 5, 4])


def padded(array, sides, width):
    for axis, dim in sides:
        size, length = (lax.axis_size(axis), array.shape[dim])
        up = [(i, (i + 1) % size) for i in range(size - 1)]
        down = [(j, i) for i, j in up]
        last = lax.slice_in_dim(array, length - width, length, axis=dim)
        first = lax.slice_in_dim(array, 0, width, axis=dim)
        before = lax.ppermute(last, axis, up)
        after = lax.ppermute(first, axis, down)
        array = jnp.concatenate([before, array, after], axis=dim)
    return array


def select_table(side_len, stride, offset):
    rows = jnp.arange(side_len)[:, None]
    cols = jnp.arange(side_len * side_len)[None, :]
    return (cols == rows * stride + offset).astype(jnp.bfloat16)


def take_face(grid_rows, table):
    return jnp.einsum("ncxq,kq->ncxk", grid_rows, table, preferred_element_type=jnp.float32).astype(
        jnp.bfloat16
    )


def place_face(face_rows, table):
    return jnp.einsum("ncxk,kq->ncxq", face_rows, table, preferred_element_type=jnp.float32)


def laplace_cells(newest, positions, usable):
    how_many, channels, cell_count = newest.shape
    plane = SIDE * SIDE
    grid_rows = newest.reshape(how_many, channels, SIDE, plane)
    y_low = select_table(SIDE, 1, 0)
    y_high = select_table(SIDE, 1, plane - SIDE)
    z_low = select_table(SIDE, SIDE, 0)
    z_high = select_table(SIDE, SIDE, SIDE - 1)
    layers = jnp.stack(
        [
            grid_rows[:, :, 0, :],
            grid_rows[:, :, -1, :],
            take_face(grid_rows, y_low).reshape(how_many, channels, plane),
            take_face(grid_rows, y_high).reshape(how_many, channels, plane),
            take_face(grid_rows, z_low).reshape(how_many, channels, plane),
            take_face(grid_rows, z_high).reshape(how_many, channels, plane),
        ],
        1,
    )
    layers = layers[:, OPPOSITE]
    beside_all = padded(layers, (("dom", 0),), how_many)
    picked = beside_all[positions, jnp.arange(6)[None, :]]
    picked = jnp.where(usable[:, :, None, None], picked, jnp.zeros_like(picked))
    field = grid_rows.astype(jnp.float32)
    picked_wide = picked.astype(jnp.float32)
    x_plus = jnp.concatenate([field[:, :, 1:, :], picked_wide[:, 1][:, :, None, :]], 2)
    x_minus = jnp.concatenate([picked_wide[:, 0][:, :, None, :], field[:, :, :-1, :]], 2)
    zero_row = jnp.zeros((how_many, channels, SIDE, SIDE), jnp.float32)
    y_plus = jnp.concatenate([field[..., SIDE:], zero_row], 3)
    y_plus = y_plus + place_face(picked[:, 3].reshape(how_many, channels, SIDE, SIDE), y_high)
    y_minus = jnp.concatenate([zero_row, field[..., :-SIDE]], 3)
    y_minus = y_minus + place_face(picked[:, 2].reshape(how_many, channels, SIDE, SIDE), y_low)
    z_index = jnp.arange(plane) % SIDE
    zero_cell = jnp.zeros((how_many, channels, SIDE, 1), jnp.float32)
    z_plus = jnp.concatenate([field[..., 1:], zero_cell], 3)
    z_plus = jnp.where(z_index == SIDE - 1, 0.0, z_plus)
    z_plus = z_plus + place_face(picked[:, 5].reshape(how_many, channels, SIDE, SIDE), z_high)
    z_minus = jnp.concatenate([zero_cell, field[..., :-1]], 3)
    z_minus = jnp.where(z_index == 0, 0.0, z_minus)
    z_minus = z_minus + place_face(picked[:, 4].reshape(how_many, channels, SIDE, SIDE), z_low)
    neighbour_sum = x_plus + x_minus + y_plus + y_minus + z_plus + z_minus
    spread = neighbour_sum - 6.0 * field
    return spread.reshape(how_many, channels, cell_count).astype(jnp.bfloat16)


def local_general(history, face_patch, refined, dest_slot, w_in, in_bias, w_out):
    per_dev = history.shape[0]
    my_index = lax.axis_index("dom")
    lowest = (my_index - 1) * per_dev
    my_slots = my_index * per_dev + jnp.arange(per_dev, dtype=jnp.int32)
    patch_ids = jnp.arange(dest_slot.shape[0], dtype=jnp.int32)
    inverse = jnp.zeros_like(dest_slot).at[dest_slot].set(patch_ids)

    def advance(inputs):
        how_many = inputs.shape[0]
        cell_count = inputs.shape[3]
        stacked = inputs.reshape(how_many, -1, cell_count)
        preact = (
            jnp.einsum("nkc,kh->nch", stacked, w_in, preferred_element_type=jnp.float32) + in_bias
        )
        hidden = jax.nn.silu(preact).astype(jnp.bfloat16)
        update = jnp.einsum(
            "nch,hk->nkc", hidden, w_out, preferred_element_type=jnp.float32
        ).astype(jnp.bfloat16)
        back = lax.all_to_all(update, "grp", split_axis=1, concat_axis=2, tiled=True)
        return (back, update, inputs[:, : HIST - 1])

    first_nb = face_patch[my_slots]
    first_pos = jnp.clip(first_nb - lowest, 0, 3 * per_dev - 1)
    first_ok = first_nb >= 0
    first_spread = laplace_cells(history[:, 0], first_pos, first_ok)
    first_in = jnp.concatenate([history, first_spread[:, None]], 1)
    first_back, _, _ = advance(
        lax.all_to_all(first_in, "grp", split_axis=3, concat_axis=2, tiled=True)
    )
    first_step = 1.0 - 0.5 * refined[my_slots].astype(jnp.float32)
    first_state = (
        history[:, 0].astype(jnp.float32)
        + first_step[:, None, None] * first_back.astype(jnp.float32)
    ).astype(jnp.bfloat16)
    carried = jnp.concatenate([first_state[:, None], history[:, : HIST - 1]], 1)
    owners = inverse[my_slots]
    second_nb = face_patch[owners]
    second_pos = jnp.clip(dest_slot[jnp.maximum(second_nb, 0)] - lowest, 0, 3 * per_dev - 1)
    second_ok = second_nb >= 0
    second_step = 1.0 - 0.5 * refined[owners].astype(jnp.float32)
    sources = inverse[my_slots]
    beside_all = padded(carried.reshape(per_dev, -1), (("dom", 0),), per_dev)
    moved_carried = jnp.take(beside_all, sources - lowest, axis=0).reshape(carried.shape)
    newest = moved_carried[:, 0]
    second_spread = laplace_cells(newest, second_pos, second_ok)
    second_in = jnp.concatenate([moved_carried, second_spread[:, None]], 1)
    second_back, _, _ = advance(
        lax.all_to_all(second_in, "grp", split_axis=3, concat_axis=2, tiled=True)
    )
    second_state = (
        newest.astype(jnp.float32) + second_step[:, None, None] * second_back.astype(jnp.float32)
    ).astype(jnp.bfloat16)
    return jnp.stack([moved_carried[:, 0], second_state], 1)


SLAB = 4 * PLANE
HALF = 2 * PLANE
FACE_LANES = 3 * PLANE
PLAN_SIZE = 64
SMALL, LARGE = 8, 16
VMEM = pltpu.VMEM
SMEM = pltpu.SMEM


def face_tables():
    lay = np.zeros((SLAB, PLANE), np.float32)
    put = np.zeros((PLANE, SLAB), np.float32)
    source = {2: lambda m: 240 + m, 3: lambda m: m, 4: lambda m: 16 * m + 15, 5: lambda m: 16 * m}
    target = {2: lambda m: m, 3: lambda m: 240 + m, 4: lambda m: 16 * m, 5: lambda m: 16 * m + 15}
    for face in (2, 3, 4, 5):
        for plane in range(4):
            for m in range(SIDE):
                lane = (face - 2) * 64 + plane * 16 + m
                lay[plane * PLANE + source[face](m), lane] = 1
                put[lane, plane * PLANE + target[face](m)] = 1
    flat = np.zeros((PLANE, PLANE), np.float32)
    for y in range(SIDE):
        for z in range(SIDE):
            flat[y * SIDE + z, y * SIDE + z] = -6
            for dy, dz in ((1, 0), (-1, 0), (0, 1), (0, -1)):
                if 0 <= y + dy < SIDE and 0 <= z + dz < SIDE:
                    flat[(y + dy) * SIDE + z + dz, y * SIDE + z] = 1
    return lay, put, flat


def grant(mebibytes):
    return pltpu.CompilerParams(vmem_limit_bytes=mebibytes * 2**20)


def vmem_specs(count):
    return [pl.BlockSpec(memory_space=VMEM)] * count


def plan_kernel(per_dev, place, face_patch, refined, dest_slot, *refs):
    plan = refs[-1]
    dom, grp = place[0], place[1]
    patches = dest_slot.shape[0]
    plan[0] = dom
    plan[1] = grp
    up, down = jnp.int32(0), jnp.int32(0)
    for s in range(per_dev):
        new_dom = dest_slot[dom * per_dev + s] // per_dev
        up = jnp.where(new_dom == dom + 1, s, up)
        down = jnp.where(new_dom == dom - 1, s, down)
    plan[2] = up
    plan[3] = down
    for j in range(per_dev):
        code, patch = jnp.int32(0), jnp.int32(0)
        for o in (-1, 0, 1):
            for s in range(per_dev):
                p = (dom + o) * per_dev + s
                ok = (p >= 0) & (p < patches)
                p = jnp.clip(p, 0, patches - 1)
                ok = ok & (dest_slot[p] == dom * per_dev + j)
                code = jnp.where(ok, s if o == 0 else per_dev + (o + 1) // 2, code)
                patch = jnp.where(ok, p, patch)
        plan[4 + j] = code
        plan[6 + j] = refined[patch]
        for f in range(6):
            beside = face_patch[f, patch]
            slot = dest_slot[jnp.maximum(beside, 0)]
            plan[8 + 6 * j + f] = jnp.where(beside < 0, -1, slot - (dom - 1) * per_dev)


def slab_lanes(slab, size):
    low = pl.multiple_of(slab * HALF, HALF)
    high = pl.multiple_of((2 * size - 1 - slab) * HALF, HALF)
    return ((slice(0, HALF), pl.ds(low, HALF)), (slice(HALF, SLAB), pl.ds(high, HALF)))


def channel_rows(grp, k, size, width, first=0):
    row = lax.rem(grp - k + size, size) * width
    return pl.ds(pl.multiple_of(first + row, width), width)


def settle(plan, j, own, below, above, store):
    per_dev = own.shape[0]
    code = plan[4 + j]

    @pl.when(code < per_dev)
    def _():
        store(own.at[jnp.minimum(code, per_dev - 1)])

    @pl.when(code == per_dev)
    def _():
        store(below)

    @pl.when(code == per_dev + 1)
    def _():
        store(above)


def send_kernel(plan, up_in, down_in, up_out, down_out):
    up_out[...] = up_in[0]
    down_out[...] = down_in[0]


def early_pack_kernel(size, states, place, *refs):
    for k in range(1, size + 1):
        k = k % size
        out = refs[k - size]
        for here, there in slab_lanes(lax.rem(place[1] + k, size), size):
            for t in range(states):
                for j in range(out.shape[0]):
                    out[j, t, :, here] = refs[t][j, 0, :, there]


def pack_kernel(size, states, plan, below, above, *refs):
    per_dev = refs[0].shape[0]
    outs = refs[-size * per_dev :]
    for j in range(per_dev):
        for t in range(states):

            def store(source):
                for k in range(1, size + 1):
                    k = k % size
                    for here, there in slab_lanes(lax.rem(plan[1] + k, size), size):
                        outs[j * size + k][t, :, here] = source[0, :, there]

            settle(plan, j, refs[t], below.at[pl.ds(t, 1)], above.at[pl.ds(t, 1)], store)


def emit_edges(plan, slab, lay, a_out, b_out, f_out):
    even = lax.rem(plan[1], 2) == 0
    for j in range(slab.shape[0]):
        @pl.when(even)
        def _():
            a_out[j] = slab[j, :, PLANE : 3 * PLANE]
            b_out[j, :, 0:PLANE] = slab[j, :, 0:PLANE]
            b_out[j, :, PLANE:HALF] = slab[j, :, 3 * PLANE : SLAB]

        @pl.when(jnp.logical_not(even))
        def _():
            b_out[j] = slab[j, :, PLANE : 3 * PLANE]
            a_out[j, :, 0:PLANE] = slab[j, :, 0:PLANE]
            a_out[j, :, PLANE:HALF] = slab[j, :, 3 * PLANE : SLAB]

        f_out[j, :, 0:PLANE] = jnp.dot(
            slab[j], lay[...], preferred_element_type=jnp.float32
        ).astype(jnp.bfloat16)
        f_out[j, :, PLANE:HALF] = slab[j, :, 0:PLANE]
        f_out[j, :, HALF:FACE_LANES] = slab[j, :, 3 * PLANE : SLAB]


def gather_kernel(size, plan, *refs):
    pieces, (slab, up, down) = refs[:size], refs[-3:]
    per_dev, states, width = pieces[0].shape[:3]
    for k in range(size):
        rows = channel_rows(plan[1], k, size, width)
        for t in range(states):
            up[t, rows] = pieces[k][plan[2], t]
            down[t, rows] = pieces[k][plan[3], t]
            for j in range(per_dev):
                slab[j, t, rows] = pieces[k][j, t]


def edge_kernel(plan, lay, old, below, above, *refs):
    slab, a_out, b_out, f_out = refs[-4:]
    for j in range(slab.shape[0]):

        def store(source):
            slab[j] = source[0]

        settle(plan, j, old, below, above, store)
    emit_edges(plan, slab, lay, a_out, b_out, f_out)


def laplacian(plan, slab, a_in, b_in, mine, below, above, put, flat, spread, first_row):
    f32, bf16 = jnp.float32, jnp.bfloat16
    grp = plan[1]
    per_dev, channels = slab.shape[0], slab.shape[1]
    odd = lax.rem(grp, 2)
    lowest, highest = (grp == 0).astype(jnp.int32), (grp == 3).astype(jnp.int32)

    def weight(chosen):
        return jnp.full((16, PLANE), chosen, jnp.int32).astype(f32).astype(bf16)

    def scaled(value, chosen):
        rows = value.shape[0]
        return (value.reshape(rows // 16, 16, PLANE) * chosen[None]).reshape(rows, PLANE)

    inner_a, inner_b, inner_own = weight(1 - odd), weight(odd - highest), weight(highest)
    outer_a, outer_b = weight(odd), weight(1 - odd - lowest)
    cands = [ref.at[s] for ref in (below, mine, above) for s in range(per_dev)]
    face_of_lane = lax.broadcasted_iota(jnp.int32, (16, PLANE), 1) // 64
    low, high = slice(0, PLANE), slice(PLANE, HALF)
    for j in range(per_dev):
        layer = [slab[j, :, i * PLANE : (i + 1) * PLANE] for i in range(4)]
        a, b = a_in[j], b_in[j]
        inner0 = scaled(a[:, low], inner_a) + scaled(b[:, low], inner_b) + scaled(layer[2], inner_own)
        inner1 = scaled(a[:, high], inner_a) + scaled(b[:, high], inner_b) + scaled(layer[1], inner_own)
        outer0 = scaled(a[:, low], outer_a) + scaled(b[:, low], outer_b)
        outer1 = scaled(a[:, high], outer_a) + scaled(b[:, high], outer_b)
        code = [plan[8 + 6 * j + f] for f in range(6)]
        lane_code = jnp.where(
            face_of_lane < 2,
            jnp.where(face_of_lane == 0, code[2], code[3]),
            jnp.where(face_of_lane == 2, code[4], code[5]),
        )
        rest = jnp.zeros((channels, PLANE), bf16)
        for c, cand in enumerate(cands):
            outer0 = outer0 + scaled(cand[:, HALF:FACE_LANES], weight(jnp.where(code[0] == c, lowest, 0)))
            outer1 = outer1 + scaled(cand[:, PLANE:HALF], weight(jnp.where(code[1] == c, lowest, 0)))
            rest = rest + scaled(cand[:, low], jnp.where(lane_code == c, 1.0, 0.0).astype(bf16))
        placed = jnp.dot(rest, put[...], preferred_element_type=f32)
        sides = ((outer0, layer[1]), (layer[0], inner0), (inner1, layer[3]), (layer[2], outer1))
        for i in range(4):
            total = jnp.dot(layer[i], flat[...], preferred_element_type=f32)
            total = total + placed[:, i * PLANE : (i + 1) * PLANE]
            total = total + sides[i][0].astype(f32) + sides[i][1].astype(f32)
            spread[first_row : first_row + channels, j * SLAB + i * PLANE : j * SLAB + (i + 1) * PLANE] = (
                total.astype(bf16)
            )


TILE = 512


def network(plan, j, inputs, slab, w_in, bias, w_out, state):
    step = 1.0 - 0.5 * plan[6 + j].astype(jnp.float32)
    for n in range(SLAB // TILE):
        lanes = slice(j * SLAB + n * TILE, j * SLAB + (n + 1) * TILE)
        shift = jnp.concatenate([bias[...]] * (TILE // bias.shape[1]), 1)
        pre = jnp.dot(w_in[...], inputs[:, lanes], preferred_element_type=jnp.float32) + shift
        half = 0.5 * pre
        hidden = (half + half * jnp.tanh(half)).astype(jnp.bfloat16)
        update = jnp.dot(w_out[...], hidden, preferred_element_type=jnp.float32)
        update = update.astype(jnp.bfloat16).astype(jnp.float32)
        here = slice(n * TILE, (n + 1) * TILE)
        state[j, :, here] = (slab[j, :, here].astype(jnp.float32) + step * update).astype(jnp.bfloat16)


def weights_kernel(w_in, bias, w_out, w_first, w_second, w_out_t, bias_t):
    channels = w_out.shape[1]
    turned = w_in[...].astype(jnp.float32).T.astype(jnp.bfloat16)
    older = (HIST - 1) * channels
    w_first[...] = turned
    w_second[:, 0:older] = turned[:, channels : HIST * channels]
    w_second[:, older : HIST * channels] = turned[:, 0:channels]
    w_second[:, HIST * channels :] = turned[:, HIST * channels :]
    w_out_t[...] = w_out[...].astype(jnp.float32).T.astype(jnp.bfloat16)
    for r in range(bias.shape[0]):
        bias_t[r * 128 : (r + 1) * 128, :] = jnp.broadcast_to(bias[r : r + 1, :], (128, 128)).T


def emit_back(plan, state, j, backs):
    grp, size = plan[1], len(backs)
    width = backs[0].shape[0]
    for k in range(size):
        backs[k][...] = state[j, channel_rows(grp, k, size, width), :]


def fill_late(plan, j, pieces, inputs, first):
    size, width = len(pieces), pieces[0].shape[1]
    channels = size * width
    for k in range(size):
        for t in range(pieces[k].shape[0]):
            rows = channel_rows(plan[1], k, size, width, (first + t) * channels)
            inputs[rows, j * SLAB : (j + 1) * SLAB] = pieces[k][t]


def first_kernel(size, plan, put, flat, w_in, bias, w_out, slab, a_in, b_in, mine, below, above, old, old_below, old_above, *refs):
    pieces, (inputs, state), backs = refs[:size], refs[size : size + 2], refs[size + 2 :]
    per_dev, channels = slab.shape[0], slab.shape[1]
    early = old.shape[1]
    for j in range(per_dev):
        lanes = slice(j * SLAB, (j + 1) * SLAB)
        inputs[0:channels, lanes] = slab[j]

        def store(source):
            for t in range(early):
                inputs[(1 + t) * channels : (2 + t) * channels, lanes] = source[t]

        settle(plan, j, old, old_below, old_above, store)
    fill_late(plan, 0, pieces, inputs, 1 + early)
    laplacian(plan, slab, a_in, b_in, mine, below, above, put, flat, inputs, HIST * channels)
    network(plan, 0, inputs, slab, w_in, bias, w_out, state)
    emit_back(plan, state, 0, backs)


def rest_kernel(size, early, plan, lay, w_in, bias, w_out, slab, ready, passed, *refs):
    pieces = refs[:size]
    inputs, state, a_out, b_out, f_out = refs[size : size + 5]
    backs = refs[size + 5 :]
    per_dev = slab.shape[0]
    for j in range(1, per_dev):
        fill_late(plan, j, pieces[(j - 1) * size : j * size], inputs, 1 + early)
    state[0] = ready[0]
    for j in range(1, per_dev):
        network(plan, j, inputs, slab, w_in, bias, w_out, state)
        emit_back(plan, state, j, backs[(j - 1) * size : j * size])
    emit_edges(plan, state, lay, a_out, b_out, f_out)


def second_kernel(size, plan, put, flat, w_in, bias, w_out, slab, a_in, b_in, mine, below, above, passed, *refs):
    backs = refs[:size]
    inputs, state = refs[size:]
    per_dev, channels = slab.shape[0], slab.shape[1]
    for j in range(per_dev):
        inputs[(HIST - 1) * channels : HIST * channels, j * SLAB : (j + 1) * SLAB] = slab[j]
    laplacian(plan, slab, a_in, b_in, mine, below, above, put, flat, inputs, HIST * channels)
    for j in range(per_dev):
        network(plan, j, inputs, slab, w_in, bias, w_out, state)
    for k in range(size):
        rows = channel_rows(plan[1], k, size, backs[k].shape[1])
        for j in range(per_dev):
            backs[k][j] = state[j, rows, :]


def finish_kernel(size, plan, *refs):
    out = refs[-1]
    for k in range(size):
        for here, there in slab_lanes(lax.rem(plan[1] + k, size), size):
            for j in range(out.shape[0]):
                out[j, 0, :, there] = refs[k][j, :, here] if len(refs[k].shape) == 3 else refs[j * size + k][:, here]


def local_folded(history, face_patch, refined, dest_slot, w_in, in_bias, w_out):
    bf16 = jnp.bfloat16
    per_dev, hist, width, cells = history.shape
    size = lax.axis_size("grp")
    channels = width * size
    hidden = w_in.shape[1]
    doms = lax.axis_size("dom")
    smem = pl.BlockSpec(memory_space=SMEM)
    anywhere = pl.BlockSpec(memory_space=pl.ANY)
    shape = jax.ShapeDtypeStruct
    place = jnp.stack([lax.axis_index("dom"), lax.axis_index("grp")]).astype(jnp.int32)
    up_ring = [(i, (i + 1) % doms) for i in range(doms)]
    down_ring = [(i, (i - 1) % doms) for i in range(doms)]

    def state_block(t):
        return pl.BlockSpec((per_dev, 1, width, cells), lambda i: (0, t, 0, 0))

    def early_pack(first, states, *after):
        return pl.pallas_call(
            functools.partial(early_pack_kernel, size, states),
            grid=(1,),
            out_shape=[shape((per_dev, states, width, SLAB), bf16)] * size,
            in_specs=[smem] + [state_block(first + t) for t in range(states)] + [anywhere] * len(after),
            out_specs=vmem_specs(size),
            compiler_params=grant(SMALL),
        )(place, *([history] * states), *after)

    early = 1
    late = hist - 1 - early
    newest = early_pack(0, 1)
    plan = pl.pallas_call(
        functools.partial(plan_kernel, per_dev),
        out_shape=shape((PLAN_SIZE,), jnp.int32),
        in_specs=[smem] * 4 + [anywhere] * size,
        out_specs=smem,
        compiler_params=grant(SMALL),
        name="plan",
    )(place, face_patch.T, refined, dest_slot, *newest)

    def movers(first, states):
        block = (1, 1, width, cells)
        return pl.pallas_call(
            send_kernel,
            grid_spec=pltpu.PrefetchScalarGridSpec(
                num_scalar_prefetch=1,
                grid=(states,),
                in_specs=[
                    pl.BlockSpec(block, lambda i, plan: (plan[2], first + i, 0, 0)),
                    pl.BlockSpec(block, lambda i, plan: (plan[3], first + i, 0, 0)),
                ],
                out_specs=[pl.BlockSpec((1, width, cells), lambda i, plan: (i, 0, 0))] * 2,
            ),
            out_shape=[shape((states, width, cells), bf16)] * 2,
            compiler_params=grant(SMALL),
        )(plan, history, history)

    def across_dom(up, down):
        return lax.ppermute(up, "dom", up_ring), lax.ppermute(down, "dom", down_ring)

    def pack(first, states, below, above, *after):
        block = (states, width, SLAB)
        return pl.pallas_call(
            functools.partial(pack_kernel, size, states),
            grid=(1,),
            out_shape=[shape(block, bf16)] * (size * per_dev),
            in_specs=[smem] + vmem_specs(2)
            + [state_block(first + t) for t in range(states)]
            + [anywhere] * len(after),
            out_specs=vmem_specs(size * per_dev),
            compiler_params=grant(SMALL),
        )(plan, below, above, *([history] * states), *after)

    def across_grp(pieces, sign):
        moved = [pieces[0]]
        for k in range(1, size):
            moved.append(lax.ppermute(pieces[k], "grp", [(i, (i + sign * k) % size) for i in range(size)]))
        return moved

    pair_a = [(i, i ^ 1) for i in range(size)]
    pair_b = [(i, i if i in (0, size - 1) else ((i + 1) ^ 1) - 1) for i in range(size)]

    def exchange(a_out, b_out, f_out):
        a_in = lax.ppermute(a_out, "grp", pair_a)
        b_in = lax.ppermute(b_out, "grp", pair_b)
        below, above = across_dom(f_out, f_out)
        return a_in, b_in, f_out, below, above

    lay, put, flat = (jnp.asarray(table, bf16) for table in face_tables())
    w_first, w_second, w_out_t, bias = pl.pallas_call(
        weights_kernel,
        out_shape=[shape((hidden, (hist + 1) * channels), bf16)] * 2
        + [shape((channels, hidden), bf16), shape((hidden, 128), jnp.float32)],
        in_specs=vmem_specs(3),
        out_specs=vmem_specs(4),
        compiler_params=grant(SMALL),
        name="weights",
    )(w_in, in_bias.reshape(-1, 128), w_out)

    slab_shape = shape((per_dev, channels, SLAB), bf16)
    edge_shapes = [
        shape((per_dev, channels, HALF), bf16),
        shape((per_dev, channels, HALF), bf16),
        shape((per_dev, channels, FACE_LANES), bf16),
    ]
    back_shape = shape((width, SLAB), bf16)

    def gather(pieces, *after):
        states = pieces[0].shape[1]
        return pl.pallas_call(
            functools.partial(gather_kernel, size),
            out_shape=[shape((per_dev, states, channels, SLAB), bf16)]
            + [shape((states, channels, SLAB), bf16)] * 2,
            in_specs=[smem] + vmem_specs(size) + [anywhere] * len(after),
            out_specs=vmem_specs(3),
            compiler_params=grant(SMALL),
        )(plan, *pieces, *after)

    newest = across_grp(newest, 1)
    up, down = movers(1 + early, late)
    below, above = across_dom(up, down)
    middle = early_pack(1, early, up)
    old0, up0, down0 = gather(newest, *middle)
    middle = across_grp(middle, 1)
    below0, above0 = across_dom(up0, down0)
    packed = pack(1 + early, late, below, above, up0)
    late0 = across_grp(packed[:size], 1)
    late1 = across_grp(packed[size:], 1)
    slab0, *edges = pl.pallas_call(
        edge_kernel,
        out_shape=[slab_shape] + edge_shapes,
        in_specs=[smem] + vmem_specs(4) + [anywhere] * len(packed),
        out_specs=vmem_specs(4),
        compiler_params=grant(SMALL),
        name="edges",
    )(plan, lay, old0, below0, above0, *packed)
    old1, up1, down1 = gather(middle, *edges)
    below1, above1 = across_dom(up1, down1)

    inputs = shape(((hist + 1) * channels, per_dev * SLAB), bf16)
    stacked, ready, *back0 = pl.pallas_call(
        functools.partial(first_kernel, size),
        out_shape=[inputs, shape((1, channels, SLAB), bf16)] + [back_shape] * size,
        in_specs=[smem] + vmem_specs(14 + size),
        out_specs=vmem_specs(2 + size),
        compiler_params=grant(LARGE),
        name="first",
    )(
        plan, put, flat, w_first, bias, w_out_t, slab0, *exchange(*edges),
        old1, below1, above1, *late0,
    )
    back0 = across_grp(back0, -1)
    stacked, slab1, *rest = pl.pallas_call(
        functools.partial(rest_kernel, size, early),
        out_shape=[inputs, slab_shape] + edge_shapes + [back_shape] * (size * (per_dev - 1)),
        in_specs=[smem] + vmem_specs(7 + size * (per_dev - 1)),
        out_specs=vmem_specs(5 + size * (per_dev - 1)),
        input_output_aliases={7: 0},
        compiler_params=grant(LARGE),
        name="rest",
    )(plan, lay, w_first, bias, w_out_t, slab0, ready, stacked, *late1)
    parts = exchange(*rest[:3])
    back1 = across_grp(rest[3:], -1)
    *back2, stacked = pl.pallas_call(
        functools.partial(second_kernel, size),
        out_shape=[shape((per_dev, width, SLAB), bf16)] * size + [inputs],
        in_specs=[smem] + vmem_specs(12),
        out_specs=vmem_specs(size + 1),
        scratch_shapes=[pltpu.VMEM((per_dev, channels, SLAB), bf16)],
        input_output_aliases={12: size},
        compiler_params=grant(LARGE),
        name="second",
    )(plan, put, flat, w_second, bias, w_out_t, slab1, *parts, stacked)

    def finish(state, pieces, *before):
        return pl.pallas_call(
            functools.partial(finish_kernel, size),
            grid=(1,),
            out_shape=shape((per_dev, 2, width, cells), bf16),
            in_specs=[smem] + vmem_specs(len(pieces)) + [anywhere] * len(before),
            out_specs=state_block(state),
            input_output_aliases={1 + len(pieces): 0} if before else {},
            compiler_params=grant(SMALL),
        )(plan, *pieces, *before)

    out = finish(0, back0 + back1)
    back2 = across_grp(back2, -1)
    return finish(1, back2, out)


def solution(mesh):
    placed = (P("dom", None, "grp", None), P(), P(), P(), P(), P(), P())
    folded = mesh.shape["grp"] == 4

    def body(*arrays):
        return (local_folded if folded else local_general)(*arrays)

    return jax.shard_map(
        body, mesh=mesh, in_specs=placed, out_specs=P("dom", None, "grp", None), check_vma=False
    )
```

```python
import functools

import jax
import jax.numpy as jnp
import numpy as np
from jax import lax
from jax.experimental import pallas as pl
from jax.experimental.pallas import tpu as pltpu
from jax.sharding import PartitionSpec as P

SIDE = 16
HIST = 4
PLANE = SIDE * SIDE


OPPOSITE = np.array([1, 0, 3, 2, 5, 4])


def padded(array, sides, width):
    for axis, dim in sides:
        size, length = (lax.axis_size(axis), array.shape[dim])
        up = [(i, (i + 1) % size) for i in range(size - 1)]
        down = [(j, i) for i, j in up]
        last = lax.slice_in_dim(array, length - width, length, axis=dim)
        first = lax.slice_in_dim(array, 0, width, axis=dim)
        before = lax.ppermute(last, axis, up)
        after = lax.ppermute(first, axis, down)
        array = jnp.concatenate([before, array, after], axis=dim)
    return array


def select_table(side_len, stride, offset):
    rows = jnp.arange(side_len)[:, None]
    cols = jnp.arange(side_len * side_len)[None, :]
    return (cols == rows * stride + offset).astype(jnp.bfloat16)


def take_face(grid_rows, table):
    return jnp.einsum("ncxq,kq->ncxk", grid_rows, table, preferred_element_type=jnp.float32).astype(
        jnp.bfloat16
    )


def place_face(face_rows, table):
    return jnp.einsum("ncxk,kq->ncxq", face_rows, table, preferred_element_type=jnp.float32)


def laplace_cells(newest, positions, usable):
    how_many, channels, cell_count = newest.shape
    plane = SIDE * SIDE
    grid_rows = newest.reshape(how_many, channels, SIDE, plane)
    y_low = select_table(SIDE, 1, 0)
    y_high = select_table(SIDE, 1, plane - SIDE)
    z_low = select_table(SIDE, SIDE, 0)
    z_high = select_table(SIDE, SIDE, SIDE - 1)
    layers = jnp.stack(
        [
            grid_rows[:, :, 0, :],
            grid_rows[:, :, -1, :],
            take_face(grid_rows, y_low).reshape(how_many, channels, plane),
            take_face(grid_rows, y_high).reshape(how_many, channels, plane),
            take_face(grid_rows, z_low).reshape(how_many, channels, plane),
            take_face(grid_rows, z_high).reshape(how_many, channels, plane),
        ],
        1,
    )
    layers = layers[:, OPPOSITE]
    beside_all = padded(layers, (("dom", 0),), how_many)
    picked = beside_all[positions, jnp.arange(6)[None, :]]
    picked = jnp.where(usable[:, :, None, None], picked, jnp.zeros_like(picked))
    field = grid_rows.astype(jnp.float32)
    picked_wide = picked.astype(jnp.float32)
    x_plus = jnp.concatenate([field[:, :, 1:, :], picked_wide[:, 1][:, :, None, :]], 2)
    x_minus = jnp.concatenate([picked_wide[:, 0][:, :, None, :], field[:, :, :-1, :]], 2)
    zero_row = jnp.zeros((how_many, channels, SIDE, SIDE), jnp.float32)
    y_plus = jnp.concatenate([field[..., SIDE:], zero_row], 3)
    y_plus = y_plus + place_face(picked[:, 3].reshape(how_many, channels, SIDE, SIDE), y_high)
    y_minus = jnp.concatenate([zero_row, field[..., :-SIDE]], 3)
    y_minus = y_minus + place_face(picked[:, 2].reshape(how_many, channels, SIDE, SIDE), y_low)
    z_index = jnp.arange(plane) % SIDE
    zero_cell = jnp.zeros((how_many, channels, SIDE, 1), jnp.float32)
    z_plus = jnp.concatenate([field[..., 1:], zero_cell], 3)
    z_plus = jnp.where(z_index == SIDE - 1, 0.0, z_plus)
    z_plus = z_plus + place_face(picked[:, 5].reshape(how_many, channels, SIDE, SIDE), z_high)
    z_minus = jnp.concatenate([zero_cell, field[..., :-1]], 3)
    z_minus = jnp.where(z_index == 0, 0.0, z_minus)
    z_minus = z_minus + place_face(picked[:, 4].reshape(how_many, channels, SIDE, SIDE), z_low)
    neighbour_sum = x_plus + x_minus + y_plus + y_minus + z_plus + z_minus
    spread = neighbour_sum - 6.0 * field
    return spread.reshape(how_many, channels, cell_count).astype(jnp.bfloat16)


def local_general(history, face_patch, refined, dest_slot, w_in, in_bias, w_out):
    per_dev = history.shape[0]
    my_index = lax.axis_index("dom")
    lowest = (my_index - 1) * per_dev
    my_slots = my_index * per_dev + jnp.arange(per_dev, dtype=jnp.int32)
    patch_ids = jnp.arange(dest_slot.shape[0], dtype=jnp.int32)
    inverse = jnp.zeros_like(dest_slot).at[dest_slot].set(patch_ids)

    def advance(inputs):
        how_many = inputs.shape[0]
        cell_count = inputs.shape[3]
        stacked = inputs.reshape(how_many, -1, cell_count)
        preact = (
            jnp.einsum("nkc,kh->nch", stacked, w_in, preferred_element_type=jnp.float32) + in_bias
        )
        hidden = jax.nn.silu(preact).astype(jnp.bfloat16)
        update = jnp.einsum(
            "nch,hk->nkc", hidden, w_out, preferred_element_type=jnp.float32
        ).astype(jnp.bfloat16)
        back = lax.all_to_all(update, "grp", split_axis=1, concat_axis=2, tiled=True)
        return (back, update, inputs[:, : HIST - 1])

    first_nb = face_patch[my_slots]
    first_pos = jnp.clip(first_nb - lowest, 0, 3 * per_dev - 1)
    first_ok = first_nb >= 0
    first_spread = laplace_cells(history[:, 0], first_pos, first_ok)
    first_in = jnp.concatenate([history, first_spread[:, None]], 1)
    first_back, _, _ = advance(
        lax.all_to_all(first_in, "grp", split_axis=3, concat_axis=2, tiled=True)
    )
    first_step = 1.0 - 0.5 * refined[my_slots].astype(jnp.float32)
    first_state = (
        history[:, 0].astype(jnp.float32)
        + first_step[:, None, None] * first_back.astype(jnp.float32)
    ).astype(jnp.bfloat16)
    carried = jnp.concatenate([first_state[:, None], history[:, : HIST - 1]], 1)
    owners = inverse[my_slots]
    second_nb = face_patch[owners]
    second_pos = jnp.clip(dest_slot[jnp.maximum(second_nb, 0)] - lowest, 0, 3 * per_dev - 1)
    second_ok = second_nb >= 0
    second_step = 1.0 - 0.5 * refined[owners].astype(jnp.float32)
    sources = inverse[my_slots]
    beside_all = padded(carried.reshape(per_dev, -1), (("dom", 0),), per_dev)
    moved_carried = jnp.take(beside_all, sources - lowest, axis=0).reshape(carried.shape)
    newest = moved_carried[:, 0]
    second_spread = laplace_cells(newest, second_pos, second_ok)
    second_in = jnp.concatenate([moved_carried, second_spread[:, None]], 1)
    second_back, _, _ = advance(
        lax.all_to_all(second_in, "grp", split_axis=3, concat_axis=2, tiled=True)
    )
    second_state = (
        newest.astype(jnp.float32) + second_step[:, None, None] * second_back.astype(jnp.float32)
    ).astype(jnp.bfloat16)
    return jnp.stack([moved_carried[:, 0], second_state], 1)


SLAB = 4 * PLANE
HALF = 2 * PLANE
FACE_LANES = 3 * PLANE
PLAN_SIZE = 64
SMALL, LARGE = 8, 16
VMEM = pltpu.VMEM
SMEM = pltpu.SMEM


def face_tables():
    lay = np.zeros((SLAB, PLANE), np.float32)
    put = np.zeros((PLANE, SLAB), np.float32)
    source = {2: lambda m: 240 + m, 3: lambda m: m, 4: lambda m: 16 * m + 15, 5: lambda m: 16 * m}
    target = {2: lambda m: m, 3: lambda m: 240 + m, 4: lambda m: 16 * m, 5: lambda m: 16 * m + 15}
    for face in (2, 3, 4, 5):
        for plane in range(4):
            for m in range(SIDE):
                lane = (face - 2) * 64 + plane * 16 + m
                lay[plane * PLANE + source[face](m), lane] = 1
                put[lane, plane * PLANE + target[face](m)] = 1
    flat = np.zeros((PLANE, PLANE), np.float32)
    for y in range(SIDE):
        for z in range(SIDE):
            flat[y * SIDE + z, y * SIDE + z] = -6
            for dy, dz in ((1, 0), (-1, 0), (0, 1), (0, -1)):
                if 0 <= y + dy < SIDE and 0 <= z + dz < SIDE:
                    flat[(y + dy) * SIDE + z + dz, y * SIDE + z] = 1
    return lay, put, flat


def grant(mebibytes):
    return pltpu.CompilerParams(vmem_limit_bytes=mebibytes * 2**20)


def vmem_specs(count):
    return [pl.BlockSpec(memory_space=VMEM)] * count


def plan_kernel(per_dev, place, face_patch, refined, dest_slot, *refs):
    plan = refs[-1]
    dom, grp = place[0], place[1]
    patches = dest_slot.shape[0]
    plan[0] = dom
    plan[1] = grp
    up, down = jnp.int32(0), jnp.int32(0)
    for s in range(per_dev):
        new_dom = dest_slot[dom * per_dev + s] // per_dev
        up = jnp.where(new_dom == dom + 1, s, up)
        down = jnp.where(new_dom == dom - 1, s, down)
    plan[2] = up
    plan[3] = down
    for j in range(per_dev):
        code, patch = jnp.int32(0), jnp.int32(0)
        for o in (-1, 0, 1):
            for s in range(per_dev):
                p = (dom + o) * per_dev + s
                ok = (p >= 0) & (p < patches)
                p = jnp.clip(p, 0, patches - 1)
                ok = ok & (dest_slot[p] == dom * per_dev + j)
                code = jnp.where(ok, s if o == 0 else per_dev + (o + 1) // 2, code)
                patch = jnp.where(ok, p, patch)
        plan[4 + j] = code
        plan[6 + j] = refined[patch]
        for f in range(6):
            beside = face_patch[f, patch]
            slot = dest_slot[jnp.maximum(beside, 0)]
            plan[8 + 6 * j + f] = jnp.where(beside < 0, -1, slot - (dom - 1) * per_dev)


def slab_lanes(slab, size):
    low = pl.multiple_of(slab * HALF, HALF)
    high = pl.multiple_of((2 * size - 1 - slab) * HALF, HALF)
    return ((slice(0, HALF), pl.ds(low, HALF)), (slice(HALF, SLAB), pl.ds(high, HALF)))


def channel_rows(grp, k, size, width, first=0):
    row = lax.rem(grp - k + size, size) * width
    return pl.ds(pl.multiple_of(first + row, width), width)


def settle(plan, j, own, below, above, store):
    per_dev = own.shape[0]
    code = plan[4 + j]

    @pl.when(code < per_dev)
    def _():
        store(own.at[jnp.minimum(code, per_dev - 1)])

    @pl.when(code == per_dev)
    def _():
        store(below)

    @pl.when(code == per_dev + 1)
    def _():
        store(above)


def send_kernel(plan, up_in, down_in, up_out, down_out):
    up_out[...] = up_in[0]
    down_out[...] = down_in[0]


def early_pack_kernel(size, states, place, *refs):
    for k in range(1, size + 1):
        k = k % size
        out = refs[k - size]
        for here, there in slab_lanes(lax.rem(place[1] + k, size), size):
            for t in range(states):
                for j in range(out.shape[0]):
                    out[j, t, :, here] = refs[t][j, 0, :, there]


def pack_kernel(size, states, plan, below, above, *refs):
    per_dev = refs[0].shape[0]
    outs = refs[-size * per_dev :]
    for j in range(per_dev):
        for t in range(states):

            def store(source):
                for k in range(1, size + 1):
                    k = k % size
                    for here, there in slab_lanes(lax.rem(plan[1] + k, size), size):
                        outs[j * size + k][t, :, here] = source[0, :, there]

            settle(plan, j, refs[t], below.at[pl.ds(t, 1)], above.at[pl.ds(t, 1)], store)


def emit_edges(plan, slab, lay, a_out, b_out, f_out):
    even = lax.rem(plan[1], 2) == 0
    for j in range(slab.shape[0]):
        @pl.when(even)
        def _():
            a_out[j] = slab[j, :, PLANE : 3 * PLANE]
            b_out[j, :, 0:PLANE] = slab[j, :, 0:PLANE]
            b_out[j, :, PLANE:HALF] = slab[j, :, 3 * PLANE : SLAB]

        @pl.when(jnp.logical_not(even))
        def _():
            b_out[j] = slab[j, :, PLANE : 3 * PLANE]
            a_out[j, :, 0:PLANE] = slab[j, :, 0:PLANE]
            a_out[j, :, PLANE:HALF] = slab[j, :, 3 * PLANE : SLAB]

        f_out[j, :, 0:PLANE] = jnp.dot(
            slab[j], lay[...], preferred_element_type=jnp.float32
        ).astype(jnp.bfloat16)
        f_out[j, :, PLANE:HALF] = slab[j, :, 0:PLANE]
        f_out[j, :, HALF:FACE_LANES] = slab[j, :, 3 * PLANE : SLAB]


def gather_kernel(size, plan, *refs):
    pieces, (slab, up, down) = refs[:size], refs[-3:]
    per_dev, states, width = pieces[0].shape[:3]
    for k in range(size):
        rows = channel_rows(plan[1], k, size, width)
        for t in range(states):
            up[t, rows] = pieces[k][plan[2], t]
            down[t, rows] = pieces[k][plan[3], t]
            for j in range(per_dev):
                slab[j, t, rows] = pieces[k][j, t]


def edge_kernel(plan, lay, old, below, above, *refs):
    slab, a_out, b_out, f_out = refs[-4:]
    for j in range(slab.shape[0]):

        def store(source):
            slab[j] = source[0]

        settle(plan, j, old, below, above, store)
    emit_edges(plan, slab, lay, a_out, b_out, f_out)


def laplacian(plan, slab, a_in, b_in, mine, below, above, put, flat, spread, first_row):
    f32, bf16 = jnp.float32, jnp.bfloat16
    grp = plan[1]
    per_dev, channels = slab.shape[0], slab.shape[1]
    odd = lax.rem(grp, 2)
    lowest, highest = (grp == 0).astype(jnp.int32), (grp == 3).astype(jnp.int32)

    def weight(chosen):
        return jnp.full((16, PLANE), chosen, jnp.int32).astype(f32).astype(bf16)

    def scaled(value, chosen):
        rows = value.shape[0]
        return (value.reshape(rows // 16, 16, PLANE) * chosen[None]).reshape(rows, PLANE)

    inner_a, inner_b, inner_own = weight(1 - odd), weight(odd - highest), weight(highest)
    outer_a, outer_b = weight(odd), weight(1 - odd - lowest)
    cands = [ref.at[s] for ref in (below, mine, above) for s in range(per_dev)]
    face_of_lane = lax.broadcasted_iota(jnp.int32, (16, PLANE), 1) // 64
    low, high = slice(0, PLANE), slice(PLANE, HALF)
    for j in range(per_dev):
        layer = [slab[j, :, i * PLANE : (i + 1) * PLANE] for i in range(4)]
        a, b = a_in[j], b_in[j]
        inner0 = scaled(a[:, low], inner_a) + scaled(b[:, low], inner_b) + scaled(layer[2], inner_own)
        inner1 = scaled(a[:, high], inner_a) + scaled(b[:, high], inner_b) + scaled(layer[1], inner_own)
        outer0 = scaled(a[:, low], outer_a) + scaled(b[:, low], outer_b)
        outer1 = scaled(a[:, high], outer_a) + scaled(b[:, high], outer_b)
        code = [plan[8 + 6 * j + f] for f in range(6)]
        lane_code = jnp.where(
            face_of_lane < 2,
            jnp.where(face_of_lane == 0, code[2], code[3]),
            jnp.where(face_of_lane == 2, code[4], code[5]),
        )
        rest = jnp.zeros((channels, PLANE), bf16)
        for c, cand in enumerate(cands):
            outer0 = outer0 + scaled(cand[:, HALF:FACE_LANES], weight(jnp.where(code[0] == c, lowest, 0)))
            outer1 = outer1 + scaled(cand[:, PLANE:HALF], weight(jnp.where(code[1] == c, lowest, 0)))
            rest = rest + scaled(cand[:, low], jnp.where(lane_code == c, 1.0, 0.0).astype(bf16))
        placed = jnp.dot(rest, put[...], preferred_element_type=f32)
        sides = ((outer0, layer[1]), (layer[0], inner0), (inner1, layer[3]), (layer[2], outer1))
        for i in range(4):
            total = jnp.dot(layer[i], flat[...], preferred_element_type=f32)
            total = total + placed[:, i * PLANE : (i + 1) * PLANE]
            total = total + sides[i][0].astype(f32) + sides[i][1].astype(f32)
            spread[first_row : first_row + channels, j * SLAB + i * PLANE : j * SLAB + (i + 1) * PLANE] = (
                total.astype(bf16)
            )


TILE = 1024


def network(plan, j, inputs, slab, w_in, bias, w_out, state):
    step = 1.0 - 0.5 * plan[6 + j].astype(jnp.float32)
    for n in range(SLAB // TILE):
        lanes = slice(j * SLAB + n * TILE, j * SLAB + (n + 1) * TILE)
        shift = jnp.concatenate([bias[...]] * (TILE // bias.shape[1]), 1)
        pre = jnp.dot(w_in[...], inputs[:, lanes], preferred_element_type=jnp.float32) + shift
        half = 0.5 * pre
        hidden = (half + half * jnp.tanh(half)).astype(jnp.bfloat16)
        update = jnp.dot(w_out[...], hidden, preferred_element_type=jnp.float32)
        update = update.astype(jnp.bfloat16).astype(jnp.float32)
        here = slice(n * TILE, (n + 1) * TILE)
        state[j, :, here] = (slab[j, :, here].astype(jnp.float32) + step * update).astype(jnp.bfloat16)


def weights_kernel(w_in, bias, w_out, w_first, w_second, w_out_t, bias_t):
    channels = w_out.shape[1]
    turned = w_in[...].astype(jnp.float32).T.astype(jnp.bfloat16)
    older = (HIST - 1) * channels
    w_first[...] = turned
    w_second[:, 0:older] = turned[:, channels : HIST * channels]
    w_second[:, older : HIST * channels] = turned[:, 0:channels]
    w_second[:, HIST * channels :] = turned[:, HIST * channels :]
    w_out_t[...] = w_out[...].astype(jnp.float32).T.astype(jnp.bfloat16)
    for r in range(bias.shape[0]):
        bias_t[r * 128 : (r + 1) * 128, :] = jnp.broadcast_to(bias[r : r + 1, :], (128, 128)).T


def emit_back(plan, state, j, backs):
    grp, size = plan[1], len(backs)
    width = backs[0].shape[0]
    for k in range(size):
        backs[k][...] = state[j, channel_rows(grp, k, size, width), :]


def fill_late(plan, j, pieces, inputs, first):
    size, width = len(pieces), pieces[0].shape[1]
    channels = size * width
    for k in range(size):
        for t in range(pieces[k].shape[0]):
            rows = channel_rows(plan[1], k, size, width, (first + t) * channels)
            inputs[rows, j * SLAB : (j + 1) * SLAB] = pieces[k][t]


def first_kernel(size, plan, put, flat, w_in, bias, w_out, slab, a_in, b_in, mine, below, above, old, old_below, old_above, *refs):
    pieces, (inputs, state), backs = refs[:size], refs[size : size + 2], refs[size + 2 :]
    per_dev, channels = slab.shape[0], slab.shape[1]
    early = old.shape[1]
    for j in range(per_dev):
        lanes = slice(j * SLAB, (j + 1) * SLAB)
        inputs[0:channels, lanes] = slab[j]

        def store(source):
            for t in range(early):
                inputs[(1 + t) * channels : (2 + t) * channels, lanes] = source[t]

        settle(plan, j, old, old_below, old_above, store)
    fill_late(plan, 0, pieces, inputs, 1 + early)
    laplacian(plan, slab, a_in, b_in, mine, below, above, put, flat, inputs, HIST * channels)
    network(plan, 0, inputs, slab, w_in, bias, w_out, state)
    emit_back(plan, state, 0, backs)


def rest_kernel(size, early, plan, lay, w_in, bias, w_out, slab, ready, passed, *refs):
    pieces = refs[:size]
    inputs, state, a_out, b_out, f_out = refs[size : size + 5]
    backs = refs[size + 5 :]
    per_dev = slab.shape[0]
    for j in range(1, per_dev):
        fill_late(plan, j, pieces[(j - 1) * size : j * size], inputs, 1 + early)
    state[0] = ready[0]
    for j in range(1, per_dev):
        network(plan, j, inputs, slab, w_in, bias, w_out, state)
        emit_back(plan, state, j, backs[(j - 1) * size : j * size])
    emit_edges(plan, state, lay, a_out, b_out, f_out)


def second_kernel(size, plan, put, flat, w_in, bias, w_out, slab, a_in, b_in, mine, below, above, passed, *refs):
    backs = refs[:size]
    inputs, state = refs[size:]
    per_dev, channels = slab.shape[0], slab.shape[1]
    for j in range(per_dev):
        inputs[(HIST - 1) * channels : HIST * channels, j * SLAB : (j + 1) * SLAB] = slab[j]
    laplacian(plan, slab, a_in, b_in, mine, below, above, put, flat, inputs, HIST * channels)
    for j in range(per_dev):
        network(plan, j, inputs, slab, w_in, bias, w_out, state)
    for k in range(size):
        rows = channel_rows(plan[1], k, size, backs[k].shape[1])
        for j in range(per_dev):
            backs[k][j] = state[j, rows, :]


def finish_kernel(size, plan, *refs):
    out = refs[-1]
    for k in range(size):
        for here, there in slab_lanes(lax.rem(plan[1] + k, size), size):
            for j in range(out.shape[0]):
                out[j, 0, :, there] = refs[k][j, :, here] if len(refs[k].shape) == 3 else refs[j * size + k][:, here]


def local_folded(history, face_patch, refined, dest_slot, w_in, in_bias, w_out):
    bf16 = jnp.bfloat16
    per_dev, hist, width, cells = history.shape
    size = lax.axis_size("grp")
    channels = width * size
    hidden = w_in.shape[1]
    doms = lax.axis_size("dom")
    smem = pl.BlockSpec(memory_space=SMEM)
    anywhere = pl.BlockSpec(memory_space=pl.ANY)
    shape = jax.ShapeDtypeStruct
    place = jnp.stack([lax.axis_index("dom"), lax.axis_index("grp")]).astype(jnp.int32)
    up_ring = [(i, (i + 1) % doms) for i in range(doms)]
    down_ring = [(i, (i - 1) % doms) for i in range(doms)]

    def state_block(t):
        return pl.BlockSpec((per_dev, 1, width, cells), lambda i: (0, t, 0, 0))

    def early_pack(first, states, *after):
        return pl.pallas_call(
            functools.partial(early_pack_kernel, size, states),
            grid=(1,),
            out_shape=[shape((per_dev, states, width, SLAB), bf16)] * size,
            in_specs=[smem] + [state_block(first + t) for t in range(states)] + [anywhere] * len(after),
            out_specs=vmem_specs(size),
            compiler_params=grant(SMALL),
        )(place, *([history] * states), *after)

    early = 1
    late = hist - 1 - early
    newest = early_pack(0, 1)
    plan = pl.pallas_call(
        functools.partial(plan_kernel, per_dev),
        out_shape=shape((PLAN_SIZE,), jnp.int32),
        in_specs=[smem] * 4 + [anywhere] * size,
        out_specs=smem,
        compiler_params=grant(SMALL),
        name="plan",
    )(place, face_patch.T, refined, dest_slot, *newest)

    def movers(first, states):
        block = (1, 1, width, cells)
        return pl.pallas_call(
            send_kernel,
            grid_spec=pltpu.PrefetchScalarGridSpec(
                num_scalar_prefetch=1,
                grid=(states,),
                in_specs=[
                    pl.BlockSpec(block, lambda i, plan: (plan[2], first + i, 0, 0)),
                    pl.BlockSpec(block, lambda i, plan: (plan[3], first + i, 0, 0)),
                ],
                out_specs=[pl.BlockSpec((1, width, cells), lambda i, plan: (i, 0, 0))] * 2,
            ),
            out_shape=[shape((states, width, cells), bf16)] * 2,
            compiler_params=grant(SMALL),
        )(plan, history, history)

    def across_dom(up, down):
        return lax.ppermute(up, "dom", up_ring), lax.ppermute(down, "dom", down_ring)

    def pack(first, states, below, above, *after):
        block = (states, width, SLAB)
        return pl.pallas_call(
            functools.partial(pack_kernel, size, states),
            grid=(1,),
            out_shape=[shape(block, bf16)] * (size * per_dev),
            in_specs=[smem] + vmem_specs(2)
            + [state_block(first + t) for t in range(states)]
            + [anywhere] * len(after),
            out_specs=vmem_specs(size * per_dev),
            compiler_params=grant(SMALL),
        )(plan, below, above, *([history] * states), *after)

    def across_grp(pieces, sign):
        moved = [pieces[0]]
        for k in range(1, size):
            moved.append(lax.ppermute(pieces[k], "grp", [(i, (i + sign * k) % size) for i in range(size)]))
        return moved

    pair_a = [(i, i ^ 1) for i in range(size)]
    pair_b = []
    for d in range(doms):
        for i in range(size):
            target = (d ^ 1, i) if i in (0, size - 1) else (d, ((i + 1) ^ 1) - 1)
            pair_b.append((d * size + i, target[0] * size + target[1]))

    def exchange(a_out, b_out, f_out):
        b_in = lax.ppermute(b_out, ("dom", "grp"), pair_b)
        a_in = lax.ppermute(a_out, "grp", pair_a)
        below, above = across_dom(f_out, f_out)
        return a_in, b_in, f_out, below, above

    lay, put, flat = (jnp.asarray(table, bf16) for table in face_tables())
    w_first, w_second, w_out_t, bias = pl.pallas_call(
        weights_kernel,
        out_shape=[shape((hidden, (hist + 1) * channels), bf16)] * 2
        + [shape((channels, hidden), bf16), shape((hidden, 128), jnp.float32)],
        in_specs=vmem_specs(3),
        out_specs=vmem_specs(4),
        compiler_params=grant(SMALL),
        name="weights",
    )(w_in, in_bias.reshape(-1, 128), w_out)

    slab_shape = shape((per_dev, channels, SLAB), bf16)
    edge_shapes = [
        shape((per_dev, channels, HALF), bf16),
        shape((per_dev, channels, HALF), bf16),
        shape((per_dev, channels, FACE_LANES), bf16),
    ]
    back_shape = shape((width, SLAB), bf16)

    def gather(pieces, *after):
        states = pieces[0].shape[1]
        return pl.pallas_call(
            functools.partial(gather_kernel, size),
            out_shape=[shape((per_dev, states, channels, SLAB), bf16)]
            + [shape((states, channels, SLAB), bf16)] * 2,
            in_specs=[smem] + vmem_specs(size) + [anywhere] * len(after),
            out_specs=vmem_specs(3),
            compiler_params=grant(SMALL),
        )(plan, *pieces, *after)

    newest = across_grp(newest, 1)
    up, down = movers(1 + early, late)
    below, above = across_dom(up, down)
    middle = early_pack(1, early, up)
    old0, up0, down0 = gather(newest, *middle)
    middle = across_grp(middle, 1)
    below0, above0 = across_dom(up0, down0)
    packed = pack(1 + early, late, below, above, up0)
    late0 = across_grp(packed[:size], 1)
    late1 = across_grp(packed[size:], 1)
    slab0, *edges = pl.pallas_call(
        edge_kernel,
        out_shape=[slab_shape] + edge_shapes,
        in_specs=[smem] + vmem_specs(4) + [anywhere] * len(packed),
        out_specs=vmem_specs(4),
        compiler_params=grant(SMALL),
        name="edges",
    )(plan, lay, old0, below0, above0, *packed)
    old1, up1, down1 = gather(middle, *edges)
    below1, above1 = across_dom(up1, down1)

    inputs = shape(((hist + 1) * channels, per_dev * SLAB), bf16)
    stacked, ready, *back0 = pl.pallas_call(
        functools.partial(first_kernel, size),
        out_shape=[inputs, shape((1, channels, SLAB), bf16)] + [back_shape] * size,
        in_specs=[smem] + vmem_specs(14 + size),
        out_specs=vmem_specs(2 + size),
        compiler_params=grant(LARGE),
        name="first",
    )(
        plan, put, flat, w_first, bias, w_out_t, slab0, *exchange(*edges),
        old1, below1, above1, *late0,
    )
    back0 = across_grp(back0, -1)
    stacked, slab1, *rest = pl.pallas_call(
        functools.partial(rest_kernel, size, early),
        out_shape=[inputs, slab_shape] + edge_shapes + [back_shape] * (size * (per_dev - 1)),
        in_specs=[smem] + vmem_specs(7 + size * (per_dev - 1)),
        out_specs=vmem_specs(5 + size * (per_dev - 1)),
        input_output_aliases={7: 0},
        compiler_params=grant(LARGE),
        name="rest",
    )(plan, lay, w_first, bias, w_out_t, slab0, ready, stacked, *late1)
    parts = exchange(*rest[:3])
    back1 = across_grp(rest[3:], -1)
    *back2, stacked = pl.pallas_call(
        functools.partial(second_kernel, size),
        out_shape=[shape((per_dev, width, SLAB), bf16)] * size + [inputs],
        in_specs=[smem] + vmem_specs(12),
        out_specs=vmem_specs(size + 1),
        scratch_shapes=[pltpu.VMEM((per_dev, channels, SLAB), bf16)],
        input_output_aliases={12: size},
        compiler_params=grant(LARGE),
        name="second",
    )(plan, put, flat, w_second, bias, w_out_t, slab1, *parts, stacked)

    def finish(state, pieces, *before):
        return pl.pallas_call(
            functools.partial(finish_kernel, size),
            grid=(1,),
            out_shape=shape((per_dev, 2, width, cells), bf16),
            in_specs=[smem] + vmem_specs(len(pieces)) + [anywhere] * len(before),
            out_specs=state_block(state),
            input_output_aliases={1 + len(pieces): 0} if before else {},
            compiler_params=grant(SMALL),
        )(plan, *pieces, *before)

    out = finish(0, back0 + back1)
    back2 = across_grp(back2, -1)
    return finish(1, back2, out)


def solution(mesh):
    placed = (P("dom", None, "grp", None), P(), P(), P(), P(), P(), P())
    folded = mesh.shape["grp"] == 4 and mesh.shape["dom"] % 2 == 0

    def body(*arrays):
        return (local_folded if folded else local_general)(*arrays)

    return jax.shard_map(
        body, mesh=mesh, in_specs=placed, out_specs=P("dom", None, "grp", None), check_vma=False
    )
```

```python
import functools

import jax
import jax.numpy as jnp
import numpy as np
from jax import lax
from jax.experimental import pallas as pl
from jax.experimental.pallas import tpu as pltpu
from jax.sharding import PartitionSpec as P

SIDE = 16
HIST = 4
PLANE = SIDE * SIDE


OPPOSITE = np.array([1, 0, 3, 2, 5, 4])


def padded(array, sides, width):
    for axis, dim in sides:
        size, length = (lax.axis_size(axis), array.shape[dim])
        up = [(i, (i + 1) % size) for i in range(size - 1)]
        down = [(j, i) for i, j in up]
        last = lax.slice_in_dim(array, length - width, length, axis=dim)
        first = lax.slice_in_dim(array, 0, width, axis=dim)
        before = lax.ppermute(last, axis, up)
        after = lax.ppermute(first, axis, down)
        array = jnp.concatenate([before, array, after], axis=dim)
    return array


def select_table(side_len, stride, offset):
    rows = jnp.arange(side_len)[:, None]
    cols = jnp.arange(side_len * side_len)[None, :]
    return (cols == rows * stride + offset).astype(jnp.bfloat16)


def take_face(grid_rows, table):
    return jnp.einsum("ncxq,kq->ncxk", grid_rows, table, preferred_element_type=jnp.float32).astype(
        jnp.bfloat16
    )


def place_face(face_rows, table):
    return jnp.einsum("ncxk,kq->ncxq", face_rows, table, preferred_element_type=jnp.float32)


def laplace_cells(newest, positions, usable):
    how_many, channels, cell_count = newest.shape
    plane = SIDE * SIDE
    grid_rows = newest.reshape(how_many, channels, SIDE, plane)
    y_low = select_table(SIDE, 1, 0)
    y_high = select_table(SIDE, 1, plane - SIDE)
    z_low = select_table(SIDE, SIDE, 0)
    z_high = select_table(SIDE, SIDE, SIDE - 1)
    layers = jnp.stack(
        [
            grid_rows[:, :, 0, :],
            grid_rows[:, :, -1, :],
            take_face(grid_rows, y_low).reshape(how_many, channels, plane),
            take_face(grid_rows, y_high).reshape(how_many, channels, plane),
            take_face(grid_rows, z_low).reshape(how_many, channels, plane),
            take_face(grid_rows, z_high).reshape(how_many, channels, plane),
        ],
        1,
    )
    layers = layers[:, OPPOSITE]
    beside_all = padded(layers, (("dom", 0),), how_many)
    picked = beside_all[positions, jnp.arange(6)[None, :]]
    picked = jnp.where(usable[:, :, None, None], picked, jnp.zeros_like(picked))
    field = grid_rows.astype(jnp.float32)
    picked_wide = picked.astype(jnp.float32)
    x_plus = jnp.concatenate([field[:, :, 1:, :], picked_wide[:, 1][:, :, None, :]], 2)
    x_minus = jnp.concatenate([picked_wide[:, 0][:, :, None, :], field[:, :, :-1, :]], 2)
    zero_row = jnp.zeros((how_many, channels, SIDE, SIDE), jnp.float32)
    y_plus = jnp.concatenate([field[..., SIDE:], zero_row], 3)
    y_plus = y_plus + place_face(picked[:, 3].reshape(how_many, channels, SIDE, SIDE), y_high)
    y_minus = jnp.concatenate([zero_row, field[..., :-SIDE]], 3)
    y_minus = y_minus + place_face(picked[:, 2].reshape(how_many, channels, SIDE, SIDE), y_low)
    z_index = jnp.arange(plane) % SIDE
    zero_cell = jnp.zeros((how_many, channels, SIDE, 1), jnp.float32)
    z_plus = jnp.concatenate([field[..., 1:], zero_cell], 3)
    z_plus = jnp.where(z_index == SIDE - 1, 0.0, z_plus)
    z_plus = z_plus + place_face(picked[:, 5].reshape(how_many, channels, SIDE, SIDE), z_high)
    z_minus = jnp.concatenate([zero_cell, field[..., :-1]], 3)
    z_minus = jnp.where(z_index == 0, 0.0, z_minus)
    z_minus = z_minus + place_face(picked[:, 4].reshape(how_many, channels, SIDE, SIDE), z_low)
    neighbour_sum = x_plus + x_minus + y_plus + y_minus + z_plus + z_minus
    spread = neighbour_sum - 6.0 * field
    return spread.reshape(how_many, channels, cell_count).astype(jnp.bfloat16)


def local_general(history, face_patch, refined, dest_slot, w_in, in_bias, w_out):
    per_dev = history.shape[0]
    my_index = lax.axis_index("dom")
    lowest = (my_index - 1) * per_dev
    my_slots = my_index * per_dev + jnp.arange(per_dev, dtype=jnp.int32)
    patch_ids = jnp.arange(dest_slot.shape[0], dtype=jnp.int32)
    inverse = jnp.zeros_like(dest_slot).at[dest_slot].set(patch_ids)

    def advance(inputs):
        how_many = inputs.shape[0]
        cell_count = inputs.shape[3]
        stacked = inputs.reshape(how_many, -1, cell_count)
        preact = (
            jnp.einsum("nkc,kh->nch", stacked, w_in, preferred_element_type=jnp.float32) + in_bias
        )
        hidden = jax.nn.silu(preact).astype(jnp.bfloat16)
        update = jnp.einsum(
            "nch,hk->nkc", hidden, w_out, preferred_element_type=jnp.float32
        ).astype(jnp.bfloat16)
        back = lax.all_to_all(update, "grp", split_axis=1, concat_axis=2, tiled=True)
        return (back, update, inputs[:, : HIST - 1])

    first_nb = face_patch[my_slots]
    first_pos = jnp.clip(first_nb - lowest, 0, 3 * per_dev - 1)
    first_ok = first_nb >= 0
    first_spread = laplace_cells(history[:, 0], first_pos, first_ok)
    first_in = jnp.concatenate([history, first_spread[:, None]], 1)
    first_back, _, _ = advance(lax.all_to_all(first_in, "grp", split_axis=3, concat_axis=2, tiled=True))
    first_step = 1.0 - 0.5 * refined[my_slots].astype(jnp.float32)
    first_state = (
        history[:, 0].astype(jnp.float32)
        + first_step[:, None, None] * first_back.astype(jnp.float32)
    ).astype(jnp.bfloat16)
    carried = jnp.concatenate([first_state[:, None], history[:, : HIST - 1]], 1)
    owners = inverse[my_slots]
    second_nb = face_patch[owners]
    second_pos = jnp.clip(dest_slot[jnp.maximum(second_nb, 0)] - lowest, 0, 3 * per_dev - 1)
    second_ok = second_nb >= 0
    second_step = 1.0 - 0.5 * refined[owners].astype(jnp.float32)
    sources = inverse[my_slots]
    beside_all = padded(carried.reshape(per_dev, -1), (("dom", 0),), per_dev)
    moved_carried = jnp.take(beside_all, sources - lowest, axis=0).reshape(carried.shape)
    newest = moved_carried[:, 0]
    second_spread = laplace_cells(newest, second_pos, second_ok)
    second_in = jnp.concatenate([moved_carried, second_spread[:, None]], 1)
    second_back, _, _ = advance(lax.all_to_all(second_in, "grp", split_axis=3, concat_axis=2, tiled=True))
    second_state = (
        newest.astype(jnp.float32) + second_step[:, None, None] * second_back.astype(jnp.float32)
    ).astype(jnp.bfloat16)
    return jnp.stack([moved_carried[:, 0], second_state], 1)


SLAB = 4 * PLANE
HALF = 2 * PLANE
FACE_LANES = 3 * PLANE
PLAN_SIZE = 64
SMALL, LARGE = 8, 16
VMEM = pltpu.VMEM
SMEM = pltpu.SMEM


def face_tables():
    lay = np.zeros((SLAB, PLANE), np.float32)
    put = np.zeros((PLANE, SLAB), np.float32)
    source = {2: lambda m: 240 + m, 3: lambda m: m, 4: lambda m: 16 * m + 15, 5: lambda m: 16 * m}
    target = {2: lambda m: m, 3: lambda m: 240 + m, 4: lambda m: 16 * m, 5: lambda m: 16 * m + 15}
    for face in (2, 3, 4, 5):
        for plane in range(4):
            for m in range(SIDE):
                lane = (face - 2) * 64 + plane * 16 + m
                lay[plane * PLANE + source[face](m), lane] = 1
                put[lane, plane * PLANE + target[face](m)] = 1
    flat = np.zeros((PLANE, PLANE), np.float32)
    for y in range(SIDE):
        for z in range(SIDE):
            flat[y * SIDE + z, y * SIDE + z] = -6
            for dy, dz in ((1, 0), (-1, 0), (0, 1), (0, -1)):
                if 0 <= y + dy < SIDE and 0 <= z + dz < SIDE:
                    flat[(y + dy) * SIDE + z + dz, y * SIDE + z] = 1
    return lay, put, flat


def grant(mebibytes):
    return pltpu.CompilerParams(vmem_limit_bytes=mebibytes * 2**20)


def vmem_specs(count):
    return [pl.BlockSpec(memory_space=VMEM)] * count


def plan_kernel(per_dev, face_patch, refined, dest_slot, *refs):
    plan = refs[-1]
    dom, grp = lax.axis_index("dom"), lax.axis_index("grp")
    patches = dest_slot.shape[0]
    plan[0] = dom
    plan[1] = grp
    up, down = jnp.int32(0), jnp.int32(0)
    for s in range(per_dev):
        new_dom = dest_slot[dom * per_dev + s] // per_dev
        up = jnp.where(new_dom == dom + 1, s, up)
        down = jnp.where(new_dom == dom - 1, s, down)
    plan[2] = up
    plan[3] = down
    for j in range(per_dev):
        code, patch = jnp.int32(0), jnp.int32(0)
        for o in (-1, 0, 1):
            for s in range(per_dev):
                p = (dom + o) * per_dev + s
                ok = (p >= 0) & (p < patches)
                p = jnp.clip(p, 0, patches - 1)
                ok = ok & (dest_slot[p] == dom * per_dev + j)
                code = jnp.where(ok, s if o == 0 else per_dev + (o + 1) // 2, code)
                patch = jnp.where(ok, p, patch)
        plan[4 + j] = code
        plan[6 + j] = refined[patch]
        for f in range(6):
            beside = face_patch[f, patch]
            slot = dest_slot[jnp.maximum(beside, 0)]
            plan[8 + 6 * j + f] = jnp.where(beside < 0, -1, slot - (dom - 1) * per_dev)


def slab_lanes(slab, size):
    low = pl.multiple_of(slab * HALF, HALF)
    high = pl.multiple_of((2 * size - 1 - slab) * HALF, HALF)
    return ((slice(0, HALF), pl.ds(low, HALF)), (slice(HALF, SLAB), pl.ds(high, HALF)))


def channel_rows(grp, k, size, width, first=0):
    row = lax.rem(grp - k + size, size) * width
    return pl.ds(pl.multiple_of(first + row, width), width)


def settle(plan, j, own, below, above, store):
    per_dev = own.shape[0]
    code = plan[4 + j]

    @pl.when(code < per_dev)
    def _():
        store(own.at[jnp.minimum(code, per_dev - 1)])

    @pl.when(code == per_dev)
    def _():
        store(below)

    @pl.when(code == per_dev + 1)
    def _():
        store(above)


def send_kernel(first, plan, history, up_out, down_out):
    last = first + up_out.shape[0]
    up_out[...] = history[plan[2], first:last]
    down_out[...] = history[plan[3], first:last]


def early_pack_kernel(size, first, states, *refs):
    grp = lax.axis_index("grp")
    for k in range(1, size + 1):
        k = k % size
        out = refs[k - size]
        for here, there in slab_lanes(lax.rem(grp + k, size), size):
            for t in range(states):
                for j in range(out.shape[0]):
                    out[j, t, :, here] = refs[0][j, first + t, :, there]


def pack_kernel(size, first, plan, history, below, above, *refs):
    per_dev = history.shape[0]
    outs = refs[-size * per_dev :]
    for j in range(per_dev):
        for t in range(below.shape[0]):

            def store(row, source):
                for k in range(1, size + 1):
                    k = k % size
                    for here, there in slab_lanes(lax.rem(plan[1] + k, size), size):
                        outs[j * size + k][t, :, here] = source[row, :, there]

            settle(
                plan, j, history, below, above,
                lambda source: store(first + t if source.shape[0] == history.shape[1] else t, source),
            )


def emit_edges(plan, patches, slab, lay, a_out, b_out, f_out):
    even = lax.rem(plan[1], 2) == 0
    for j in patches:
        @pl.when(even)
        def _():
            a_out[j] = slab[j, :, PLANE : 3 * PLANE]
            b_out[j, :, 0:PLANE] = slab[j, :, 0:PLANE]
            b_out[j, :, PLANE:HALF] = slab[j, :, 3 * PLANE : SLAB]

        @pl.when(jnp.logical_not(even))
        def _():
            b_out[j] = slab[j, :, PLANE : 3 * PLANE]
            a_out[j, :, 0:PLANE] = slab[j, :, 0:PLANE]
            a_out[j, :, PLANE:HALF] = slab[j, :, 3 * PLANE : SLAB]

        f_out[j, :, 0:PLANE] = jnp.dot(
            slab[j], lay[...], preferred_element_type=jnp.float32
        ).astype(jnp.bfloat16)
        f_out[j, :, PLANE:HALF] = slab[j, :, 0:PLANE]
        f_out[j, :, HALF:FACE_LANES] = slab[j, :, 3 * PLANE : SLAB]


def gather_kernel(size, plan, *refs):
    pieces, (slab, up, down) = refs[:size], refs[-3:]
    per_dev, states, width = pieces[0].shape[:3]
    for k in range(size):
        rows = channel_rows(plan[1], k, size, width)
        for t in range(states):
            up[t, rows] = pieces[k][plan[2], t]
            down[t, rows] = pieces[k][plan[3], t]
            for j in range(per_dev):
                slab[j, t, rows] = pieces[k][j, t]


def edge_kernel(plan, lay, old, below, above, *refs):
    slab, a_out, b_out, f_out = refs[-4:]
    for j in range(slab.shape[0]):

        def store(source):
            slab[j] = source[0]

        settle(plan, j, old, below, above, store)
    emit_edges(plan, range(slab.shape[0]), slab, lay, a_out, b_out, f_out)


def laplacian(plan, slab, a_in, b_in, mine, below, above, put, flat, spread, first_row):
    f32, bf16 = jnp.float32, jnp.bfloat16
    grp = plan[1]
    per_dev, channels = slab.shape[0], slab.shape[1]
    odd = lax.rem(grp, 2)
    lowest, highest = (grp == 0).astype(jnp.int32), (grp == 3).astype(jnp.int32)

    def weight(chosen):
        return jnp.full((16, PLANE), chosen, jnp.int32).astype(f32).astype(bf16)

    def scaled(value, chosen):
        rows = value.shape[0]
        return (value.reshape(rows // 16, 16, PLANE) * chosen[None]).reshape(rows, PLANE)

    inner_a, inner_b, inner_own = weight(1 - odd), weight(odd - highest), weight(highest)
    outer_a, outer_b = weight(odd), weight(1 - odd - lowest)
    cands = [ref.at[s] for ref in (below, mine, above) for s in range(per_dev)]
    face_of_lane = lax.broadcasted_iota(jnp.int32, (16, PLANE), 1) // 64
    low, high = slice(0, PLANE), slice(PLANE, HALF)
    for j in range(per_dev):
        layer = [slab[j, :, i * PLANE : (i + 1) * PLANE] for i in range(4)]
        a, b = a_in[j], b_in[j]
        inner0 = scaled(a[:, low], inner_a) + scaled(b[:, low], inner_b) + scaled(layer[2], inner_own)
        inner1 = scaled(a[:, high], inner_a) + scaled(b[:, high], inner_b) + scaled(layer[1], inner_own)
        outer0 = scaled(a[:, low], outer_a) + scaled(b[:, low], outer_b)
        outer1 = scaled(a[:, high], outer_a) + scaled(b[:, high], outer_b)
        code = [plan[8 + 6 * j + f] for f in range(6)]
        lane_code = jnp.where(
            face_of_lane < 2,
            jnp.where(face_of_lane == 0, code[2], code[3]),
            jnp.where(face_of_lane == 2, code[4], code[5]),
        )
        rest = jnp.zeros((channels, PLANE), bf16)
        for c, cand in enumerate(cands):
            outer0 = outer0 + scaled(cand[:, HALF:FACE_LANES], weight(jnp.where(code[0] == c, lowest, 0)))
            outer1 = outer1 + scaled(cand[:, PLANE:HALF], weight(jnp.where(code[1] == c, lowest, 0)))
            rest = rest + scaled(cand[:, low], jnp.where(lane_code == c, 1.0, 0.0).astype(bf16))
        placed = jnp.dot(rest, put[...], preferred_element_type=f32)
        sides = ((outer0, layer[1]), (layer[0], inner0), (inner1, layer[3]), (layer[2], outer1))
        for i in range(4):
            total = jnp.dot(layer[i], flat[...], preferred_element_type=f32)
            total = total + placed[:, i * PLANE : (i + 1) * PLANE]
            total = total + sides[i][0].astype(f32) + sides[i][1].astype(f32)
            spread[first_row : first_row + channels, j * SLAB + i * PLANE : j * SLAB + (i + 1) * PLANE] = (
                total.astype(bf16)
            )


TILE = 1024


def network(plan, j, inputs, slab, w_in, bias, w_out, state):
    step = 1.0 - 0.5 * plan[6 + j].astype(jnp.float32)
    for n in range(SLAB // TILE):
        lanes = slice(j * SLAB + n * TILE, j * SLAB + (n + 1) * TILE)
        shift = jnp.concatenate([bias[...]] * (TILE // bias.shape[1]), 1)
        pre = jnp.dot(w_in[...], inputs[:, lanes], preferred_element_type=jnp.float32) + shift
        half = 0.5 * pre
        hidden = (half + half * jnp.tanh(half)).astype(jnp.bfloat16)
        update = jnp.dot(w_out[...], hidden, preferred_element_type=jnp.float32)
        update = update.astype(jnp.bfloat16).astype(jnp.float32)
        here = slice(n * TILE, (n + 1) * TILE)
        state[j, :, here] = (slab[j, :, here].astype(jnp.float32) + step * update).astype(jnp.bfloat16)


def weights_kernel(w_in, bias, w_out, w_first, w_second, w_out_t, bias_t):
    channels = w_out.shape[1]
    turned = w_in[...].astype(jnp.float32).T.astype(jnp.bfloat16)
    older = (HIST - 1) * channels
    w_first[...] = turned
    w_second[:, 0:older] = turned[:, channels : HIST * channels]
    w_second[:, older : HIST * channels] = turned[:, 0:channels]
    w_second[:, HIST * channels :] = turned[:, HIST * channels :]
    w_out_t[...] = w_out[...].astype(jnp.float32).T.astype(jnp.bfloat16)
    for r in range(bias.shape[0]):
        bias_t[r * 128 : (r + 1) * 128, :] = jnp.broadcast_to(bias[r : r + 1, :], (128, 128)).T


def emit_back(plan, state, j, backs):
    grp, size = plan[1], len(backs)
    width = backs[0].shape[0]
    for k in range(size):
        backs[k][...] = state[j, channel_rows(grp, k, size, width), :]


def fill_late(plan, j, pieces, inputs, first):
    size, width = len(pieces), pieces[0].shape[1]
    channels = size * width
    for k in range(size):
        for t in range(pieces[k].shape[0]):
            rows = channel_rows(plan[1], k, size, width, (first + t) * channels)
            inputs[rows, j * SLAB : (j + 1) * SLAB] = pieces[k][t]


def first_kernel(size, plan, lay, put, flat, w_in, bias, w_out, slab, a_in, b_in, mine, below, above, old, old_below, old_above, *refs):
    pieces, (inputs, state), edges, backs = refs[:size], refs[size : size + 2], refs[size + 2 : size + 5], refs[size + 5 :]
    per_dev, channels = slab.shape[0], slab.shape[1]
    early = old.shape[1]
    for j in range(per_dev):
        lanes = slice(j * SLAB, (j + 1) * SLAB)
        inputs[0:channels, lanes] = slab[j]

        def store(source):
            for t in range(early):
                inputs[(1 + t) * channels : (2 + t) * channels, lanes] = source[t]

        settle(plan, j, old, old_below, old_above, store)
    fill_late(plan, 0, pieces, inputs, 1 + early)
    laplacian(plan, slab, a_in, b_in, mine, below, above, put, flat, inputs, HIST * channels)
    network(plan, 0, inputs, slab, w_in, bias, w_out, state)
    emit_back(plan, state, 0, backs)
    emit_edges(plan, range(1), state, lay, *edges)


def rest_kernel(size, early, plan, lay, w_in, bias, w_out, slab, *refs):
    pieces = refs[5:-5 - size * (slab.shape[0] - 1)]
    inputs, state, *edges = refs[5 + len(pieces) : 10 + len(pieces)]
    backs = refs[10 + len(pieces) :]
    per_dev = slab.shape[0]
    for j in range(1, per_dev):
        fill_late(plan, j, pieces[(j - 1) * size : j * size], inputs, 1 + early)
        network(plan, j, inputs, slab, w_in, bias, w_out, state)
    emit_edges(plan, range(1, per_dev), state, lay, *edges)
    for j in range(1, per_dev):
        emit_back(plan, state, j, backs[(j - 1) * size : j * size])


def second_kernel(size, plan, put, flat, w_in, bias, w_out, slab, a_in, b_in, mine, below, above, passed, *refs):
    backs = refs[:size]
    inputs, state = refs[size:]
    per_dev, channels = slab.shape[0], slab.shape[1]
    for j in range(per_dev):
        inputs[(HIST - 1) * channels : HIST * channels, j * SLAB : (j + 1) * SLAB] = slab[j]
    laplacian(plan, slab, a_in, b_in, mine, below, above, put, flat, inputs, HIST * channels)
    for j in range(per_dev):
        network(plan, j, inputs, slab, w_in, bias, w_out, state)
    for k in range(size):
        rows = channel_rows(plan[1], k, size, backs[k].shape[1])
        for j in range(per_dev):
            backs[k][j] = state[j, rows, :]


def finish_kernel(size, plan, *refs):
    out = refs[-1]
    for k in range(size):
        for here, there in slab_lanes(lax.rem(plan[1] + k, size), size):
            for j in range(out.shape[0]):
                out[j, 0, :, there] = refs[k][j, :, here] if len(refs[k].shape) == 3 else refs[j * size + k][:, here]


def local_folded(history, face_patch, refined, dest_slot, w_in, in_bias, w_out):
    bf16 = jnp.bfloat16
    per_dev, hist, width, cells = history.shape
    size = lax.axis_size("grp")
    channels = width * size
    hidden = w_in.shape[1]
    doms = lax.axis_size("dom")
    smem = pl.BlockSpec(memory_space=SMEM)
    anywhere = pl.BlockSpec(memory_space=pl.ANY)
    shape = jax.ShapeDtypeStruct
    up_ring = [(i, (i + 1) % doms) for i in range(doms)]
    down_ring = [(i, (i - 1) % doms) for i in range(doms)]

    def state_block(t):
        return pl.BlockSpec((per_dev, 1, width, cells), lambda i: (0, t, 0, 0))

    def early_pack(first, states, *after):
        whole = lax.slice_in_dim(history, 0, states, axis=1) if first == 0 else history
        return pl.pallas_call(
            functools.partial(early_pack_kernel, size, first, states),
            out_shape=[shape((per_dev, states, width, SLAB), bf16)] * size,
            in_specs=vmem_specs(1) + [anywhere] * len(after),
            out_specs=vmem_specs(size),
            compiler_params=grant(SMALL),
        )(whole, *after)

    early = 1
    late = hist - 1 - early
    newest = early_pack(0, 1)
    plan = pl.pallas_call(
        functools.partial(plan_kernel, per_dev),
        out_shape=shape((PLAN_SIZE,), jnp.int32),
        in_specs=[smem] * 3 + [anywhere] * size,
        out_specs=smem,
        compiler_params=grant(SMALL),
        name="plan",
    )(face_patch.T, refined, dest_slot, *newest)

    def movers(first, states):
        return pl.pallas_call(
            functools.partial(send_kernel, first),
            out_shape=[shape((states, width, cells), bf16)] * 2,
            in_specs=[smem] + vmem_specs(1),
            out_specs=vmem_specs(2),
            compiler_params=grant(SMALL),
        )(plan, history)

    def across_dom(up, down):
        return lax.ppermute(up, "dom", up_ring), lax.ppermute(down, "dom", down_ring)

    def pack(first, states, below, above, *after):
        return pl.pallas_call(
            functools.partial(pack_kernel, size, first),
            out_shape=[shape((states, width, SLAB), bf16)] * (size * per_dev),
            in_specs=[smem] + vmem_specs(3) + [anywhere] * len(after),
            out_specs=vmem_specs(size * per_dev),
            compiler_params=grant(SMALL),
        )(plan, history, below, above, *after)

    def across_grp(pieces, sign):
        moved = [pieces[0]]
        for k in range(1, size):
            moved.append(lax.ppermute(pieces[k], "grp", [(i, (i + sign * k) % size) for i in range(size)]))
        return moved

    pair_a = [(i, i ^ 1) for i in range(size)]
    pair_b = []
    for d in range(doms):
        for i in range(size):
            target = (d ^ 1, i) if i in (0, size - 1) else (d, ((i + 1) ^ 1) - 1)
            pair_b.append((d * size + i, target[0] * size + target[1]))

    def exchange(a_out, b_out, f_out):
        b_in = lax.ppermute(b_out, ("dom", "grp"), pair_b)
        a_in = lax.ppermute(a_out, "grp", pair_a)
        below, above = across_dom(f_out, f_out)
        return a_in, b_in, f_out, below, above

    lay, put, flat = (jnp.asarray(table, bf16) for table in face_tables())
    w_first, w_second, w_out_t, bias = pl.pallas_call(
        weights_kernel,
        out_shape=[shape((hidden, (hist + 1) * channels), bf16)] * 2
        + [shape((channels, hidden), bf16), shape((hidden, 128), jnp.float32)],
        in_specs=vmem_specs(3),
        out_specs=vmem_specs(4),
        compiler_params=grant(SMALL),
        name="weights",
    )(w_in, in_bias.reshape(-1, 128), w_out)

    slab_shape = shape((per_dev, channels, SLAB), bf16)
    edge_shapes = [
        shape((per_dev, channels, HALF), bf16),
        shape((per_dev, channels, HALF), bf16),
        shape((per_dev, channels, FACE_LANES), bf16),
    ]
    back_shape = shape((width, SLAB), bf16)

    def gather(pieces, *after):
        states = pieces[0].shape[1]
        return pl.pallas_call(
            functools.partial(gather_kernel, size),
            out_shape=[shape((per_dev, states, channels, SLAB), bf16)]
            + [shape((states, channels, SLAB), bf16)] * 2,
            in_specs=[smem] + vmem_specs(size) + [anywhere] * len(after),
            out_specs=vmem_specs(3),
            compiler_params=grant(SMALL),
        )(plan, *pieces, *after)

    newest = across_grp(newest, 1)
    up, down = movers(1 + early, late)
    below, above = across_dom(up, down)
    middle = early_pack(1, early, up)
    old0, up0, down0 = gather(newest, *middle)
    middle = across_grp(middle, 1)
    below0, above0 = across_dom(up0, down0)
    packed = pack(1 + early, late, below, above, up0)
    late0 = across_grp(packed[:size], 1)
    late1 = across_grp(packed[size:], 1)
    slab0, *edges = pl.pallas_call(
        edge_kernel,
        out_shape=[slab_shape] + edge_shapes,
        in_specs=[smem] + vmem_specs(4) + [anywhere] * len(packed),
        out_specs=vmem_specs(4),
        compiler_params=grant(SMALL),
        name="edges",
    )(plan, lay, old0, below0, above0, *packed)
    old1, up1, down1 = gather(middle, *edges)
    below1, above1 = across_dom(up1, down1)

    inputs = shape(((hist + 1) * channels, per_dev * SLAB), bf16)
    stacked, slab1, *rest = pl.pallas_call(
        functools.partial(first_kernel, size),
        out_shape=[inputs, slab_shape] + edge_shapes + [back_shape] * size,
        in_specs=[smem] + vmem_specs(15 + size),
        out_specs=vmem_specs(5 + size),
        compiler_params=grant(LARGE),
        name="first",
    )(
        plan, lay, put, flat, w_first, bias, w_out_t, slab0, *exchange(*edges),
        old1, below1, above1, *late0,
    )
    edges = rest[:3]
    back0 = across_grp(rest[3:], -1)
    others = size * (per_dev - 1)
    stacked, slab1, *rest = pl.pallas_call(
        functools.partial(rest_kernel, size, early),
        out_shape=[inputs, slab_shape] + edge_shapes + [back_shape] * others,
        in_specs=[smem] + vmem_specs(10 + others),
        out_specs=vmem_specs(5 + others),
        input_output_aliases={6 + i: i for i in range(5)},
        compiler_params=grant(LARGE),
        name="rest",
    )(plan, lay, w_first, bias, w_out_t, slab0, stacked, slab1, *edges, *late1)
    parts = exchange(*rest[:3])
    back1 = across_grp(rest[3:], -1)
    *back2, stacked = pl.pallas_call(
        functools.partial(second_kernel, size),
        out_shape=[shape((per_dev, width, SLAB), bf16)] * size + [inputs],
        in_specs=[smem] + vmem_specs(12),
        out_specs=vmem_specs(size + 1),
        scratch_shapes=[pltpu.VMEM((per_dev, channels, SLAB), bf16)],
        input_output_aliases={12: size},
        compiler_params=grant(LARGE),
        name="second",
    )(plan, put, flat, w_second, bias, w_out_t, slab1, *parts, stacked)

    def finish(state, pieces, *before):
        return pl.pallas_call(
            functools.partial(finish_kernel, size),
            grid=(1,),
            out_shape=shape((per_dev, 2, width, cells), bf16),
            in_specs=[smem] + vmem_specs(len(pieces)) + [anywhere] * len(before),
            out_specs=state_block(state),
            input_output_aliases={1 + len(pieces): 0} if before else {},
            compiler_params=grant(SMALL),
        )(plan, *pieces, *before)

    out = finish(0, back0 + back1)
    back2 = across_grp(back2, -1)
    return finish(1, back2, out)


def solution(mesh):
    placed = (P("dom", None, "grp", None), P(), P(), P(), P(), P(), P())
    folded = mesh.shape["grp"] == 4 and mesh.shape["dom"] % 2 == 0

    def body(*arrays):
        return (local_folded if folded else local_general)(*arrays)

    return jax.shard_map(
        body, mesh=mesh, in_specs=placed, out_specs=P("dom", None, "grp", None), check_vma=False
    )
```
